32 devices in a mesh: dp: 8 (over z, x), tensor: 4 (over y, core).
Axes of the slice: x: 2, y: 2, z: 4, core: 2. Of those that a mesh axis runs over, the one named last changes fastest.
Arguments:
- inputs: bfloat16 [1500, 8, 1024], P('tensor', 'dp'), may hold values from -6 to 6
- segments: int32 [8, 1500], P('dp'), may hold values from 0 to 3, never falling along the last dimension, each value on 1 to 750 neighbouring positions
- cotangent: bfloat16 [1500, 8, 1024], P('tensor', 'dp'), may hold values from -6 to 6
- gain_one: float32 [1024], replicated, may hold values from 0.1 to 1.9
- first_in: bfloat16 [1024, 4096], P(None, 'tensor'), may hold values from -0.1875 to 0.1875
- first_out: bfloat16 [4096, 1024], P('tensor'), may hold values from -0.1875 to 0.1875
- gain_two: float32 [1024], replicated, may hold values from 0.1 to 1.9
- w_query: bfloat16 [1024, 1024], P(None, 'tensor'), may hold values from -0.1875 to 0.1875
- w_key: bfloat16 [1024, 1024], P(None, 'tensor'), may hold values from -0.1875 to 0.1875
- w_value: bfloat16 [1024, 1024], P(None, 'tensor'), may hold values from -0.1875 to 0.1875
- w_output: bfloat16 [1024, 1024], P('tensor'), may hold values from -0.75 to 0.75
- rel_table: float32 [16, 257], P('tensor'), may hold values from -4 to 4
- gain_three: float32 [1024], replicated, may hold values from 0.1 to 1.9
- w_glu: bfloat16 [1024, 2, 1024], P(None, None, 'tensor'), may hold values from -0.1875 to 0.1875
- kernel: float32 [31, 1024], P(None, 'tensor'), may hold values from -1 to 1
- w_back: bfloat16 [1024, 1024], P('tensor'), may hold values from -0.5 to 0.5
- gain_four: float32 [1024], replicated, may hold values from 0.1 to 1.9
- second_in: bfloat16 [1024, 4096], P(None, 'tensor'), may hold values from -0.1875 to 0.1875
- second_out: bfloat16 [4096, 1024], P('tensor'), may hold values from -0.1875 to 0.1875
- gain_five: float32 [1024], replicated, may hold values from 0.1 to 1.9
Outputs:
- output: bfloat16 [1500, 8, 1024], P('tensor', 'dp')
- grad_inputs: float32 [1500, 8, 1024], P('tensor', 'dp')
- grad_gain_one: float32 [1024], replicated
- grad_first_in: float32 [1024, 4096], P('dp', 'tensor')
- grad_first_out: float32 [4096, 1024], P('tensor', 'dp')
- grad_gain_two: float32 [1024], replicated
- grad_w_query: float32 [1024, 1024], P('dp', 'tensor')
- grad_w_key: float32 [1024, 1024], P('dp', 'tensor')
- grad_w_value: float32 [1024, 1024], P('dp', 'tensor')
- grad_w_output: float32 [1024, 1024], P('tensor', 'dp')
- grad_rel_table: float32 [16, 257], P('tensor')
- grad_gain_three: float32 [1024], replicated
- grad_w_glu: float32 [1024, 2, 1024], P('dp', None, 'tensor')
- grad_kernel: float32 [31, 1024], P(None, 'tensor')
- grad_w_back: float32 [1024, 1024], P('tensor', 'dp')
- grad_gain_four: float32 [1024], replicated
- grad_second_in: float32 [1024, 4096], P('dp', 'tensor')
- grad_second_out: float32 [4096, 1024], P('tensor', 'dp')
- grad_gain_five: float32 [1024], replicated
The draws below stay inside these ranges and needn't reach their ends.
Inputs may be any that keep to these rules, and one draw needn't show every extreme that they name: `segments`: within each row of 1500 frames the segment numbers start at 0 and never fall; each of the 4 utterances holds 1 to 750 frames, and one holds exactly 750.
All inputs are finite; a program needn't handle non-finite values.
Results may differ from the reference program's by a relative error of at most 0.03.
Values may be sent and summed in bfloat16 or wider, within the bound.
No kernel may reach another device: no remote copies, remote signals or barrier semaphores. Data moves between devices by JAX's collectives and lax.ppermute only.
A program may use at most 256 MiB of HBM per device.

```python
import math
import jax
import jax.numpy as jnp
import numpy as np
from jax import lax

D = 1024
HEADS = 16
FF = 4096
KERNEL = 31
REACH = 128
FRAMES = 1500
UTTS = 4
LONGEST = 750
ROWS = 8


def raised(values, key, source, target, blocks, factor):
    owner, partner = [(jnp.arange(values.shape[position]) // (values.shape[position] // blocks)).reshape([-1 if axis == position else 1 for axis in range(values.ndim)]) for position in (source, target)]
    chosen = jax.random.permutation(key, blocks)[partner]
    strong = (owner == chosen) | (owner == (partner + blocks // 2) % blocks)
    return jnp.where(strong, factor * values, values)


def block_levels(key, shape, shards, smallest, high):
    factor_of = 1.0
    for dim, blocks in shards:
        steps = jax.random.uniform(jax.random.fold_in(jax.random.fold_in(key, 6), dim), (blocks,), jnp.float32, smallest / len(shards), high / len(shards))
        factor_of = factor_of * jnp.repeat(jnp.exp(steps), shape[dim] // blocks).reshape((-1,) + (1,) * (len(shape) - 1 - dim))
    return factor_of


def split_up(number_of, total, bound, slope):
    loads = [(1 << 20) // math.isqrt(standing ** slope) + 1 for standing in range(2, number_of + 1)]
    surplus, counts = total - bound - (number_of - 1), [1] * (number_of - 1)
    while surplus > 0:
        free = [i for i in range(number_of - 1) if counts[i] < bound]
        mass, budget = sum([loads[i] for i in free]), surplus
        for i in free:
            addition = min(bound - counts[i], max(1, budget * loads[i] // mass), surplus)
            counts[i] = counts[i] + addition
            surplus = surplus - addition
    return np.array([bound] + counts)


def uneven(own_key, amount, total, bound, slope):
    if amount == 2:
        one = jax.random.randint(own_key, (), max(1, total - bound), min(bound, total - 1) + 1)
        return jnp.stack([one, total - one])
    sizes = jnp.asarray(split_up(amount, total, bound, slope), jnp.int32)
    couples = (amount - 1) // 2
    giver, sink = sizes[1:1 + 2 * couples:2], sizes[2:2 + 2 * couples:2]
    margin = jnp.minimum(giver - 1, bound - sink)
    passed = jax.random.randint(jax.random.fold_in(own_key, 1), (couples,), 0, 1 << 20) % (margin + 1)
    sizes = sizes.at[1:1 + 2 * couples:2].set(giver - passed).at[2:2 + 2 * couples:2].set(sink + passed)
    return sizes[jax.random.permutation(jax.random.fold_in(own_key, 2), amount)]


def scatter_about(rng, shape, scale, bound, shards=(), kind=jnp.bfloat16):
    level = block_levels(rng, shape, shards, -0.22, 0.18) if shards else 1.0
    values = jax.random.normal(rng, shape, jnp.float32) * scale * level
    return jnp.minimum(jnp.maximum(values, -bound), bound).astype(kind)


def heavy_noise(own_key, shape, deviation, bound, shards, heavy, kind=jnp.bfloat16):
    array = deviation * jax.random.normal(own_key, shape, jnp.float32)
    if shards:
        array = array * block_levels(own_key, shape, shards, -0.22, 0.18)
    return jnp.clip(raised(array, jax.random.fold_in(own_key, 3), *heavy), -bound, bound).astype(kind)


def setup_inputs(seed: int = 0) -> dict:
    streams_of = jax.random.split(jax.random.key(seed), 21)
    inputs = heavy_noise(streams_of[0], (FRAMES, ROWS, D), 1.0, 6.0, ((0, 4), (1, 8)), (1, 2, 8, 2.0))
    segments = jax.vmap(lambda own: jnp.searchsorted(jnp.cumsum(uneven(own, UTTS, FRAMES, LONGEST, 2)), jnp.arange(FRAMES), side="right"))(jax.random.split(streams_of[1], ROWS)).reshape((ROWS, FRAMES)).astype(jnp.int32)
    cotangent = heavy_noise(streams_of[2], (FRAMES, ROWS, D), 1.0, 6.0, ((0, 4), (1, 8)), (1, 2, 8, 2.0))
    gain_one = jnp.clip(1.0 + 0.18 * jax.random.normal(streams_of[3], (D,), jnp.float32), 0.1, 1.9)
    first_in = scatter_about(streams_of[4], (D, FF), D ** -0.5, 0.1875, ((1, 4),))
    first_out = scatter_about(streams_of[5], (FF, D), (FF // 4) ** -0.5, 0.1875, ((0, 4),))
    gain_two = jnp.clip(1.0 + 0.18 * jax.random.normal(streams_of[6], (D,), jnp.float32), 0.1, 1.9)
    w_query = scatter_about(streams_of[7], (D, D), D ** -0.5, 0.1875, ((1, 4),))
    w_key = scatter_about(streams_of[8], (D, D), D ** -0.5, 0.1875, ((1, 4),))
    w_value = scatter_about(streams_of[9], (D, D), D ** -0.5, 0.1875, ((1, 4),))
    w_output = scatter_about(streams_of[10], (D, D), (D // 16) ** -0.5, 0.75, ((0, 4),))
    rel_table = scatter_about(streams_of[11], (HEADS, 2 * REACH + 1), 1.0, 4.0, ((0, 4),), jnp.float32)
    gain_three = jnp.clip(1.0 + 0.18 * jax.random.normal(streams_of[12], (D,), jnp.float32), 0.1, 1.9)
    w_glu = scatter_about(streams_of[13], (D, 2, D), D ** -0.5, 0.1875, ((2, 4),))
    kernel = scatter_about(streams_of[14], (KERNEL, D), KERNEL ** -0.5, 1.0, ((1, 4),), jnp.float32)
    w_back = scatter_about(streams_of[15], (D, D), (D // 8) ** -0.5, 0.5, ((0, 4),))
    gain_four = jnp.clip(1.0 + 0.18 * jax.random.normal(streams_of[16], (D,), jnp.float32), 0.1, 1.9)
    second_in = scatter_about(streams_of[17], (D, FF), D ** -0.5, 0.1875, ((1, 4),))
    second_out = scatter_about(streams_of[18], (FF, D), (FF // 4) ** -0.5, 0.1875, ((0, 4),))
    gain_five = jnp.clip(1.0 + 0.18 * jax.random.normal(streams_of[19], (D,), jnp.float32), 0.1, 1.9)
    return dict(inputs=inputs, segments=segments, cotangent=cotangent, gain_one=gain_one, first_in=first_in, first_out=first_out, gain_two=gain_two, w_query=w_query, w_key=w_key, w_value=w_value, w_output=w_output, rel_table=rel_table, gain_three=gain_three, w_glu=w_glu, kernel=kernel, w_back=w_back, gain_four=gain_four, second_in=second_in, second_out=second_out, gain_five=gain_five)


@jax.custom_vjp
def low(v):
    return lax.optimization_barrier(v.astype(jnp.bfloat16)).astype(jnp.float32)

@jax.custom_vjp
def low_back(v):
    return v

def low_keep(v):
    return (low(v), None)

def low_pass(kept, grad):
    return (grad,)

def back_keep(v):
    return (v, None)

def back_low(kept, grad):
    return (low(grad),)
low.defvjp(low_keep, low_pass)
low_back.defvjp(back_keep, back_low)

def normed(residual, gain_vec):
    row_mean = lax.optimization_barrier(jnp.mean(residual, axis=-1, keepdims=True))
    centred = residual - row_mean
    variance = lax.optimization_barrier(jnp.mean(centred * centred, axis=-1, keepdims=True))
    return centred * lax.rsqrt(variance + 1e-05) * gain_vec

def matmul(operand, weight):
    return jnp.dot(operand, weight, precision=lax.Precision.HIGHEST, preferred_element_type=jnp.float32)

def depthwise(values, kernel, labels):
    kernel_len = kernel.shape[0]
    half_width = kernel_len // 2
    frames = values.shape[0]
    padded = jnp.pad(values, ((half_width, half_width),) + ((0, 0),) * (values.ndim - 1))
    padded_labels = jnp.pad(labels, ((half_width, half_width),) + ((0, 0),) * (labels.ndim - 1), constant_values=-1)
    summed = jnp.zeros_like(values)
    for offset in range(kernel_len):
        same_seg = (padded_labels[offset:offset + frames] == labels)[..., None]
        summed = summed + jnp.where(same_seg, padded[offset:offset + frames] * kernel[offset], 0.0)
    return summed

def feed_forward(residual, gain_vec, w_in, w_out):
    normed_rows = low(normed(residual, gain_vec))
    hidden = low_back(matmul(normed_rows, w_in))
    active = low(jax.nn.silu(hidden))
    return residual + 0.5 * low_back(matmul(active, w_out))

def attention(residual, gain_vec, w_query, w_key, w_value, w_output, rel_table, labels):
    frames, width = residual.shape
    head_count = rel_table.shape[0]
    head_width = width // head_count
    reach_max = rel_table.shape[1] // 2
    normed_rows = low(normed(residual, gain_vec))

    def project(weight):
        projected = low(low_back(matmul(normed_rows, weight)))
        return projected.reshape(frames, head_count, head_width).transpose(1, 0, 2)
    query_rows, key_rows, value_rows = (project(w_query), project(w_key), project(w_value))
    positions = jnp.arange(frames, dtype=jnp.int32)
    distance_idx = (jnp.clip(positions[None, :] - positions[:, None], -reach_max, reach_max) + reach_max).astype(jnp.int32)
    allowed = labels[:, None] == labels[None, :]
    score_scale = head_width ** (-0.5)

    def one_head(record):
        query_head, key_head, value_head, table_row = record
        scores = jnp.einsum('qd,kd->qk', query_head, key_head, precision=lax.Precision.HIGHEST) * score_scale
        scores = low_back(scores + jnp.take(table_row, distance_idx))
        scores = jnp.where(allowed, scores, -1e+30)
        attend = jax.nn.softmax(scores, axis=-1)
        mixed = jnp.einsum('qk,kd->qd', low(attend), value_head, precision=lax.Precision.HIGHEST)
        return low(low_back(mixed))
    attended = lax.map(jax.checkpoint(one_head), (query_rows, key_rows, value_rows, rel_table))
    attended = attended.transpose(1, 0, 2).reshape(frames, width)
    return residual + low_back(matmul(attended, w_output))

def convolution(residual, gain_vec, w_glu, kernel, w_back, labels):
    frames, width = residual.shape
    normed_rows = low(normed(residual, gain_vec))
    glu_input = low_back(matmul(normed_rows, w_glu.reshape(width, 2 * width))).reshape(frames, 2, width)
    gated = glu_input[:, 0] * jax.nn.sigmoid(glu_input[:, 1])
    active = low(jax.nn.silu(depthwise(gated, kernel, labels)))
    return residual + low_back(matmul(active, w_back))

def conformer(frames_in, labels, params):
    gain_one, first_in, first_out, gain_two, w_query, w_key, w_value, w_output, rel_table, gain_three, w_glu, kernel, w_back, gain_four, second_in, second_out, gain_five = params
    after_one = feed_forward(frames_in, gain_one, first_in, first_out)
    after_two = attention(after_one, gain_two, w_query, w_key, w_value, w_output, rel_table, labels)
    after_three = convolution(after_two, gain_three, w_glu, kernel, w_back, labels)
    after_four = feed_forward(after_three, gain_four, second_in, second_out)
    return normed(after_four, gain_five)

def reference(inputs, segments, cotangent, gain_one, first_in, first_out, gain_two, w_query, w_key, w_value, w_output, rel_table, gain_three, w_glu, kernel, w_back, gain_four, second_in, second_out, gain_five):
    weights = (gain_one, first_in, first_out, gain_two, w_query, w_key, w_value, w_output, rel_table, gain_three, w_glu, kernel, w_back, gain_four, second_in, second_out, gain_five)
    params = tuple((weight.astype(jnp.float32) for weight in weights))
    by_row = jnp.swapaxes(inputs, 0, 1)
    upstream_rows = jnp.swapaxes(cotangent, 0, 1)

    def per_row(totals, record):
        row_block, labels, upstream = record

        def forward(values, weights_f):
            return conformer(values, labels, weights_f)
        result, pullback = jax.vjp(forward, row_block.astype(jnp.float32), params)
        row_grads, param_grads = pullback(upstream.astype(jnp.float32))
        return (jax.tree.map(jnp.add, totals, param_grads), (result.astype(jnp.bfloat16), row_grads))
    zero_grads = jax.tree.map(jnp.zeros_like, params)
    totals, (results, input_grads) = lax.scan(per_row, zero_grads, (by_row, segments, upstream_rows))
    return (jnp.swapaxes(results, 0, 1), jnp.swapaxes(input_grads, 0, 1), totals[0], totals[1], totals[2], totals[3], totals[4], totals[5], totals[6], totals[7], totals[8], totals[9], totals[10], totals[11], totals[12], totals[13], totals[14], totals[15], totals[16])
```

```python
import functools

import jax
import jax.numpy as jnp
import numpy as np
from jax import lax
from jax.experimental import pallas as pl
from jax.experimental.pallas import tpu as pltpu
from jax.sharding import PartitionSpec as P

TILE = 128
MASKED = -1e30
F32 = jnp.float32
BF16 = jnp.bfloat16


def pad_up(size, unit):
    return -(-size // unit) * unit


def dot(a, b, ca, cb):
    return lax.dot_general(a, b, (((ca,), (cb,)), ((), ())), preferred_element_type=F32)


def tile_offsets(blocks, block_frames, per_block):
    starts = np.array([b * block_frames + t * TILE for b in range(blocks) for t in range(per_block)])
    return starts[None, :] - starts[:, None]


def bias_types(offsets, reach):
    near = sorted({int(d) for d in offsets.ravel() if abs(int(d)) < reach + TILE - 1})
    far = 4 * TILE + reach
    kinds = near + [-far, far]
    index = {d: i for i, d in enumerate(near)}
    table = np.array(
        [
            [index.get(int(d), len(near) + (1 if d > 0 else 0)) for d in row]
            for row in offsets
        ],
        np.int32,
    )
    return kinds, table


def column_onehot(kinds, reach):
    lane = lax.broadcasted_iota(jnp.int32, (len(kinds), 2 * TILE), 1)
    signed = jnp.where(lane < TILE, lane, lane - 2 * TILE)
    base = jnp.array(kinds, jnp.int32)[:, None]
    column = jnp.clip(base - signed, -reach, reach) + reach
    width = 2 * reach + 1
    flat = column.reshape(-1)
    return (flat[None, :] == jnp.arange(width, dtype=jnp.int32)[:, None]).astype(F32)


def bias_body(row_ref, out_ref):
    for head in range(2):
        line = jnp.broadcast_to(row_ref[0, 0, head : head + 1, :], (TILE, 2 * TILE))
        skewed = pltpu.roll(line, 0, 1, stride=1, stride_axis=0)
        out_ref[0, 0, :, head * TILE : (head + 1) * TILE] = skewed[:, :TILE]


def bias_tiles(rel_table, onehot, kinds):
    heads = rel_table.shape[0]
    pairs = heads // 2
    count = len(kinds)
    rows = jnp.dot(rel_table, onehot, precision=lax.Precision.HIGHEST, preferred_element_type=F32)
    rows = rows.reshape(pairs, 2, count, 2 * TILE).transpose(0, 2, 1, 3)
    return pl.pallas_call(
        bias_body,
        grid=(pairs, count),
        in_specs=[pl.BlockSpec((1, 1, 2, 2 * TILE), lambda p, c: (p, c, 0, 0))],
        out_specs=pl.BlockSpec((1, 1, TILE, 2 * TILE), lambda p, c: (p, c, 0, 0)),
        out_shape=jax.ShapeDtypeStruct((pairs, count, TILE, 2 * TILE), F32),
        name="distance_bias",
    )(rows)


def stacked_heads(pair):
    low_half = lax.broadcasted_iota(jnp.int32, pair.shape, 1) < pair.shape[1] // 2
    zero = jnp.zeros_like(pair)
    return jnp.concatenate([jnp.where(low_half, pair, zero), jnp.where(low_half, zero, pair)], 0)


def own_quadrants(wide):
    half = lax.broadcasted_iota(jnp.int32, (TILE, TILE), 0) < TILE // 2
    return jnp.where(half, wide[:, :TILE], wide[:, TILE:])


def fold(values):
    return values.reshape(values.shape[0] // 8, 8, values.shape[1])


def attend_body(
    place_ref, start_ref, count_ref, kind_ref,
    qkv_ref, bias_ref, lab_ref, labrow_ref,
    out_ref, lse_ref,
    score_ref, turned_ref, acc_ref,
    *, tiles, pairs, scale,
):
    step = pl.program_id(0)
    width = pairs * TILE

    @pl.when(step == 0)
    def _():
        for tile in range(tiles):
            turned_ref[tile] = qkv_ref[place_ref[tile], :, 2 * width :].T

    mine = qkv_ref[place_ref[step]]
    queries = [
        stacked_heads(mine[:, p * TILE : (p + 1) * TILE] * scale) for p in range(pairs)
    ]
    own_label = labrow_ref[step]
    begin = start_ref[step]
    trips = count_ref[step]

    def scores(trip, best):
        for sub in range(2):
            tile = begin + 2 * trip + sub
            kind = kind_ref[step * tiles + tile]
            keys = qkv_ref[place_ref[tile], :, width : 2 * width]
            allowed = lab_ref[tile] == own_label
            parts = []
            for p in range(pairs):
                raw = dot(keys[:, p * TILE : (p + 1) * TILE], queries[p], 1, 1)
                raw = raw + bias_ref[p, kind]
                for h in range(2):
                    part = jnp.where(allowed, raw[:, h * TILE : (h + 1) * TILE], MASKED)
                    score_ref[tile, :, (2 * p + h) * TILE : (2 * p + h + 1) * TILE] = part
                    parts.append(jnp.max(fold(part), axis=0))
            best = jnp.maximum(best, jnp.concatenate(parts, 1))
        return best

    best = lax.fori_loop(0, trips, scores, jnp.full((8, 2 * width), MASKED, F32))
    top = jnp.max(best, axis=0, keepdims=True)
    acc_ref[...] = jnp.zeros_like(acc_ref)

    def mix(trip, total):
        first = begin + 2 * trip
        probs = []
        for sub in range(2):
            value = jnp.exp(score_ref[first + sub] - top)
            total = total + jnp.sum(fold(value), axis=0)
            probs.append(value.astype(BF16))
        both = jnp.concatenate(probs, 0)
        for p in range(pairs):
            turned = jnp.concatenate(
                [turned_ref[first + sub, p * TILE : (p + 1) * TILE, :] for sub in range(2)], 1
            )
            acc_ref[p] += dot(turned, both[:, 2 * p * TILE : 2 * (p + 1) * TILE], 1, 0)
        return total

    total = lax.fori_loop(0, trips, mix, jnp.zeros((8, 2 * width), F32))
    total = jnp.sum(total, axis=0, keepdims=True)
    inverse = 1.0 / total
    log_total = top + jnp.log(total)
    for p in range(pairs):
        wide = acc_ref[p] * inverse[:, 2 * p * TILE : 2 * (p + 1) * TILE]
        out_ref[0, :, p * TILE : (p + 1) * TILE] = own_quadrants(wide).T.astype(BF16)
    for h in range(2 * pairs):
        lse_ref[0, h : h + 1, :] = log_total[:, h * TILE : (h + 1) * TILE]


def attend(qkv, bias, plan):
    tiles, pairs = qkv.shape[0], bias.shape[0]
    width = pairs * TILE
    whole = lambda *shape: pl.BlockSpec(shape, lambda i, *_: (0,) * len(shape))
    return pl.pallas_call(
        functools.partial(attend_body, tiles=tiles, pairs=pairs, scale=plan["scale"]),
        grid_spec=pltpu.PrefetchScalarGridSpec(
            num_scalar_prefetch=4,
            grid=(tiles,),
            in_specs=[
                whole(*qkv.shape),
                whole(*bias.shape),
                whole(tiles, TILE, TILE),
                whole(tiles, 1, TILE),
            ],
            out_specs=[
                pl.BlockSpec((1, TILE, width), lambda i, place, *_: (place[i], 0, 0)),
                pl.BlockSpec((1, 2 * pairs, TILE), lambda i, *_: (i, 0, 0)),
            ],
            scratch_shapes=[
                pltpu.VMEM((tiles, TILE, 2 * width), F32),
                pltpu.VMEM((tiles, width, TILE), BF16),
                pltpu.VMEM((pairs, TILE, 2 * TILE), F32),
            ],
        ),
        out_shape=[
            jax.ShapeDtypeStruct((tiles, TILE, width), BF16),
            jax.ShapeDtypeStruct((tiles, 2 * pairs, TILE), F32),
        ],
        compiler_params=pltpu.CompilerParams(vmem_limit_bytes=48 * 2**20),
        name="attend",
    )(plan["place"], plan["start2"], plan["count2"], plan["kind"], qkv, bias, plan["lab"], plan["labrow"])


def unskew(values):
    wide = jnp.concatenate([values, jnp.zeros_like(values)], 1)
    rows = TILE
    while rows > 8:
        rows //= 2
        wide = wide[:rows] + pltpu.roll(wide[rows:], 2 * TILE - rows, 1)
    row = lax.broadcasted_iota(jnp.int32, wide.shape, 0)
    for bit in (4, 2, 1):
        wide = jnp.where((row & bit) != 0, pltpu.roll(wide, 2 * TILE - bit, 1), wide)
    return jnp.sum(wide, axis=0, keepdims=True)


def attend_back_body(
    place_ref, start_ref, count_ref, kind_ref,
    qkv_ref, bias_ref, lab_ref, labrow_ref, out_ref, grad_ref, lse_ref,
    dqkv_ref, table_ref,
    turned_ref, dk_ref, dv_ref, dq_ref, sums_ref,
    *, tiles, pairs, scale, kinds,
):
    step = pl.program_id(0)
    width = pairs * TILE

    @pl.when(step == 0)
    def _():
        for tile in range(tiles):
            turned_ref[tile] = qkv_ref[place_ref[tile], :, width : 2 * width].T
        dk_ref[...] = jnp.zeros_like(dk_ref)
        dv_ref[...] = jnp.zeros_like(dv_ref)
        sums_ref[...] = jnp.zeros_like(sums_ref)

    here = place_ref[step]
    queries, grads, deltas, logs = [], [], [], []
    for p in range(pairs):
        span = slice(p * TILE, (p + 1) * TILE)
        queries.append(stacked_heads(qkv_ref[here, :, span] * scale))
        grad = grad_ref[here, :, span]
        grads.append(stacked_heads(grad))
        product = (grad.astype(F32) * out_ref[here, :, span].astype(F32)).T
        half = TILE // 2
        deltas.append(
            jnp.concatenate(
                [
                    jnp.sum(product[:half], axis=0, keepdims=True),
                    jnp.sum(product[half:], axis=0, keepdims=True),
                ],
                1,
            )
        )
        logs.append(jnp.concatenate([lse_ref[step, 2 * p + h : 2 * p + h + 1, :] for h in range(2)], 1))
    own_label = labrow_ref[step]
    begin = start_ref[step]
    dq_ref[...] = jnp.zeros_like(dq_ref)

    def visit(trip, carry):
        tile = begin + trip
        kind = kind_ref[step * tiles + tile]
        there = place_ref[tile]
        allowed = lab_ref[tile] == own_label
        allowed = jnp.concatenate([allowed, allowed], 1)
        for p in range(pairs):
            span = slice(p * TILE, (p + 1) * TILE)
            keys = qkv_ref[there, :, width + p * TILE : width + (p + 1) * TILE]
            vals = qkv_ref[there, :, 2 * width + p * TILE : 2 * width + (p + 1) * TILE]
            raw = dot(keys, queries[p], 1, 1) + bias_ref[p, kind]
            prob = jnp.exp(jnp.where(allowed, raw - logs[p], MASKED))
            lift = dot(vals, grads[p], 1, 1)
            slope = prob * (lift - deltas[p])
            sums_ref[p, kind] += slope
            slope = slope.astype(BF16)
            dv_ref[tile, :, span] += dot(prob.astype(BF16), grads[p], 1, 0)
            dk_ref[tile, :, span] += dot(slope, queries[p], 1, 0)
            dq_ref[p] += dot(turned_ref[tile, span, :], slope, 1, 0)
        return carry

    lax.fori_loop(0, count_ref[step], visit, 0)
    for p in range(pairs):
        span = slice(p * TILE, (p + 1) * TILE)
        dqkv_ref[here, :, span] = (own_quadrants(dq_ref[p]).T * scale).astype(BF16)

    @pl.when(step == tiles - 1)
    def _():
        for tile in range(tiles):
            there = place_ref[tile]
            dqkv_ref[there, :, width : 2 * width] = dk_ref[tile].astype(BF16)
            dqkv_ref[there, :, 2 * width :] = dv_ref[tile].astype(BF16)
        for p in range(pairs):
            for kind in range(kinds):
                for h in range(2):
                    table_ref[2 * p + h, kind : kind + 1, :] = unskew(
                        sums_ref[p, kind, :, h * TILE : (h + 1) * TILE]
                    )


def attend_back(qkv, bias, plan, out, grad, lse):
    tiles, pairs, kinds = qkv.shape[0], bias.shape[0], bias.shape[1]
    width = pairs * TILE
    whole = lambda *shape: pl.BlockSpec(shape, lambda i, *_: (0,) * len(shape))
    return pl.pallas_call(
        functools.partial(
            attend_back_body, tiles=tiles, pairs=pairs, scale=plan["scale"], kinds=kinds
        ),
        grid_spec=pltpu.PrefetchScalarGridSpec(
            num_scalar_prefetch=4,
            grid=(tiles,),
            in_specs=[
                whole(*qkv.shape),
                whole(*bias.shape),
                whole(tiles, TILE, TILE),
                whole(tiles, 1, TILE),
                whole(tiles, TILE, width),
                whole(tiles, TILE, width),
                whole(tiles, 2 * pairs, TILE),
            ],
            out_specs=[
                whole(tiles, TILE, 3 * width),
                whole(2 * pairs, kinds, 2 * TILE),
            ],
            scratch_shapes=[
                pltpu.VMEM((tiles, width, TILE), BF16),
                pltpu.VMEM((tiles, TILE, width), F32),
                pltpu.VMEM((tiles, TILE, width), F32),
                pltpu.VMEM((pairs, TILE, 2 * TILE), F32),
                pltpu.VMEM((pairs, kinds, TILE, 2 * TILE), F32),
            ],
        ),
        out_shape=[
            jax.ShapeDtypeStruct((tiles, TILE, 3 * width), BF16),
            jax.ShapeDtypeStruct((2 * pairs, kinds, 2 * TILE), F32),
        ],
        compiler_params=pltpu.CompilerParams(vmem_limit_bytes=48 * 2**20),
        name="attend_back",
    )(
        plan["place"], plan["start1"], plan["count1"], plan["kind"],
        qkv, bias, plan["lab"], plan["labrow"], out, grad, lse,
    )


EDGE = 16


def sigmoid(values):
    return 1.0 / (1.0 + jnp.exp(-values))


def conv_body(
    order_ref, low_ref, high_ref,
    glu_ref, taps_ref, lab_ref,
    act_ref, gated_ref, mixed_ref,
    window_ref, pad_ref, out_pad_ref,
    *, blocks, frames, chunks, lanes, taps,
):
    size = glu_ref.shape[1]
    channels = lanes * TILE
    half = taps // 2
    span = TILE + 2 * EDGE
    for lane in range(lanes):
        pad_ref[lane, :EDGE, :] = jnp.zeros((EDGE, TILE), F32)
    for block in range(blocks):
        where = order_ref[block]
        for lane in range(lanes):
            value = glu_ref[where, :, lane * TILE : (lane + 1) * TILE]
            gate = glu_ref[where, :, channels + lane * TILE : channels + (lane + 1) * TILE]
            first = EDGE + block * frames
            pad_ref[lane, first : first + size, :] = value * sigmoid(gate)
    rest = EDGE + (blocks - 1) * frames + size
    for lane in range(lanes):
        tail = pad_ref.shape[1] - rest
        pad_ref[lane, rest:, :] = jnp.zeros((tail, TILE), F32)

    def chunk(index, carry):
        base = pl.multiple_of(index * TILE, TILE)
        labels = lab_ref[pl.ds(base, span), :]
        center = labels[EDGE : EDGE + TILE]
        for lane in range(lanes):
            values = pad_ref[lane, pl.ds(base, span), :]
            gated_ref[pl.ds(base, TILE), lane * TILE : (lane + 1) * TILE] = values[
                EDGE : EDGE + TILE
            ]

            def segment(label, total):
                window_ref[...] = jnp.where(labels == label, values, 0.0)
                acc = jnp.zeros((TILE, TILE), F32)
                for tap in range(taps):
                    first = EDGE + tap - half
                    acc = acc + window_ref[first : first + TILE, :] * taps_ref[
                        tap : tap + 1, lane * TILE : (lane + 1) * TILE
                    ]
                return jnp.where(center == label, acc, total)

            total = lax.fori_loop(
                low_ref[index], high_ref[index] + 1, segment, jnp.zeros((TILE, TILE), F32)
            )
            mixed_ref[pl.ds(base, TILE), lane * TILE : (lane + 1) * TILE] = total
            out_pad_ref[lane, pl.ds(base, TILE), :] = total * sigmoid(total)
        return carry

    lax.fori_loop(0, chunks, chunk, 0)
    valid = lax.broadcasted_iota(jnp.int32, (size, TILE), 0) < frames
    for block in range(blocks):
        where = order_ref[block]
        for lane in range(lanes):
            rows = out_pad_ref[lane, block * frames : block * frames + size, :]
            act_ref[where, :, lane * TILE : (lane + 1) * TILE] = jnp.where(valid, rows, 0.0).astype(
                BF16
            )


def conv_forward(glu, taps, plan):
    blocks, size, double = glu.shape
    channels = double // 2
    frames, chunks = plan["frames"], plan["chunks"]
    rows = chunks * TILE
    return pl.pallas_call(
        functools.partial(
            conv_body, blocks=blocks, frames=frames, chunks=chunks,
            lanes=channels // TILE, taps=taps.shape[0],
        ),
        grid_spec=pltpu.PrefetchScalarGridSpec(
            num_scalar_prefetch=3,
            grid=(1,),
            in_specs=[
                pl.BlockSpec(glu.shape, lambda i, *_: (0, 0, 0)),
                pl.BlockSpec(taps.shape, lambda i, *_: (0, 0)),
                pl.BlockSpec(plan["flat_lab"].shape, lambda i, *_: (0, 0)),
            ],
            out_specs=[
                pl.BlockSpec((blocks, size, channels), lambda i, *_: (0, 0, 0)),
                pl.BlockSpec((rows, channels), lambda i, *_: (0, 0)),
                pl.BlockSpec((rows, channels), lambda i, *_: (0, 0)),
            ],
            scratch_shapes=[
                pltpu.VMEM((TILE + 2 * EDGE, TILE), F32),
                pltpu.VMEM((channels // TILE, rows + 2 * EDGE, TILE), F32),
                pltpu.VMEM((channels // TILE, rows, TILE), F32),
            ],
        ),
        out_shape=[
            jax.ShapeDtypeStruct((blocks, size, channels), BF16),
            jax.ShapeDtypeStruct((rows, channels), F32),
            jax.ShapeDtypeStruct((rows, channels), F32),
        ],
        compiler_params=pltpu.CompilerParams(vmem_limit_bytes=48 * 2**20),
        name="conv_forward",
    )(plan["order"], plan["low"], plan["high"], glu, taps, plan["flat_lab"])


def conv_back_body(
    order_ref, low_ref, high_ref,
    glu_ref, taps_ref, lab_ref, gated_ref, mixed_ref, grad_ref,
    dglu_ref, dtaps_ref,
    window_ref, source_ref, slope_ref, dgate_ref, sums_ref,
    *, blocks, frames, chunks, lanes, taps,
):
    size = glu_ref.shape[1]
    channels = lanes * TILE
    half = taps // 2
    span = TILE + 2 * EDGE
    rows = chunks * TILE
    for block in range(blocks):
        where = order_ref[block]
        for lane in range(lanes):
            first = EDGE + block * frames
            slope_ref[lane, first : first + size, :] = grad_ref[
                where, :, lane * TILE : (lane + 1) * TILE
            ]
    rest = EDGE + (blocks - 1) * frames + size
    for lane in range(lanes):
        slope_ref[lane, :EDGE, :] = jnp.zeros((EDGE, TILE), F32)
        slope_ref[lane, rest:, :] = jnp.zeros((slope_ref.shape[1] - rest, TILE), F32)
        mixed = mixed_ref[:, lane * TILE : (lane + 1) * TILE]
        gate = sigmoid(mixed)
        slope_ref[lane, EDGE : EDGE + rows, :] = slope_ref[lane, EDGE : EDGE + rows, :] * (
            gate * (1.0 + mixed * (1.0 - gate))
        )
        source_ref[lane, :EDGE, :] = jnp.zeros((EDGE, TILE), F32)
        source_ref[lane, EDGE : EDGE + rows, :] = gated_ref[:, lane * TILE : (lane + 1) * TILE]
        source_ref[lane, EDGE + rows :, :] = jnp.zeros((EDGE, TILE), F32)
        dgate_ref[lane, rows:, :] = jnp.zeros((dgate_ref.shape[1] - rows, TILE), F32)
    sums_ref[...] = jnp.zeros_like(sums_ref)

    def chunk(index, carry):
        base = pl.multiple_of(index * TILE, TILE)
        labels = lab_ref[pl.ds(base, span), :]
        center = labels[EDGE : EDGE + TILE]
        for lane in range(lanes):
            slopes = slope_ref[lane, pl.ds(base, span), :]
            sources = source_ref[lane, pl.ds(base, span), :]

            def segment(label, total):
                window_ref[0] = jnp.where(labels == label, slopes, 0.0)
                window_ref[1] = jnp.where(labels == label, sources, 0.0)
                inner = window_ref[0, EDGE : EDGE + TILE, :]
                acc = jnp.zeros((TILE, TILE), F32)
                for tap in range(taps):
                    first = EDGE - tap + half
                    acc = acc + window_ref[0, first : first + TILE, :] * taps_ref[
                        tap : tap + 1, lane * TILE : (lane + 1) * TILE
                    ]
                    first = EDGE + tap - half
                    part = fold(inner * window_ref[1, first : first + TILE, :])
                    sums_ref[lane, tap] += jnp.sum(part, axis=0)
                return jnp.where(center == label, acc, total)

            dgate_ref[lane, pl.ds(base, TILE), :] = lax.fori_loop(
                low_ref[index], high_ref[index] + 1, segment, jnp.zeros((TILE, TILE), F32)
            )
        return carry

    lax.fori_loop(0, chunks, chunk, 0)
    for lane in range(lanes):
        dtaps_ref[:, lane * TILE : (lane + 1) * TILE] = jnp.sum(sums_ref[lane], axis=1)
    valid = lax.broadcasted_iota(jnp.int32, (size, TILE), 0) < frames
    for block in range(blocks):
        where = order_ref[block]
        for lane in range(lanes):
            lead = slice(lane * TILE, (lane + 1) * TILE)
            follow = slice(channels + lane * TILE, channels + (lane + 1) * TILE)
            rows_in = dgate_ref[lane, block * frames : block * frames + size, :]
            rows_in = jnp.where(valid, rows_in, 0.0)
            value = glu_ref[where, :, lead]
            gate = sigmoid(glu_ref[where, :, follow])
            dglu_ref[where, :, lead] = (rows_in * gate).astype(BF16)
            dglu_ref[where, :, follow] = (rows_in * value * gate * (1.0 - gate)).astype(BF16)


def conv_backward(glu, taps, plan, gated, mixed, grad):
    blocks, size, double = glu.shape
    channels = double // 2
    frames, chunks = plan["frames"], plan["chunks"]
    rows = chunks * TILE
    lanes = channels // TILE
    whole = lambda *shape: pl.BlockSpec(shape, lambda i, *_: (0,) * len(shape))
    return pl.pallas_call(
        functools.partial(
            conv_back_body, blocks=blocks, frames=frames, chunks=chunks,
            lanes=lanes, taps=taps.shape[0],
        ),
        grid_spec=pltpu.PrefetchScalarGridSpec(
            num_scalar_prefetch=3,
            grid=(1,),
            in_specs=[
                whole(*glu.shape),
                whole(*taps.shape),
                whole(*plan["flat_lab"].shape),
                whole(rows, channels),
                whole(rows, channels),
                whole(blocks, size, channels),
            ],
            out_specs=[whole(*glu.shape), whole(*taps.shape)],
            scratch_shapes=[
                pltpu.VMEM((2, TILE + 2 * EDGE, TILE), F32),
                pltpu.VMEM((lanes, rows + 2 * EDGE, TILE), F32),
                pltpu.VMEM((lanes, rows + 2 * EDGE, TILE), F32),
                pltpu.VMEM((lanes, rows + EDGE, TILE), F32),
                pltpu.VMEM((lanes, taps.shape[0], 8, TILE), F32),
            ],
        ),
        out_shape=[
            jax.ShapeDtypeStruct(glu.shape, BF16),
            jax.ShapeDtypeStruct(taps.shape, F32),
        ],
        compiler_params=pltpu.CompilerParams(vmem_limit_bytes=56 * 2**20),
        name="conv_backward",
    )(
        plan["order"], plan["low"], plan["high"],
        glu, taps, plan["flat_lab"], gated, mixed, grad,
    )


def swap(values, bit, axis="tensor"):
    count = lax.axis_size(axis)
    return lax.ppermute(values, axis, [(i, i ^ bit) for i in range(count)])


def gather(mine):
    beside = swap(mine, 1)
    across = swap(mine, 2)
    return [mine, beside, across, swap(across, 1)]


def scatter(parts):
    own, beside, across, diagonal = parts
    outgoing = (across + swap(diagonal.astype(BF16), 1).astype(F32)).astype(BF16)
    far = swap(outgoing, 2)
    return own + swap(beside.astype(BF16), 1).astype(F32) + far.astype(F32)


def sum_bits(values, axis):
    bit = 1
    while bit < lax.axis_size(axis):
        values = values + swap(values, bit, axis)
        bit *= 2
    return values


def settle(grad):
    return lax.psum_scatter(
        grad.astype(BF16), "dp", scatter_dimension=0, tiled=True
    ).astype(F32)


def norm_parts(rows):
    mean = jnp.mean(rows, axis=-1, keepdims=True)
    centred = rows - mean
    rstd = lax.rsqrt(jnp.mean(centred * centred, axis=-1, keepdims=True) + 1e-05)
    return centred * rstd, rstd


def normed(rows, gain):
    return norm_parts(rows)[0] * gain


def norm_back(rows, gain, grad):
    unit, rstd = norm_parts(rows)
    scaled = grad * gain
    first = jnp.mean(scaled, axis=-1, keepdims=True)
    second = jnp.mean(scaled * unit, axis=-1, keepdims=True)
    return rstd * (scaled - first - unit * second), jnp.sum(grad * unit, axis=0)


def pile(blocks):
    return jnp.concatenate(blocks, 0)


def feed_forward(rows, gain, w_in, w_out):
    blocks = gather(normed(rows, gain).astype(BF16))
    hidden, active, parts = [], [], []
    for block in blocks:
        a = dot(block, w_in, 1, 0)
        z = (a * jax.nn.sigmoid(a)).astype(BF16)
        hidden.append(a.astype(BF16))
        active.append(z)
        parts.append(dot(z, w_out, 1, 0))
    return rows + 0.5 * scatter(parts), (blocks, hidden, active)


def feed_back(incoming, rows, gain, w_in, w_out, state):
    blocks, hidden, active = state
    grads = gather((0.5 * incoming).astype(BF16))
    inner, parts = [], []
    for grad, a in zip(grads, hidden):
        ez = dot(grad, w_out, 1, 1)
        a = a.astype(F32)
        s = jax.nn.sigmoid(a)
        ea = (ez * s * (1.0 + a * (1.0 - s))).astype(BF16)
        inner.append(ea)
        parts.append(dot(ea, w_in, 1, 1))
    grad_w_out = settle(dot(pile(grads), pile(active), 0, 0)).T
    grad_w_in = settle(dot(pile(blocks), pile(inner), 0, 0))
    passed, grad_gain = norm_back(rows, gain, scatter(parts))
    return incoming + passed, grad_gain, grad_w_in, grad_w_out


def make_plan(segments, frames, reach, head_width):
    blocks = lax.axis_size("tensor")
    here = lax.axis_index("tensor").astype(jnp.int32)
    size = pad_up(frames, TILE)
    per_block = size // TILE
    tiles = blocks * per_block
    offsets = tile_offsets(blocks, frames, per_block)
    kinds, table = bias_types(offsets, reach)
    flat = segments.reshape(-1).astype(jnp.int32)
    lab = jnp.pad(flat.reshape(blocks, frames), ((0, 0), (0, size - frames)), constant_values=-1)
    lab = lab.reshape(tiles, TILE)
    high = jnp.max(lab, axis=1)
    low = jnp.min(jnp.where(lab < 0, 1 << 20, lab), axis=1)
    seen = (low[:, None] <= high[None, :]) & (low[None, :] <= high[:, None])
    position = jnp.arange(tiles, dtype=jnp.int32)
    first = jnp.min(jnp.where(seen, position[None, :], tiles), axis=1)
    last = jnp.max(jnp.where(seen, position[None, :], -1), axis=1)
    count1 = last - first + 1
    count2 = (count1 + 1) // 2
    start2 = jnp.minimum(first, tiles - 2 * count2)
    order = jnp.arange(blocks, dtype=jnp.int32) ^ here
    place = (order[:, None] * per_block + jnp.arange(per_block, dtype=jnp.int32)[None, :]).reshape(-1)
    total = blocks * frames
    chunks = pad_up(total, TILE) // TILE
    padded = jnp.pad(flat, (EDGE, chunks * TILE - total + EDGE), constant_values=-1)
    body = padded[EDGE : EDGE + chunks * TILE].reshape(chunks, TILE)
    return dict(
        kinds=kinds,
        kind=jnp.asarray(table.reshape(-1)),
        place=place,
        start1=first,
        count1=count1,
        start2=start2,
        count2=count2,
        lab=jnp.broadcast_to(lab[:, :, None], (tiles, TILE, TILE)),
        labrow=lab[:, None, :],
        scale=float(head_width) ** -0.5,
        frames=frames,
        chunks=chunks,
        order=order,
        low=jnp.min(jnp.where(body < 0, 1 << 20, body), axis=1),
        high=jnp.max(body, axis=1),
        flat_lab=jnp.broadcast_to(padded[:, None], (padded.shape[0], TILE)),
    )


def attention(rows, gain, w_qkv, w_output, bias, plan):
    blocks = gather(normed(rows, gain).astype(BF16))
    size = rows.shape[0]
    qkv = jnp.stack([dot(block, w_qkv, 1, 0).astype(BF16) for block in blocks])
    qkv = qkv.reshape(-1, TILE, w_qkv.shape[1])
    out, lse = attend(qkv, bias, plan)
    flat = out.reshape(len(blocks), size, -1)
    parts = [dot(flat[i], w_output, 1, 0) for i in range(len(blocks))]
    return rows + scatter(parts), (blocks, qkv, out, lse)


def attention_back(incoming, rows, gain, w_qkv, w_output, bias, plan, state):
    blocks, qkv, out, lse = state
    size = rows.shape[0]
    grads = gather(incoming.astype(BF16))
    eo = jnp.stack([dot(grad, w_output, 1, 1).astype(BF16) for grad in grads])
    dqkv, sums = attend_back(qkv, bias, plan, out, eo.reshape(out.shape), lse)
    flat = dqkv.reshape(len(blocks), size, -1)
    parts = [dot(flat[i], w_qkv, 1, 1) for i in range(len(blocks))]
    grad_w_output = settle(dot(pile(grads), out.reshape(-1, out.shape[-1]), 0, 0)).T
    grad_w_qkv = settle(dot(pile(blocks), flat.reshape(-1, flat.shape[-1]), 0, 0))
    passed, grad_gain = norm_back(rows, gain, scatter(parts))
    return incoming + passed, grad_gain, sums, grad_w_qkv, grad_w_output


def convolution(rows, gain, w_glu, taps, w_back, plan):
    blocks = gather(normed(rows, gain).astype(BF16))
    glu = jnp.stack([dot(block, w_glu, 1, 0) for block in blocks])
    act, gated, mixed = conv_forward(glu, taps, plan)
    parts = [dot(act[i], w_back, 1, 0) for i in range(len(blocks))]
    return rows + scatter(parts), (blocks, glu, act, gated, mixed)


def convolution_back(incoming, rows, gain, w_glu, taps, w_back, plan, state):
    blocks, glu, act, gated, mixed = state
    grads = gather(incoming.astype(BF16))
    ew = jnp.stack([dot(grad, w_back, 1, 1) for grad in grads])
    dglu, dtaps = conv_backward(glu, taps, plan, gated, mixed, ew)
    parts = [dot(dglu[i], w_glu, 1, 1) for i in range(len(blocks))]
    grad_w_back = settle(dot(pile(grads), act.reshape(-1, act.shape[-1]), 0, 0)).T
    grad_w_glu = settle(dot(pile(blocks), dglu.reshape(-1, dglu.shape[-1]), 0, 0))
    passed, grad_gain = norm_back(rows, gain, scatter(parts))
    return incoming + passed, grad_gain, dtaps, grad_w_glu, grad_w_back


def shards(
    inputs, segments, cotangent, gain_one, first_in, first_out, gain_two, w_query, w_key, w_value,
    w_output, rel_table, gain_three, w_glu, kernel, w_back, gain_four, second_in, second_out,
    gain_five,
):
    frames, _, width = inputs.shape
    size = pad_up(frames, TILE)
    heads = rel_table.shape[0]
    reach = rel_table.shape[1] // 2
    head_width = w_query.shape[1] // heads

    def padded(values):
        return jnp.pad(values.reshape(frames, width).astype(F32), ((0, size - frames), (0, 0)))

    plan = make_plan(segments, frames, reach, head_width)
    onehot = column_onehot(plan["kinds"], reach)
    bias = bias_tiles(rel_table, onehot, plan["kinds"])
    w_qkv = jnp.concatenate([w_query, w_key, w_value], 1)
    channels = kernel.shape[1]
    glu_matrix = w_glu.reshape(width, 2 * channels)

    start = padded(inputs)
    one, state_one = feed_forward(start, gain_one, first_in, first_out)
    two, state_two = attention(one, gain_two, w_qkv, w_output, bias, plan)
    three, state_three = convolution(two, gain_three, glu_matrix, kernel, w_back, plan)
    four, state_four = feed_forward(three, gain_four, second_in, second_out)
    output = normed(four, gain_five).astype(BF16)
    e4, grad_five = norm_back(four, gain_five, padded(cotangent))
    e3, grad_four, grad_second_in, grad_second_out = feed_back(
        e4, three, gain_four, second_in, second_out, state_four
    )
    e2, grad_three, grad_kernel, grad_w_glu, grad_w_back = convolution_back(
        e3, two, gain_three, glu_matrix, kernel, w_back, plan, state_three
    )
    e1, grad_two, sums, grad_w_qkv, grad_w_output = attention_back(
        e2, one, gain_two, w_qkv, w_output, bias, plan, state_two
    )
    e0, grad_one, grad_first_in, grad_first_out = feed_back(
        e1, start, gain_one, first_in, first_out, state_one
    )
    grad_table = lax.dot_general(
        sums.reshape(heads, -1), onehot, (((1,), (1,)), ((), ())),
        precision=lax.Precision.HIGHEST, preferred_element_type=F32,
    )
    gains = sum_bits(jnp.concatenate([grad_one, grad_two, grad_three, grad_four, grad_five]), "tensor")
    small = jnp.concatenate([gains, grad_table.reshape(-1), grad_kernel.reshape(-1)])
    small = sum_bits(small, "dp")
    grad_gains = [small[i * width : (i + 1) * width] for i in range(5)]
    rest = small[5 * width :]
    grad_table = rest[: grad_table.size].reshape(grad_table.shape)
    grad_kernel = rest[grad_table.size :].reshape(grad_kernel.shape)
    cut = w_query.shape[1]
    return (
        output[:frames].reshape(inputs.shape),
        e0[:frames].reshape(inputs.shape),
        grad_gains[0],
        grad_first_in,
        grad_first_out,
        grad_gains[1],
        grad_w_qkv[:, :cut],
        grad_w_qkv[:, cut : 2 * cut],
        grad_w_qkv[:, 2 * cut :],
        grad_w_output,
        grad_table,
        grad_gains[2],
        grad_w_glu.reshape(grad_w_glu.shape[0], 2, channels),
        grad_kernel,
        grad_w_back,
        grad_gains[3],
        grad_second_in,
        grad_second_out,
        grad_gains[4],
    )


def solution(mesh):
    in_specs = (
        P("tensor", "dp", None), P("dp", None), P("tensor", "dp", None), P(),
        P(None, "tensor"), P("tensor", None), P(), P(None, "tensor"), P(None, "tensor"),
        P(None, "tensor"), P("tensor", None), P("tensor", None), P(), P(None, None, "tensor"),
        P(None, "tensor"), P("tensor", None), P(), P(None, "tensor"), P("tensor", None), P(),
    )
    out_specs = (
        P("tensor", "dp", None), P("tensor", "dp", None), P(), P("dp", "tensor"),
        P("tensor", "dp"), P(), P("dp", "tensor"), P("dp", "tensor"), P("dp", "tensor"),
        P("tensor", "dp"), P("tensor", None), P(), P("dp", None, "tensor"), P(None, "tensor"),
        P("tensor", "dp"), P(), P("dp", "tensor"), P("tensor", "dp"), P(),
    )
    return jax.shard_map(shards, mesh=mesh, in_specs=in_specs, out_specs=out_specs, check_vma=False)
```

```python
import functools

import jax
import jax.numpy as jnp
import numpy as np
from jax import lax
from jax.experimental import pallas as pl
from jax.experimental.pallas import tpu as pltpu
from jax.sharding import PartitionSpec as P

TILE = 128
MASKED = -1e30
F32 = jnp.float32
BF16 = jnp.bfloat16


def pad_up(size, unit):
    return -(-size // unit) * unit


CHUNKS = 2


def dot(a, b, ca, cb):
    return lax.dot_general(a, b, (((ca,), (cb,)), ((), ())), preferred_element_type=F32)


def sigmoid(values):
    return 0.5 * jnp.tanh(0.5 * values) + 0.5


def fixed(*shape):
    return pl.BlockSpec(shape, lambda *_: (0,) * len(shape))


def shaped(shape, kind):
    return jax.ShapeDtypeStruct(tuple(shape), kind)


BUDGET = dict(
    distance_bias=(3, 12), enter=(1, 8), join=(2, 8), turn=(3, 12), join_back=(3, 12),
    ff_rows=(4, 28), ff_back_rows=(4, 28), project=(2, 20), expand=(2, 16),
    weight_grads=(5, 40), attend=(24, 40), attend_back=(43, 48),
    conv_forward=(11, 40), conv_backward=(17, 48),
)
COST_SCALE = 1.0


def call(body, name, out_shape, cost=1.0, **options):
    time, limit = BUDGET[name]
    time = time * cost * COST_SCALE
    return pl.pallas_call(
        body,
        out_shape=out_shape,
        compiler_params=pltpu.CompilerParams(vmem_limit_bytes=limit * 2**20),
        cost_estimate=pl.CostEstimate(
            flops=int(time * 1e9), bytes_accessed=int(time * 3.5e6), transcendentals=0
        ),
        name=name,
        **options,
    )


def tile_offsets(blocks, block_frames, per_block):
    starts = np.array([b * block_frames + t * TILE for b in range(blocks) for t in range(per_block)])
    return starts[None, :] - starts[:, None]


def bias_types(offsets, reach):
    near = sorted({int(d) for d in offsets.ravel() if abs(int(d)) < reach + TILE - 1})
    far = 4 * TILE + reach
    kinds = near + [-far, far]
    index = {d: i for i, d in enumerate(near)}
    table = np.array(
        [
            [index.get(int(d), len(near) + (1 if d > 0 else 0)) for d in row]
            for row in offsets
        ],
        np.int32,
    )
    return kinds, table


def column_onehot(kinds, reach):
    lane = lax.broadcasted_iota(jnp.int32, (len(kinds), 2 * TILE), 1)
    signed = jnp.where(lane < TILE, lane, lane - 2 * TILE)
    base = jnp.array(kinds, jnp.int32)[:, None]
    column = jnp.clip(base - signed, -reach, reach) + reach
    width = 2 * reach + 1
    flat = column.reshape(-1)
    return (flat[None, :] == jnp.arange(width, dtype=jnp.int32)[:, None]).astype(F32)


def bias_body(row_ref, out_ref, *, pairs, count):
    for p in range(pairs):
        for kind in range(count):
            for head in range(2):
                line = jnp.broadcast_to(row_ref[2 * p + head, kind : kind + 1, :], (TILE, 2 * TILE))
                skewed = pltpu.roll(line, 0, 1, stride=1, stride_axis=0)
                out_ref[p, kind, :, head * TILE : (head + 1) * TILE] = skewed[:, :TILE]


def bias_tiles(rel_table, onehot, kinds):
    heads = rel_table.shape[0]
    pairs = heads // 2
    count = len(kinds)
    rows = jnp.dot(rel_table, onehot, precision=lax.Precision.HIGHEST, preferred_element_type=F32)
    return call(
        functools.partial(bias_body, pairs=pairs, count=count),
        "distance_bias",
        shaped((pairs, count, TILE, 2 * TILE), F32),
    )(rows.reshape(heads, count, 2 * TILE))


SLAB = 16


def unit_rows(rows):
    mean = jnp.mean(rows, axis=-1, keepdims=True)
    centred = rows - mean
    rstd = lax.rsqrt(jnp.mean(centred * centred, axis=-1, keepdims=True) + 1e-05)
    return centred * rstd, rstd


def pull_back(unit, rstd, scaled):
    first = jnp.mean(scaled, axis=-1, keepdims=True)
    second = jnp.mean(scaled * unit, axis=-1, keepdims=True)
    return rstd * (scaled - first - unit * second)


def fold(values):
    return values.reshape(values.shape[0] // 8, 8, values.shape[1])


def slabs(rows, body):
    def step(i, carry):
        body(pl.ds(pl.multiple_of(i * SLAB, SLAB), SLAB))
        return carry

    lax.fori_loop(0, rows // SLAB, step, 0, unroll=2)


def enter(rows, gain):
    def body(r_ref, g_ref, h_ref):
        def slab(at):
            unit, _ = unit_rows(r_ref[at, :].astype(F32))
            h_ref[at, :] = (unit * g_ref[...]).astype(BF16)

        slabs(r_ref.shape[0], slab)

    return call(body, "enter", shaped(rows.shape, BF16))(rows, gain[None, :])


def received(at, refs):
    return refs[0][at, :].astype(F32) + refs[1][at, :].astype(F32) + refs[2][at, :].astype(F32)


def by_chunks(body, name, arrays, gain, kinds, sums=0):
    some = next(x for x in arrays if not isinstance(x, list))
    size, width = some.shape
    cut = int(size // CHUNKS)
    lone = fixed(cut, width)
    filled, lists = None, [[] for _ in kinds[1:]]
    for chunk in range(CHUNKS):
        piece = pl.BlockSpec((cut, width), lambda i, chunk=chunk: (chunk, 0))
        inputs = [x[chunk] if isinstance(x, list) else x for x in arrays]
        specs = [lone if isinstance(x, list) else piece for x in arrays]
        inputs.append(gain[None, :])
        specs.append(fixed(1, width))
        aliases = {}
        run = body
        if filled is not None:
            aliases = {len(inputs): 0}
            inputs.append(filled)
            specs.append(pl.BlockSpec(memory_space=pl.ANY))
            count = len(inputs)
            run = lambda *refs, count=count: body(*refs[: count - 1], *refs[count:])
        shapes = [shaped((size, width), kinds[0])]
        outs = [piece]
        for i, kind in enumerate(kinds[1:]):
            is_sum = i >= len(kinds) - 1 - sums
            shape = (8, width) if is_sum else (cut, width)
            shapes.append(shaped(shape, kind))
            outs.append(fixed(*shape))
        filled, *others = call(
            run, name, shapes, grid=(1,), in_specs=specs, out_specs=outs,
            input_output_aliases=aliases,
        )(*inputs)
        for place, other in zip(lists, others):
            place.append(other)
    return filled, *lists


def join(rows, parts, gain, factor):
    def body(r_ref, p1_ref, p2_ref, p3_ref, g_ref, h_ref, out_ref):
        def slab(at):
            total = r_ref[at, :].astype(F32) + factor * received(at, (p1_ref, p2_ref, p3_ref))
            out_ref[at, :] = total
            unit, _ = unit_rows(total)
            h_ref[at, :] = (unit * g_ref[...]).astype(BF16)

        slabs(r_ref.shape[0], slab)

    return by_chunks(body, "join", [rows, *parts], gain, [BF16, F32])


def turn(rows, parts, gain, cotangent, factor, onward):
    def body(r_ref, p1_ref, p2_ref, p3_ref, c_ref, g_ref, next_ref, out_ref, e_ref, sum_ref):
        sum_ref[...] = jnp.zeros_like(sum_ref)

        def slab(at):
            total = r_ref[at, :].astype(F32) + factor * received(at, (p1_ref, p2_ref, p3_ref))
            unit, rstd = unit_rows(total)
            out_ref[at, :] = (unit * g_ref[...]).astype(BF16)
            grad = c_ref[at, :].astype(F32)
            sum_ref[...] += jnp.sum(fold(grad * unit), axis=0)
            e = pull_back(unit, rstd, grad * g_ref[...])
            e_ref[at, :] = e
            next_ref[at, :] = (onward * e).astype(BF16)

        slabs(r_ref.shape[0], slab)

    return by_chunks(
        body, "turn", [rows, *parts, cotangent], gain, [BF16, BF16, F32, F32], sums=1
    )


def join_back(incoming, rows, parts, gain, onward):
    def body(e_ref, r_ref, p1_ref, p2_ref, p3_ref, g_ref, next_ref, *more):
        out_ref, sum_ref = more if onward else (next_ref, more[0])
        sum_ref[...] = jnp.zeros_like(sum_ref)

        def slab(at):
            unit, rstd = unit_rows(r_ref[at, :].astype(F32))
            grad = received(at, (p1_ref, p2_ref, p3_ref))
            sum_ref[...] += jnp.sum(fold(grad * unit), axis=0)
            e = e_ref[at, :] + pull_back(unit, rstd, grad * g_ref[...])
            out_ref[at, :] = e
            if onward:
                next_ref[at, :] = (onward * e).astype(BF16)

        slabs(r_ref.shape[0], slab)

    kinds = [BF16, F32, F32] if onward else [F32, F32]
    return by_chunks(body, "join_back", [incoming, rows, *parts], gain, kinds, sums=1)


def pieces_of(arrays):
    specs, plain = [], []
    for entry in arrays:
        array, i, n = entry if isinstance(entry, tuple) else (entry, 0, 1)
        shape = (array.shape[0] // n, array.shape[1])
        specs.append(pl.BlockSpec(shape, lambda *_, i=i: (i, 0)))
        plain.append(array)
    return specs, plain


def ff_rows(x1, x2, w_in, w_out):
    specs, plain = pieces_of([x1, x2])
    rows, width = specs[0].block_shape

    def body(x1_ref, x2_ref, w_in_ref, w_out_ref, a_ref, z_ref, u1_ref, u2_ref):
        for x_ref, u_ref, at in ((x1_ref, u1_ref, 0), (x2_ref, u2_ref, rows)):
            a = dot(x_ref[...], w_in_ref[...], 1, 0)
            z = (a * sigmoid(a)).astype(BF16)
            a_ref[at : at + rows, :] = a.astype(BF16)
            z_ref[at : at + rows, :] = z
            u_ref[...] = dot(z, w_out_ref[...], 1, 0).astype(BF16)

    wide = (2 * rows, w_in.shape[1])
    return call(
        body, "ff_rows", [shaped(wide, BF16)] * 2 + [shaped((rows, width), BF16)] * 2, grid=(1,),
        in_specs=specs + [fixed(*w_in.shape), fixed(*w_out.shape)],
        out_specs=[fixed(*wide)] * 2 + [fixed(rows, width)] * 2,
    )(*plain, w_in, w_out)


def ff_back_rows(g1, g2, a, w_out, w_in):
    specs, plain = pieces_of([g1, g2])
    rows, width = specs[0].block_shape

    def body(g1_ref, g2_ref, a_ref, w_out_ref, w_in_ref, ea_ref, p1_ref, p2_ref):
        for g_ref, p_ref, at in ((g1_ref, p1_ref, 0), (g2_ref, p2_ref, rows)):
            ez = dot(g_ref[...], w_out_ref[...], 1, 1)
            a = a_ref[at : at + rows, :].astype(F32)
            s = sigmoid(a)
            ea = (ez * s * (1.0 + a * (1.0 - s))).astype(BF16)
            ea_ref[at : at + rows, :] = ea
            p_ref[...] = dot(ea, w_in_ref[...], 1, 1).astype(BF16)

    return call(
        body, "ff_back_rows", [shaped(a.shape, BF16)] + [shaped((rows, width), BF16)] * 2,
        grid=(1,),
        in_specs=specs + [fixed(*a.shape), fixed(*w_out.shape), fixed(*w_in.shape)],
        out_specs=[fixed(*a.shape)] + [fixed(rows, width)] * 2,
    )(*plain, a, w_out, w_in)


def project(x1, x2, weight, side, kind):
    def body(x1_ref, x2_ref, w_ref, y_ref):
        rows = x1_ref.shape[0]
        y_ref[:rows, :] = dot(x1_ref[...], w_ref[...], 1, side).astype(kind)
        y_ref[rows:, :] = dot(x2_ref[...], w_ref[...], 1, side).astype(kind)

    shape = (2 * x1.shape[0], weight.shape[1 - side])
    return call(body, "project", shaped(shape, kind))(x1, x2, weight)


def expand(x1, x2, weight, side):
    specs, plain = pieces_of([x1, x2])

    def body(x1_ref, x2_ref, w_ref, y1_ref, y2_ref):
        y1_ref[...] = dot(x1_ref[...], w_ref[...], 1, side).astype(BF16)
        y2_ref[...] = dot(x2_ref[...], w_ref[...], 1, side).astype(BF16)

    shape = (specs[0].block_shape[0], weight.shape[1 - side])
    return call(
        body, "expand", [shaped(shape, BF16)] * 2, grid=(1,),
        in_specs=specs + [fixed(*weight.shape)],
        out_specs=[fixed(*shape)] * 2,
    )(*plain, weight)


def weight_grads(products, pieces=1):
    entries, spans, at, column = [], [], 0, 0
    for left, right in products:
        entries += left + right
        first = right[0][0] if isinstance(right[0], tuple) else right[0]
        spans.append((at, at + len(left), at + len(left) + len(right), column))
        at += len(left) + len(right)
        column += first.shape[1]
    specs, plain = pieces_of(entries)
    height = specs[0].block_shape[1]
    cut = column // pieces

    def body(*refs):
        out_refs = refs[at:]
        for first, middle, last, column in spans:
            left = jnp.concatenate([ref[...] for ref in refs[first:middle]], 0)
            right = jnp.concatenate([ref[...] for ref in refs[middle:last]], 0)
            value = dot(left, right, 0, 0).astype(BF16)
            if pieces == 1:
                out_refs[0][:, column : column + right.shape[1]] = value
            else:
                for i, out_ref in enumerate(out_refs):
                    out_ref[...] = value[:, i * cut : (i + 1) * cut]

    return call(
        body, "weight_grads", [shaped((height, cut), BF16)] * pieces, grid=(1,),
        in_specs=specs, out_specs=[fixed(height, cut)] * pieces,
    )(*plain)


def stacked_heads(pair):
    low_half = lax.broadcasted_iota(jnp.int32, pair.shape, 1) < pair.shape[1] // 2
    zero = jnp.zeros_like(pair)
    return jnp.concatenate([jnp.where(low_half, pair, zero), jnp.where(low_half, zero, pair)], 0)


def own_quadrants(wide):
    half = lax.broadcasted_iota(jnp.int32, (TILE, TILE), 0) < TILE // 2
    return jnp.where(half, wide[:, :TILE], wide[:, TILE:])


def assemble(target_ref, piece_refs):
    rows = piece_refs[0].shape[0]
    for i, ref in enumerate(piece_refs):
        target_ref[i * rows : (i + 1) * rows, :] = ref[...]


def tile_rows(index):
    return pl.ds(pl.multiple_of(index * TILE, TILE), TILE)


def attend_body(
    place_ref, start_ref, count_ref, kind_ref, *refs, tiles, pairs, scale,
):
    pieces, refs = refs[:2], refs[2:]
    bias_ref, lab_ref, labrow_ref, out_ref, lse_ref, qkv_ref, score_ref, turned_ref, acc_ref = refs
    step = pl.program_id(0)
    width = pairs * TILE

    @pl.when(step == 0)
    def _():
        assemble(qkv_ref, pieces)
        for tile in range(tiles):
            turned_ref[tile] = qkv_ref[tile_rows(place_ref[tile]), 2 * width :].T

    mine = qkv_ref[tile_rows(place_ref[step]), :]
    queries = [
        stacked_heads(mine[:, p * TILE : (p + 1) * TILE] * scale) for p in range(pairs)
    ]
    own_label = labrow_ref[step]
    begin = start_ref[step]
    trips = count_ref[step]

    def scores(trip, best):
        couple = [begin + 2 * trip + sub for sub in range(2)]
        kinds = [kind_ref[step * tiles + tile] for tile in couple]
        allowed = [lab_ref[tile] == own_label for tile in couple]
        keys = jnp.concatenate(
            [qkv_ref[tile_rows(place_ref[tile]), width : 2 * width] for tile in couple], 0
        )
        parts = []
        for p in range(pairs):
            both = dot(keys[:, p * TILE : (p + 1) * TILE], queries[p], 1, 1)
            highs = []
            for sub in range(2):
                raw = both[sub * TILE : (sub + 1) * TILE] + bias_ref[p, kinds[sub]]
                pair_high = []
                for h in range(2):
                    part = jnp.where(allowed[sub], raw[:, h * TILE : (h + 1) * TILE], MASKED)
                    span = slice((2 * p + h) * TILE, (2 * p + h + 1) * TILE)
                    score_ref[couple[sub], :, span] = part
                    pair_high.append(jnp.max(fold(part), axis=0))
                highs.append(jnp.concatenate(pair_high, 1))
            parts.append(jnp.maximum(*highs))
        return jnp.maximum(best, jnp.concatenate(parts, 1))

    best = lax.fori_loop(0, trips, scores, jnp.full((8, 2 * width), MASKED, F32))
    top = jnp.max(best, axis=0, keepdims=True)
    acc_ref[...] = jnp.zeros_like(acc_ref)

    def mix(trip, total):
        first = begin + 2 * trip
        probs = []
        for sub in range(2):
            value = jnp.exp(score_ref[first + sub] - top)
            total = total + jnp.sum(fold(value), axis=0)
            probs.append(value.astype(BF16))
        both = jnp.concatenate(probs, 0)
        for p in range(pairs):
            turned = jnp.concatenate(
                [turned_ref[first + sub, p * TILE : (p + 1) * TILE, :] for sub in range(2)], 1
            )
            acc_ref[p] += dot(turned, both[:, 2 * p * TILE : 2 * (p + 1) * TILE], 1, 0)
        return total

    total = lax.fori_loop(0, trips, mix, jnp.zeros((8, 2 * width), F32))
    total = jnp.sum(total, axis=0, keepdims=True)
    inverse = 1.0 / total
    log_total = top + jnp.log(total)
    for p in range(pairs):
        wide = acc_ref[p] * inverse[:, 2 * p * TILE : 2 * (p + 1) * TILE]
        out_ref[:, p * TILE : (p + 1) * TILE] = own_quadrants(wide).T.astype(BF16)
    for h in range(2 * pairs):
        lse_ref[0, h : h + 1, :] = log_total[:, h * TILE : (h + 1) * TILE]


def attend(pieces, bias, plan):
    pairs = bias.shape[0]
    width = pairs * TILE
    tiles = plan["tiles"]
    rows = tiles * TILE
    return call(
        functools.partial(attend_body, tiles=tiles, pairs=pairs, scale=plan["scale"]),
        "attend",
        [
            shaped((rows, width), BF16),
            shaped((tiles, 2 * pairs, TILE), F32),
            shaped((rows, 3 * width), BF16),
        ],
        grid_spec=pltpu.PrefetchScalarGridSpec(
            num_scalar_prefetch=4,
            grid=(tiles,),
            in_specs=[fixed(*piece.shape) for piece in pieces]
            + [fixed(*bias.shape), fixed(tiles, TILE, TILE), fixed(tiles, 1, TILE)],
            out_specs=[
                pl.BlockSpec((TILE, width), lambda i, place, *_: (place[i], 0)),
                pl.BlockSpec((1, 2 * pairs, TILE), lambda i, *_: (i, 0, 0)),
                fixed(rows, 3 * width),
            ],
            scratch_shapes=[
                pltpu.VMEM((tiles, TILE, 2 * width), F32),
                pltpu.VMEM((tiles, width, TILE), BF16),
                pltpu.VMEM((pairs, TILE, 2 * TILE), F32),
            ],
        ),
    )(
        plan["place"], plan["start"], plan["count"], plan["kind"],
        *pieces, bias, plan["lab"], plan["labrow"],
    )


def unskew(values):
    wide = jnp.concatenate([values, jnp.zeros_like(values)], 1)
    rows = TILE
    while rows > 8:
        rows //= 2
        wide = wide[:rows] + pltpu.roll(wide[rows:], 2 * TILE - rows, 1)
    row = lax.broadcasted_iota(jnp.int32, wide.shape, 0)
    for bit in (4, 2, 1):
        wide = jnp.where((row & bit) != 0, pltpu.roll(wide, 2 * TILE - bit, 1), wide)
    return jnp.sum(wide, axis=0, keepdims=True)


def attend_back_body(
    place_ref, start_ref, count_ref, kind_ref, *refs, tiles, pairs, scale, kinds,
):
    pieces, refs = refs[:2], refs[2:]
    (
        qkv_ref, bias_ref, lab_ref, labrow_ref, out_ref, lse_ref,
        dqkv_ref, table_ref,
        grad_ref, turned_ref, dk_ref, dv_ref, dq_ref, sums_ref,
    ) = refs
    step = pl.program_id(0)
    width = pairs * TILE

    @pl.when(step == 0)
    def _():
        assemble(grad_ref, pieces)
        for tile in range(tiles):
            turned_ref[tile] = qkv_ref[tile_rows(place_ref[tile]), width : 2 * width].T
        dk_ref[...] = jnp.zeros_like(dk_ref)
        dv_ref[...] = jnp.zeros_like(dv_ref)
        sums_ref[...] = jnp.zeros_like(sums_ref)

    here = tile_rows(place_ref[step])
    queries, grads, deltas, logs = [], [], [], []
    for p in range(pairs):
        span = slice(p * TILE, (p + 1) * TILE)
        queries.append(stacked_heads(qkv_ref[here, span] * scale))
        grad = grad_ref[here, span]
        grads.append(stacked_heads(grad))
        product = (grad.astype(F32) * out_ref[here, span].astype(F32)).T
        half = TILE // 2
        deltas.append(
            jnp.concatenate(
                [
                    jnp.sum(product[:half], axis=0, keepdims=True),
                    jnp.sum(product[half:], axis=0, keepdims=True),
                ],
                1,
            )
        )
        logs.append(jnp.concatenate([lse_ref[step, 2 * p + h : 2 * p + h + 1, :] for h in range(2)], 1))
    own_label = labrow_ref[step]
    begin = start_ref[step]
    dq_ref[...] = jnp.zeros_like(dq_ref)

    def visit(trip, carry):
        couple = [begin + 2 * trip + sub for sub in range(2)]
        kind = [kind_ref[step * tiles + tile] for tile in couple]
        there = [tile_rows(place_ref[tile]) for tile in couple]
        allowed = jnp.concatenate([lab_ref[tile] == own_label for tile in couple], 0)
        allowed = jnp.concatenate([allowed, allowed], 1)
        for p in range(pairs):
            span = slice(p * TILE, (p + 1) * TILE)
            key_span = slice(width + p * TILE, width + (p + 1) * TILE)
            value_span = slice(2 * width + p * TILE, 2 * width + (p + 1) * TILE)
            keys = jnp.concatenate([qkv_ref[at, key_span] for at in there], 0)
            vals = jnp.concatenate([qkv_ref[at, value_span] for at in there], 0)
            bias = jnp.concatenate([bias_ref[p, k] for k in kind], 0)
            raw = dot(keys, queries[p], 1, 1) + bias
            prob = jnp.exp(jnp.where(allowed, raw - logs[p], MASKED))
            lift = dot(vals, grads[p], 1, 1)
            slope = prob * (lift - deltas[p])
            low = slope.astype(BF16)
            dv = dot(prob.astype(BF16), grads[p], 1, 0)
            dk = dot(low, queries[p], 1, 0)
            for sub in range(2):
                part = slice(sub * TILE, (sub + 1) * TILE)
                sums_ref[p, kind[sub]] += slope[part]
                dv_ref[couple[sub], :, span] += dv[part]
                dk_ref[couple[sub], :, span] += dk[part]
            turned = jnp.concatenate([turned_ref[tile, span, :] for tile in couple], 1)
            dq_ref[p] += dot(turned, low, 1, 0)
        return carry

    lax.fori_loop(0, count_ref[step], visit, 0)
    for p in range(pairs):
        span = slice(p * TILE, (p + 1) * TILE)
        dqkv_ref[here, span] = (own_quadrants(dq_ref[p]).T * scale).astype(BF16)

    @pl.when(step == tiles - 1)
    def _():
        for tile in range(tiles):
            there = tile_rows(place_ref[tile])
            dqkv_ref[there, width : 2 * width] = dk_ref[tile].astype(BF16)
            dqkv_ref[there, 2 * width :] = dv_ref[tile].astype(BF16)
        for p in range(pairs):
            for kind in range(kinds):
                for h in range(2):
                    table_ref[2 * p + h, kind : kind + 1, :] = unskew(
                        sums_ref[p, kind, :, h * TILE : (h + 1) * TILE]
                    )


def attend_back(pieces, qkv, bias, plan, out, lse):
    tiles, pairs, kinds = plan["tiles"], bias.shape[0], bias.shape[1]
    width = pairs * TILE
    rows = tiles * TILE
    return call(
        functools.partial(
            attend_back_body, tiles=tiles, pairs=pairs, scale=plan["scale"], kinds=kinds
        ),
        "attend_back",
        [shaped((rows, 3 * width), BF16), shaped((2 * pairs, kinds, 2 * TILE), F32)],
        grid_spec=pltpu.PrefetchScalarGridSpec(
            num_scalar_prefetch=4,
            grid=(tiles,),
            in_specs=[fixed(*piece.shape) for piece in pieces]
            + [
                fixed(*qkv.shape), fixed(*bias.shape), fixed(tiles, TILE, TILE),
                fixed(tiles, 1, TILE), fixed(*out.shape), fixed(*lse.shape),
            ],
            out_specs=[fixed(rows, 3 * width), fixed(2 * pairs, kinds, 2 * TILE)],
            scratch_shapes=[
                pltpu.VMEM((rows, width), BF16),
                pltpu.VMEM((tiles, width, TILE), BF16),
                pltpu.VMEM((tiles, TILE, width), F32),
                pltpu.VMEM((tiles, TILE, width), F32),
                pltpu.VMEM((pairs, TILE, 2 * TILE), F32),
                pltpu.VMEM((pairs, kinds, TILE, 2 * TILE), F32),
            ],
        ),
    )(
        plan["place"], plan["start"], plan["count"], plan["kind"],
        *pieces, qkv, bias, plan["lab"], plan["labrow"], out, lse,
    )


EDGE = 16


def conv_body(
    order_ref, low_ref, high_ref, *refs, blocks, frames, chunks, lanes, taps,
):
    pieces, refs = refs[:2], refs[2:]
    taps_ref, lab_ref, act_ref, gated_ref, mixed_ref, glu_ref, window_ref, pad_ref, out_pad_ref = refs
    size = glu_ref.shape[0] // blocks
    assemble(glu_ref, pieces)
    channels = lanes * TILE
    half = taps // 2
    span = TILE + 2 * EDGE
    for lane in range(lanes):
        pad_ref[lane, :EDGE, :] = jnp.zeros((EDGE, TILE), F32)
    for block in range(blocks):
        here = pl.ds(pl.multiple_of(order_ref[block] * size, TILE), size)
        for lane in range(lanes):
            value = glu_ref[here, lane * TILE : (lane + 1) * TILE]
            gate = glu_ref[here, channels + lane * TILE : channels + (lane + 1) * TILE]
            first = EDGE + block * frames
            pad_ref[lane, first : first + size, :] = value * sigmoid(gate)
    rest = EDGE + (blocks - 1) * frames + size
    for lane in range(lanes):
        tail = pad_ref.shape[1] - rest
        pad_ref[lane, rest:, :] = jnp.zeros((tail, TILE), F32)

    def chunk(index, carry):
        base = pl.multiple_of(index * TILE, TILE)
        labels = lab_ref[pl.ds(base, span), :]
        center = labels[EDGE : EDGE + TILE]
        for lane in range(lanes):
            values = pad_ref[lane, pl.ds(base, span), :]
            gated_ref[pl.ds(base, TILE), lane * TILE : (lane + 1) * TILE] = values[
                EDGE : EDGE + TILE
            ]

            def segment(label, total):
                window_ref[...] = jnp.where(labels == label, values, 0.0)
                acc = jnp.zeros((TILE, TILE), F32)
                for tap in range(taps):
                    first = EDGE + tap - half
                    acc = acc + window_ref[first : first + TILE, :] * taps_ref[
                        tap : tap + 1, lane * TILE : (lane + 1) * TILE
                    ]
                return jnp.where(center == label, acc, total)

            total = lax.fori_loop(
                low_ref[index], high_ref[index] + 1, segment, jnp.zeros((TILE, TILE), F32)
            )
            mixed_ref[pl.ds(base, TILE), lane * TILE : (lane + 1) * TILE] = total
            out_pad_ref[lane, pl.ds(base, TILE), :] = total * sigmoid(total)
        return carry

    lax.fori_loop(0, chunks, chunk, 0)
    valid = lax.broadcasted_iota(jnp.int32, (size, TILE), 0) < frames
    for block in range(blocks):
        here = pl.ds(pl.multiple_of(order_ref[block] * size, TILE), size)
        for lane in range(lanes):
            rows = out_pad_ref[lane, block * frames : block * frames + size, :]
            act_ref[here, lane * TILE : (lane + 1) * TILE] = jnp.where(valid, rows, 0.0).astype(BF16)


def conv_forward(pieces, taps, plan):
    channels = pieces[0].shape[1] // 2
    blocks, frames, chunks = 4, plan["frames"], plan["chunks"]
    total = plan["tiles"] * TILE
    rows = chunks * TILE
    lanes = channels // TILE
    return call(
        functools.partial(
            conv_body, blocks=blocks, frames=frames, chunks=chunks, lanes=lanes, taps=taps.shape[0]
        ),
        "conv_forward",
        [
            shaped((total, channels), BF16),
            shaped((rows, channels), F32),
            shaped((rows, channels), F32),
            shaped((total, 2 * channels), F32),
        ],
        grid_spec=pltpu.PrefetchScalarGridSpec(
            num_scalar_prefetch=3,
            grid=(1,),
            in_specs=[fixed(*piece.shape) for piece in pieces]
            + [fixed(*taps.shape), fixed(*plan["flat_lab"].shape)],
            out_specs=[
                fixed(total, channels), fixed(rows, channels), fixed(rows, channels),
                fixed(total, 2 * channels),
            ],
            scratch_shapes=[
                pltpu.VMEM((TILE + 2 * EDGE, TILE), F32),
                pltpu.VMEM((lanes, rows + 2 * EDGE, TILE), F32),
                pltpu.VMEM((lanes, rows, TILE), F32),
            ],
        ),
    )(plan["order"], plan["low"], plan["high"], *pieces, taps, plan["flat_lab"])


def conv_back_body(
    order_ref, low_ref, high_ref, *refs, blocks, frames, chunks, lanes, taps,
):
    pieces, refs = refs[:2], refs[2:]
    (
        glu_ref, taps_ref, lab_ref, gated_ref, mixed_ref,
        dglu_ref, dtaps_ref,
        grad_ref, window_ref, source_ref, slope_ref, dgate_ref, sums_ref,
    ) = refs
    size = glu_ref.shape[0] // blocks
    assemble(grad_ref, pieces)
    channels = lanes * TILE
    half = taps // 2
    span = TILE + 2 * EDGE
    rows = chunks * TILE
    for block in range(blocks):
        here = pl.ds(pl.multiple_of(order_ref[block] * size, TILE), size)
        for lane in range(lanes):
            first = EDGE + block * frames
            slope_ref[lane, first : first + size, :] = grad_ref[
                here, lane * TILE : (lane + 1) * TILE
            ]
    rest = EDGE + (blocks - 1) * frames + size
    for lane in range(lanes):
        slope_ref[lane, :EDGE, :] = jnp.zeros((EDGE, TILE), F32)
        slope_ref[lane, rest:, :] = jnp.zeros((slope_ref.shape[1] - rest, TILE), F32)
        mixed = mixed_ref[:, lane * TILE : (lane + 1) * TILE]
        gate = sigmoid(mixed)
        slope_ref[lane, EDGE : EDGE + rows, :] = slope_ref[lane, EDGE : EDGE + rows, :] * (
            gate * (1.0 + mixed * (1.0 - gate))
        )
        source_ref[lane, :EDGE, :] = jnp.zeros((EDGE, TILE), F32)
        source_ref[lane, EDGE : EDGE + rows, :] = gated_ref[:, lane * TILE : (lane + 1) * TILE]
        source_ref[lane, EDGE + rows :, :] = jnp.zeros((EDGE, TILE), F32)
        dgate_ref[lane, rows:, :] = jnp.zeros((dgate_ref.shape[1] - rows, TILE), F32)
    sums_ref[...] = jnp.zeros_like(sums_ref)

    def chunk(index, carry):
        base = pl.multiple_of(index * TILE, TILE)
        labels = lab_ref[pl.ds(base, span), :]
        center = labels[EDGE : EDGE + TILE]
        for lane in range(lanes):
            slopes = slope_ref[lane, pl.ds(base, span), :]
            sources = source_ref[lane, pl.ds(base, span), :]

            def segment(label, total):
                window_ref[0] = jnp.where(labels == label, slopes, 0.0)
                window_ref[1] = jnp.where(labels == label, sources, 0.0)
                inner = window_ref[0, EDGE : EDGE + TILE, :]
                acc = jnp.zeros((TILE, TILE), F32)
                for tap in range(taps):
                    first = EDGE - tap + half
                    acc = acc + window_ref[0, first : first + TILE, :] * taps_ref[
                        tap : tap + 1, lane * TILE : (lane + 1) * TILE
                    ]
                    first = EDGE + tap - half
                    part = fold(inner * window_ref[1, first : first + TILE, :])
                    sums_ref[lane, tap] += jnp.sum(part, axis=0)
                return jnp.where(center == label, acc, total)

            dgate_ref[lane, pl.ds(base, TILE), :] = lax.fori_loop(
                low_ref[index], high_ref[index] + 1, segment, jnp.zeros((TILE, TILE), F32)
            )
        return carry

    lax.fori_loop(0, chunks, chunk, 0)
    for lane in range(lanes):
        dtaps_ref[:, lane * TILE : (lane + 1) * TILE] = jnp.sum(sums_ref[lane], axis=1)
    valid = lax.broadcasted_iota(jnp.int32, (size, TILE), 0) < frames
    for block in range(blocks):
        here = pl.ds(pl.multiple_of(order_ref[block] * size, TILE), size)
        for lane in range(lanes):
            lead = slice(lane * TILE, (lane + 1) * TILE)
            follow = slice(channels + lane * TILE, channels + (lane + 1) * TILE)
            rows_in = dgate_ref[lane, block * frames : block * frames + size, :]
            rows_in = jnp.where(valid, rows_in, 0.0)
            value = glu_ref[here, lead]
            gate = sigmoid(glu_ref[here, follow])
            dglu_ref[here, lead] = (rows_in * gate).astype(BF16)
            dglu_ref[here, follow] = (rows_in * value * gate * (1.0 - gate)).astype(BF16)


def conv_backward(pieces, glu, taps, plan, gated, mixed):
    channels = glu.shape[1] // 2
    blocks, frames, chunks = 4, plan["frames"], plan["chunks"]
    rows = chunks * TILE
    lanes = channels // TILE
    return call(
        functools.partial(
            conv_back_body, blocks=blocks, frames=frames, chunks=chunks,
            lanes=lanes, taps=taps.shape[0],
        ),
        "conv_backward",
        [shaped(glu.shape, BF16), shaped(taps.shape, F32)],
        grid_spec=pltpu.PrefetchScalarGridSpec(
            num_scalar_prefetch=3,
            grid=(1,),
            in_specs=[fixed(*piece.shape) for piece in pieces]
            + [
                fixed(*glu.shape), fixed(*taps.shape), fixed(*plan["flat_lab"].shape),
                fixed(rows, channels), fixed(rows, channels),
            ],
            out_specs=[fixed(*glu.shape), fixed(*taps.shape)],
            scratch_shapes=[
                pltpu.VMEM((glu.shape[0], channels), F32),
                pltpu.VMEM((2, TILE + 2 * EDGE, TILE), F32),
                pltpu.VMEM((lanes, rows + 2 * EDGE, TILE), F32),
                pltpu.VMEM((lanes, rows + 2 * EDGE, TILE), F32),
                pltpu.VMEM((lanes, rows + EDGE, TILE), F32),
                pltpu.VMEM((lanes, taps.shape[0], 8, TILE), F32),
            ],
        ),
    )(
        plan["order"], plan["low"], plan["high"],
        *pieces, glu, taps, plan["flat_lab"], gated, mixed,
    )


def swap(values, bit, axis="tensor"):
    count = lax.axis_size(axis)
    return lax.ppermute(values, axis, [(i, i ^ bit) for i in range(count)])


def gather(mine):
    return [mine, swap(mine, 1), swap(mine, 2)]


def tie(value, other):
    return lax.optimization_barrier((value, other))


def complete(blocks, near):
    blocks[2], near[0] = tie(blocks[2], near[0])
    blocks.append(swap(blocks[2], 1))


def scatter(own, beside, far):
    arriving = []
    for across, diagonal in far:
        outgoing = (across.astype(F32) + swap(diagonal, 1).astype(F32)).astype(BF16)
        arriving.append(swap(outgoing, 2))
    return [own, swap(beside, 1), arriving]


def sum_bits(values, axis):
    bit = 1
    while bit < lax.axis_size(axis):
        values = values + swap(values, bit, axis)
        bit *= 2
    return values


def settle_halving(grad, first_bits):
    count = lax.axis_size("dp")
    bits = count.bit_length() - 1
    here = lax.axis_index("dp")
    values = grad.astype(BF16).reshape((2,) * bits + (grad.shape[0] // count, grad.shape[1]))
    left = list(range(bits - 1, -1, -1))
    order = [b for b in first_bits if b < bits] + [b for b in range(bits) if b not in first_bits]
    for bit in order:
        dim = left.index(bit)
        keep = (here >> bit) & 1
        sent = lax.dynamic_index_in_dim(values, 1 - keep, dim, keepdims=False)
        kept = lax.dynamic_index_in_dim(values, keep, dim, keepdims=False)
        values = kept.astype(F32) + swap(sent, 1 << bit, "dp").astype(F32)
        left.pop(dim)
        if left:
            values = values.astype(BF16)
    return values


def settle(grads):
    return lax.psum_scatter(grads, "dp", scatter_dimension=0, tiled=True).astype(F32)


PIECES = 2


def settle_split(grads):
    return jnp.concatenate([settle_halving(grad, (0, 1, 2)) for grad in grads], 1)


def halves(array):
    return [(array, c, CHUNKS) for c in range(CHUNKS)]


def feed_forward(blocks, w_in, w_out):
    near = list(ff_rows(blocks[0], blocks[1], w_in, w_out))
    complete(blocks, near)
    far = [ff_rows(x1, x2, w_in, w_out) for x1, x2 in zip(halves(blocks[2]), halves(blocks[3]))]
    state = ([near[0]] + [f[0] for f in far], [near[1]] + [f[1] for f in far])
    return scatter(near[2], near[3], [f[2:] for f in far]), state


def feed_back(blocks, state, w_in, w_out):
    hidden, _ = state
    near = list(ff_back_rows(blocks[0], blocks[1], hidden[0], w_out, w_in))
    complete(blocks, near)
    far = [
        ff_back_rows(g1, g2, a, w_out, w_in)
        for g1, g2, a in zip(halves(blocks[2]), halves(blocks[3]), hidden[1:])
    ]
    return scatter(near[1], near[2], [f[1:] for f in far]), [near[0]] + [f[0] for f in far]


def zigzag(blocks):
    far = [item for pair in zip(halves(blocks[2]), halves(blocks[3])) for item in pair]
    return [blocks[0], blocks[1]] + far


def spread(blocks, weight, side, kind):
    near = [project(blocks[0], blocks[1], weight, side, kind)]
    complete(blocks, near)
    return near[0], project(blocks[2], blocks[3], weight, side, kind)


def collect(flat, weight, side):
    count = 4 * CHUNKS
    far = [
        expand((flat, 2 * CHUNKS + c, count), (flat, 3 * CHUNKS + c, count), weight, side)
        for c in range(CHUNKS)
    ]
    own, beside = expand((flat, 0, 4), (flat, 1, 4), weight, side)
    return scatter(own, beside, far)


def delayed(parts, other):
    own, beside, (first, *rest) = parts
    first, other = tie(first, other)
    return [own, beside, [first, *rest]], other


def make_plan(segments, frames, reach, head_width):
    blocks = lax.axis_size("tensor")
    here = lax.axis_index("tensor").astype(jnp.int32)
    size = pad_up(frames, TILE)
    per_block = size // TILE
    tiles = blocks * per_block
    offsets = tile_offsets(blocks, frames, per_block)
    kinds, table = bias_types(offsets, reach)
    flat = segments.reshape(-1).astype(jnp.int32)
    lab = jnp.pad(flat.reshape(blocks, frames), ((0, 0), (0, size - frames)), constant_values=-1)
    lab = lab.reshape(tiles, TILE)
    high = jnp.max(lab, axis=1)
    low = jnp.min(jnp.where(lab < 0, 1 << 20, lab), axis=1)
    seen = (low[:, None] <= high[None, :]) & (low[None, :] <= high[:, None])
    position = jnp.arange(tiles, dtype=jnp.int32)
    first = jnp.min(jnp.where(seen, position[None, :], tiles), axis=1)
    last = jnp.max(jnp.where(seen, position[None, :], -1), axis=1)
    count1 = last - first + 1
    count = (count1 + 1) // 2
    start = jnp.minimum(first, tiles - 2 * count)
    order = jnp.arange(blocks, dtype=jnp.int32) ^ here
    place = (order[:, None] * per_block + jnp.arange(per_block, dtype=jnp.int32)[None, :]).reshape(-1)
    total = blocks * frames
    chunks = pad_up(total, TILE) // TILE
    padded = jnp.pad(flat, (EDGE, chunks * TILE - total + EDGE), constant_values=-1)
    body = padded[EDGE : EDGE + chunks * TILE].reshape(chunks, TILE)
    return dict(
        kinds=kinds,
        kind=jnp.asarray(table.reshape(-1)),
        place=place,
        tiles=tiles,
        start=start,
        count=count,
        lab=jnp.broadcast_to(lab[:, :, None], (tiles, TILE, TILE)),
        labrow=lab[:, None, :],
        scale=float(head_width) ** -0.5,
        frames=frames,
        chunks=chunks,
        order=order,
        low=jnp.min(jnp.where(body < 0, 1 << 20, body), axis=1),
        high=jnp.max(body, axis=1),
        flat_lab=jnp.broadcast_to(padded[:, None], (padded.shape[0], TILE)),
    )


def shards(
    inputs, segments, cotangent, gain_one, first_in, first_out, gain_two, w_query, w_key, w_value,
    w_output, rel_table, gain_three, w_glu, kernel, w_back, gain_four, second_in, second_out,
    gain_five,
):
    frames, _, width = inputs.shape
    size = pad_up(frames, TILE)
    heads = rel_table.shape[0]
    reach = rel_table.shape[1] // 2
    head_width = w_query.shape[1] // heads

    def padded(values):
        return jnp.pad(values.reshape(frames, width), ((0, size - frames), (0, 0)))

    def total(sums):
        return sum(jnp.sum(part, axis=0) for part in sums)

    plan = make_plan(segments, frames, reach, head_width)
    onehot = column_onehot(plan["kinds"], reach)
    bias = bias_tiles(rel_table, onehot, plan["kinds"])
    w_qkv = jnp.concatenate([w_query, w_key, w_value], 1)
    channels = kernel.shape[1]
    glu_matrix = w_glu.reshape(width, 2 * channels)

    start = padded(inputs)
    h_one = gather(enter(start, gain_one))
    parts, state_one = feed_forward(h_one, first_in, first_out)
    h_two, one = join(start, parts, gain_two, 0.5)
    h_two = gather(h_two)
    out, lse, qkv = attend(spread(h_two, w_qkv, 0, BF16), bias, plan)
    h_three, two = join(one, collect(out, w_output, 0), gain_three, 1.0)
    h_three = gather(h_three)
    act, gated, mixed, glu = conv_forward(spread(h_three, glu_matrix, 0, F32), kernel, plan)
    h_four, three = join(two, collect(act, w_back, 0), gain_four, 1.0)
    h_four = gather(h_four)
    parts, state_four = feed_forward(h_four, second_in, second_out)

    grads, output, e4, sums = turn(three, parts, gain_five, padded(cotangent), 0.5, 0.5)
    grad_five = total(sums)
    grads = gather(grads)
    parts, inner = feed_back(grads, state_four, second_in, second_out)
    parts, grad_w = delayed(
        parts, weight_grads([(zigzag(grads), state_four[1]), (zigzag(h_four), inner)])[0]
    )
    settled_four = settle(grad_w)
    grads, e3, sums = join_back(e4, three, parts, gain_four, 1.0)
    grad_four = total(sums)
    grads = gather(grads)
    dglu, grad_kernel = conv_backward(
        spread(grads, w_back, 1, F32), glu, kernel, plan, gated, mixed
    )
    parts, grad_w = delayed(
        collect(dglu, glu_matrix, 1), weight_grads([(grads, [act]), (h_three, [dglu])])[0]
    )
    settled_three = settle(grad_w)
    grads, e2, sums = join_back(e3, two, parts, gain_three, 1.0)
    grad_three = total(sums)
    grads = gather(grads)
    pulled = spread(grads, w_output, 1, BF16)
    dqkv, table_sums = attend_back(pulled, qkv, bias, plan, out, lse)
    dqkv, settled_four = tie(dqkv, settled_four)
    parts, grad_w = delayed(
        collect(dqkv, w_qkv, 1), weight_grads([(grads, [out]), (h_two, [dqkv])])[0]
    )
    settled_two = settle(grad_w)
    grads, e1, sums = join_back(e2, one, parts, gain_two, 0.5)
    grad_two = total(sums)
    grads = gather(grads)
    grads[0], settled_three = tie(grads[0], settled_three)
    parts, inner = feed_back(grads, state_one, first_in, first_out)
    grad_w, = weight_grads([(zigzag(grads), state_one[1])])
    parts, grad_first_in = delayed(parts, weight_grads([(zigzag(h_one), inner)], PIECES))
    parts, grad_w = delayed(parts, grad_w)
    grad_first_out = settle(grad_w)
    small, grad_first_in = tie(
        (table_sums, grad_kernel, grad_two, grad_three, grad_four, grad_five), grad_first_in
    )
    table_sums, grad_kernel, grad_two, grad_three, grad_four, grad_five = small
    grad_first_in = settle_split(grad_first_in)
    e0, sums = join_back(e1, start, parts, gain_one, 0.0)
    grad_one = total(sums)
    grad_table = lax.dot_general(
        table_sums.reshape(heads, -1), onehot, (((1,), (1,)), ((), ())),
        precision=lax.Precision.HIGHEST, preferred_element_type=F32,
    )
    gains = sum_bits(jnp.concatenate([grad_two, grad_three, grad_four, grad_five]), "tensor")
    small = jnp.concatenate([gains, grad_table.reshape(-1), grad_kernel.reshape(-1)])
    small = sum_bits(small, "dp")
    grad_one = sum_bits(sum_bits(grad_one, "tensor"), "dp")
    grad_gains = [grad_one] + [small[i * width : (i + 1) * width] for i in range(4)]
    rest = small[4 * width :]
    grad_table = rest[: grad_table.size].reshape(grad_table.shape)
    grad_kernel = rest[grad_table.size :].reshape(grad_kernel.shape)
    part, own = w_query.shape[1], w_output.shape[0]
    return (
        jnp.concatenate(output, 0)[:frames].reshape(inputs.shape),
        e0[:frames].reshape(inputs.shape),
        grad_gains[0],
        grad_first_in,
        grad_first_out.T,
        grad_gains[1],
        settled_two[:, own : own + part],
        settled_two[:, own + part : own + 2 * part],
        settled_two[:, own + 2 * part :],
        settled_two[:, :own].T,
        grad_table,
        grad_gains[2],
        settled_three[:, channels:].reshape(-1, 2, channels),
        grad_kernel,
        settled_three[:, :channels].T,
        grad_gains[3],
        settled_four[:, second_out.shape[0] :],
        settled_four[:, : second_out.shape[0]].T,
        grad_gains[4],
    )


def solution(mesh):
    in_specs = (
        P("tensor", "dp", None), P("dp", None), P("tensor", "dp", None), P(),
        P(None, "tensor"), P("tensor", None), P(), P(None, "tensor"), P(None, "tensor"),
        P(None, "tensor"), P("tensor", None), P("tensor", None), P(), P(None, None, "tensor"),
        P(None, "tensor"), P("tensor", None), P(), P(None, "tensor"), P("tensor", None), P(),
    )
    out_specs = (
        P("tensor", "dp", None), P("tensor", "dp", None), P(), P("dp", "tensor"),
        P("tensor", "dp"), P(), P("dp", "tensor"), P("dp", "tensor"), P("dp", "tensor"),
        P("tensor", "dp"), P("tensor", None), P(), P("dp", None, "tensor"), P(None, "tensor"),
        P("tensor", "dp"), P(), P("dp", "tensor"), P("tensor", "dp"), P(),
    )
    return jax.shard_map(shards, mesh=mesh, in_specs=in_specs, out_specs=out_specs, check_vma=False)
```

```python
import functools

import jax
import jax.numpy as jnp
import numpy as np
from jax import lax
from jax.experimental import pallas as pl
from jax.experimental.pallas import tpu as pltpu
from jax.sharding import PartitionSpec as P

TILE = 128
MASKED = -1e30
F32 = jnp.float32
BF16 = jnp.bfloat16


def pad_up(size, unit):
    return -(-size // unit) * unit


CHUNKS = 2


def dot(a, b, ca, cb):
    return lax.dot_general(a, b, (((ca,), (cb,)), ((), ())), preferred_element_type=F32)


def sigmoid(values):
    return 0.5 * jnp.tanh(0.5 * values) + 0.5


def fixed(*shape):
    return pl.BlockSpec(shape, lambda *_: (0,) * len(shape))


def shaped(shape, kind):
    return jax.ShapeDtypeStruct(tuple(shape), kind)


BUDGET = dict(
    distance_bias=(3, 12), enter=(1, 8), join=(2, 8), turn=(3, 12), join_back=(3, 12),
    ff_rows=(4, 28), ff_back_rows=(4, 28), project=(2, 20), expand=(2, 16),
    weight_grads=(5, 40), attend=(24, 40), attend_back=(43, 48),
    conv_forward=(11, 40), conv_backward=(17, 48),
)
COST_SCALE = 0.1


def call(body, name, out_shape, cost=1.0, **options):
    time, limit = BUDGET[name]
    time = time * cost * COST_SCALE
    return pl.pallas_call(
        body,
        out_shape=out_shape,
        compiler_params=pltpu.CompilerParams(vmem_limit_bytes=limit * 2**20),
        cost_estimate=pl.CostEstimate(
            flops=int(time * 1e9), bytes_accessed=int(time * 3.5e6), transcendentals=0
        ),
        name=name,
        **options,
    )


def tile_offsets(blocks, block_frames, per_block):
    starts = np.array([b * block_frames + t * TILE for b in range(blocks) for t in range(per_block)])
    return starts[None, :] - starts[:, None]


def bias_types(offsets, reach):
    near = sorted({int(d) for d in offsets.ravel() if abs(int(d)) < reach + TILE - 1})
    far = 4 * TILE + reach
    kinds = near + [-far, far]
    index = {d: i for i, d in enumerate(near)}
    table = np.array(
        [
            [index.get(int(d), len(near) + (1 if d > 0 else 0)) for d in row]
            for row in offsets
        ],
        np.int32,
    )
    return kinds, table


def column_onehot(kinds, reach):
    lane = lax.broadcasted_iota(jnp.int32, (len(kinds), 2 * TILE), 1)
    signed = jnp.where(lane < TILE, lane, lane - 2 * TILE)
    base = jnp.array(kinds, jnp.int32)[:, None]
    column = jnp.clip(base - signed, -reach, reach) + reach
    width = 2 * reach + 1
    flat = column.reshape(-1)
    return (flat[None, :] == jnp.arange(width, dtype=jnp.int32)[:, None]).astype(F32)


def bias_body(row_ref, out_ref, *, pairs, count):
    for p in range(pairs):
        for kind in range(count):
            for head in range(2):
                line = jnp.broadcast_to(row_ref[2 * p + head, kind : kind + 1, :], (TILE, 2 * TILE))
                skewed = pltpu.roll(line, 0, 1, stride=1, stride_axis=0)
                out_ref[p, kind, :, head * TILE : (head + 1) * TILE] = skewed[:, :TILE]


def bias_tiles(rel_table, onehot, kinds):
    heads = rel_table.shape[0]
    pairs = heads // 2
    count = len(kinds)
    rows = jnp.dot(rel_table, onehot, precision=lax.Precision.HIGHEST, preferred_element_type=F32)
    return call(
        functools.partial(bias_body, pairs=pairs, count=count),
        "distance_bias",
        shaped((pairs, count, TILE, 2 * TILE), F32),
    )(rows.reshape(heads, count, 2 * TILE))


SLAB = 16


def unit_rows(rows):
    mean = jnp.mean(rows, axis=-1, keepdims=True)
    centred = rows - mean
    rstd = lax.rsqrt(jnp.mean(centred * centred, axis=-1, keepdims=True) + 1e-05)
    return centred * rstd, rstd


def pull_back(unit, rstd, scaled):
    first = jnp.mean(scaled, axis=-1, keepdims=True)
    second = jnp.mean(scaled * unit, axis=-1, keepdims=True)
    return rstd * (scaled - first - unit * second)


def fold(values):
    return values.reshape(values.shape[0] // 8, 8, values.shape[1])


def slabs(rows, body):
    def step(i, carry):
        body(pl.ds(pl.multiple_of(i * SLAB, SLAB), SLAB))
        return carry

    lax.fori_loop(0, rows // SLAB, step, 0, unroll=2)


def enter(rows, gain):
    def body(r_ref, g_ref, h_ref):
        def slab(at):
            unit, _ = unit_rows(r_ref[at, :].astype(F32))
            h_ref[at, :] = (unit * g_ref[...]).astype(BF16)

        slabs(r_ref.shape[0], slab)

    return call(body, "enter", shaped(rows.shape, BF16))(rows, gain[None, :])


def received(at, refs):
    return refs[0][at, :].astype(F32) + refs[1][at, :].astype(F32) + refs[2][at, :].astype(F32)


def by_chunks(body, name, arrays, gain, kinds, sums=0):
    some = next(x for x in arrays if not isinstance(x, list))
    size, width = some.shape
    cut = int(size // CHUNKS)
    lone = fixed(cut, width)
    filled, lists = None, [[] for _ in kinds[1:]]
    for chunk in range(CHUNKS):
        piece = pl.BlockSpec((cut, width), lambda i, chunk=chunk: (chunk, 0))
        inputs = [x[chunk] if isinstance(x, list) else x for x in arrays]
        specs = [lone if isinstance(x, list) else piece for x in arrays]
        inputs.append(gain[None, :])
        specs.append(fixed(1, width))
        aliases = {}
        run = body
        if filled is not None:
            aliases = {len(inputs): 0}
            inputs.append(filled)
            specs.append(pl.BlockSpec(memory_space=pl.ANY))
            count = len(inputs)
            run = lambda *refs, count=count: body(*refs[: count - 1], *refs[count:])
        shapes = [shaped((size, width), kinds[0])]
        outs = [piece]
        for i, kind in enumerate(kinds[1:]):
            is_sum = i >= len(kinds) - 1 - sums
            shape = (8, width) if is_sum else (cut, width)
            shapes.append(shaped(shape, kind))
            outs.append(fixed(*shape))
        filled, *others = call(
            run, name, shapes, grid=(1,), in_specs=specs, out_specs=outs,
            input_output_aliases=aliases,
        )(*inputs)
        for place, other in zip(lists, others):
            place.append(other)
    return filled, *lists


def join(rows, parts, gain, factor):
    def body(r_ref, p1_ref, p2_ref, p3_ref, g_ref, h_ref, out_ref):
        def slab(at):
            total = r_ref[at, :].astype(F32) + factor * received(at, (p1_ref, p2_ref, p3_ref))
            out_ref[at, :] = total
            unit, _ = unit_rows(total)
            h_ref[at, :] = (unit * g_ref[...]).astype(BF16)

        slabs(r_ref.shape[0], slab)

    return by_chunks(body, "join", [rows, *parts], gain, [BF16, F32])


def turn(rows, parts, gain, cotangent, factor, onward):
    def body(r_ref, p1_ref, p2_ref, p3_ref, c_ref, g_ref, next_ref, out_ref, e_ref, sum_ref):
        sum_ref[...] = jnp.zeros_like(sum_ref)

        def slab(at):
            total = r_ref[at, :].astype(F32) + factor * received(at, (p1_ref, p2_ref, p3_ref))
            unit, rstd = unit_rows(total)
            out_ref[at, :] = (unit * g_ref[...]).astype(BF16)
            grad = c_ref[at, :].astype(F32)
            sum_ref[...] += jnp.sum(fold(grad * unit), axis=0)
            e = pull_back(unit, rstd, grad * g_ref[...])
            e_ref[at, :] = e
            next_ref[at, :] = (onward * e).astype(BF16)

        slabs(r_ref.shape[0], slab)

    return by_chunks(
        body, "turn", [rows, *parts, cotangent], gain, [BF16, BF16, F32, F32], sums=1
    )


def join_back(incoming, rows, parts, gain, onward):
    def body(e_ref, r_ref, p1_ref, p2_ref, p3_ref, g_ref, next_ref, *more):
        out_ref, sum_ref = more if onward else (next_ref, more[0])
        sum_ref[...] = jnp.zeros_like(sum_ref)

        def slab(at):
            unit, rstd = unit_rows(r_ref[at, :].astype(F32))
            grad = received(at, (p1_ref, p2_ref, p3_ref))
            sum_ref[...] += jnp.sum(fold(grad * unit), axis=0)
            e = e_ref[at, :] + pull_back(unit, rstd, grad * g_ref[...])
            out_ref[at, :] = e
            if onward:
                next_ref[at, :] = (onward * e).astype(BF16)

        slabs(r_ref.shape[0], slab)

    kinds = [BF16, F32, F32] if onward else [F32, F32]
    return by_chunks(body, "join_back", [incoming, rows, *parts], gain, kinds, sums=1)


def pieces_of(arrays):
    specs, plain = [], []
    for entry in arrays:
        array, i, n = entry if isinstance(entry, tuple) else (entry, 0, 1)
        shape = (array.shape[0] // n, array.shape[1])
        specs.append(pl.BlockSpec(shape, lambda *_, i=i: (i, 0)))
        plain.append(array)
    return specs, plain


def row_blocks(rows, at, block):
    step = rows // 2 if rows > 256 else rows

    def one(i, carry):
        here = pl.multiple_of(i * step, step)
        block(pl.ds(here, step), pl.ds(here + at, step))
        return carry

    lax.fori_loop(0, rows // step, one, 0)


def ff_rows(x1, x2, w_in, w_out):
    specs, plain = pieces_of([x1, x2])
    rows, width = specs[0].block_shape

    def body(x1_ref, x2_ref, w_in_ref, w_out_ref, a_ref, z_ref, u1_ref, u2_ref):
        for x_ref, u_ref, at in ((x1_ref, u1_ref, 0), (x2_ref, u2_ref, rows)):

            def block(here, there):
                a = dot(x_ref[here, :], w_in_ref[...], 1, 0)
                z = (a * sigmoid(a)).astype(BF16)
                a_ref[there, :] = a.astype(BF16)
                z_ref[there, :] = z
                u_ref[here, :] = dot(z, w_out_ref[...], 1, 0).astype(BF16)

            row_blocks(rows, at, block)

    wide = (2 * rows, w_in.shape[1])
    return call(
        body, "ff_rows", [shaped(wide, BF16)] * 2 + [shaped((rows, width), BF16)] * 2, grid=(1,),
        in_specs=specs + [fixed(*w_in.shape), fixed(*w_out.shape)],
        out_specs=[fixed(*wide)] * 2 + [fixed(rows, width)] * 2,
    )(*plain, w_in, w_out)


def ff_back_rows(g1, g2, a, w_out, w_in):
    specs, plain = pieces_of([g1, g2])
    rows, width = specs[0].block_shape

    def body(g1_ref, g2_ref, a_ref, w_out_ref, w_in_ref, ea_ref, p1_ref, p2_ref):
        for g_ref, p_ref, at in ((g1_ref, p1_ref, 0), (g2_ref, p2_ref, rows)):

            def block(here, there):
                ez = dot(g_ref[here, :], w_out_ref[...], 1, 1)
                a = a_ref[there, :].astype(F32)
                s = sigmoid(a)
                ea = (ez * s * (1.0 + a * (1.0 - s))).astype(BF16)
                ea_ref[there, :] = ea
                p_ref[here, :] = dot(ea, w_in_ref[...], 1, 1).astype(BF16)

            row_blocks(rows, at, block)

    return call(
        body, "ff_back_rows", [shaped(a.shape, BF16)] + [shaped((rows, width), BF16)] * 2,
        grid=(1,),
        in_specs=specs + [fixed(*a.shape), fixed(*w_out.shape), fixed(*w_in.shape)],
        out_specs=[fixed(*a.shape)] + [fixed(rows, width)] * 2,
    )(*plain, a, w_out, w_in)


def project(x1, x2, weight, side, kind):
    def body(x1_ref, x2_ref, w_ref, y_ref):
        rows = x1_ref.shape[0]
        y_ref[:rows, :] = dot(x1_ref[...], w_ref[...], 1, side).astype(kind)
        y_ref[rows:, :] = dot(x2_ref[...], w_ref[...], 1, side).astype(kind)

    shape = (2 * x1.shape[0], weight.shape[1 - side])
    return call(body, "project", shaped(shape, kind))(x1, x2, weight)


def expand(x1, x2, weight, side):
    specs, plain = pieces_of([x1, x2])

    def body(x1_ref, x2_ref, w_ref, y1_ref, y2_ref):
        y1_ref[...] = dot(x1_ref[...], w_ref[...], 1, side).astype(BF16)
        y2_ref[...] = dot(x2_ref[...], w_ref[...], 1, side).astype(BF16)

    shape = (specs[0].block_shape[0], weight.shape[1 - side])
    return call(
        body, "expand", [shaped(shape, BF16)] * 2, grid=(1,),
        in_specs=specs + [fixed(*weight.shape)],
        out_specs=[fixed(*shape)] * 2,
    )(*plain, weight)


def weight_grads(products):
    entries, spans, at, column = [], [], 0, 0
    for left, right in products:
        entries += left + right
        first = right[0][0] if isinstance(right[0], tuple) else right[0]
        spans.append((at, at + len(left), at + len(left) + len(right), column))
        at += len(left) + len(right)
        column += first.shape[1]
    specs, plain = pieces_of(entries)
    height = specs[0].block_shape[1]
    tile = 2 * TILE

    def body(*refs):
        out_ref = refs[-1]

        def band(i, carry):
            here = pl.ds(pl.multiple_of(i * tile, tile), tile)
            for first, middle, last, column in spans:
                left = jnp.concatenate([ref[:, here] for ref in refs[first:middle]], 0)
                right = jnp.concatenate([ref[...] for ref in refs[middle:last]], 0)
                out_ref[here, column : column + right.shape[1]] = dot(left, right, 0, 0).astype(
                    BF16
                )
            return carry

        lax.fori_loop(0, height // tile, band, 0)

    return call(
        body, "weight_grads", shaped((height, column), BF16), grid=(1,),
        in_specs=specs, out_specs=fixed(height, column),
    )(*plain)


def stacked_heads(pair):
    low_half = lax.broadcasted_iota(jnp.int32, pair.shape, 1) < pair.shape[1] // 2
    zero = jnp.zeros_like(pair)
    return jnp.concatenate([jnp.where(low_half, pair, zero), jnp.where(low_half, zero, pair)], 0)


def own_quadrants(wide):
    half = lax.broadcasted_iota(jnp.int32, (TILE, TILE), 0) < TILE // 2
    return jnp.where(half, wide[:, :TILE], wide[:, TILE:])


def assemble(target_ref, piece_refs):
    rows = piece_refs[0].shape[0]
    for i, ref in enumerate(piece_refs):
        target_ref[i * rows : (i + 1) * rows, :] = ref[...]


def tile_rows(index):
    return pl.ds(pl.multiple_of(index * TILE, TILE), TILE)


def attend_body(
    place_ref, start_ref, count_ref, kind_ref, *refs, tiles, pairs, scale,
):
    pieces, refs = refs[:2], refs[2:]
    bias_ref, lab_ref, labrow_ref, out_ref, lse_ref, qkv_ref, score_ref, turned_ref, acc_ref = refs
    step = pl.program_id(0)
    width = pairs * TILE

    @pl.when(step == 0)
    def _():
        assemble(qkv_ref, pieces)
        for tile in range(tiles):
            turned_ref[tile] = qkv_ref[tile_rows(place_ref[tile]), 2 * width :].T

    mine = qkv_ref[tile_rows(place_ref[step]), :]
    queries = [
        stacked_heads(mine[:, p * TILE : (p + 1) * TILE] * scale) for p in range(pairs)
    ]
    own_label = labrow_ref[step]
    begin = start_ref[step]
    trips = count_ref[step]

    def scores(trip, best):
        couple = [begin + 2 * trip + sub for sub in range(2)]
        kinds = [kind_ref[step * tiles + tile] for tile in couple]
        allowed = [lab_ref[tile] == own_label for tile in couple]
        keys = jnp.concatenate(
            [qkv_ref[tile_rows(place_ref[tile]), width : 2 * width] for tile in couple], 0
        )
        parts = []
        for p in range(pairs):
            both = dot(keys[:, p * TILE : (p + 1) * TILE], queries[p], 1, 1)
            highs = []
            for sub in range(2):
                raw = both[sub * TILE : (sub + 1) * TILE] + bias_ref[p, kinds[sub]]
                pair_high = []
                for h in range(2):
                    part = jnp.where(allowed[sub], raw[:, h * TILE : (h + 1) * TILE], MASKED)
                    span = slice((2 * p + h) * TILE, (2 * p + h + 1) * TILE)
                    score_ref[couple[sub], :, span] = part
                    pair_high.append(jnp.max(fold(part), axis=0))
                highs.append(jnp.concatenate(pair_high, 1))
            parts.append(jnp.maximum(*highs))
        return jnp.maximum(best, jnp.concatenate(parts, 1))

    best = lax.fori_loop(0, trips, scores, jnp.full((8, 2 * width), MASKED, F32))
    top = jnp.max(best, axis=0, keepdims=True)
    acc_ref[...] = jnp.zeros_like(acc_ref)

    def mix(trip, total):
        first = begin + 2 * trip
        probs = []
        for sub in range(2):
            value = jnp.exp(score_ref[first + sub] - top)
            total = total + jnp.sum(fold(value), axis=0)
            probs.append(value.astype(BF16))
        both = jnp.concatenate(probs, 0)
        for p in range(pairs):
            turned = jnp.concatenate(
                [turned_ref[first + sub, p * TILE : (p + 1) * TILE, :] for sub in range(2)], 1
            )
            acc_ref[p] += dot(turned, both[:, 2 * p * TILE : 2 * (p + 1) * TILE], 1, 0)
        return total

    total = lax.fori_loop(0, trips, mix, jnp.zeros((8, 2 * width), F32))
    total = jnp.sum(total, axis=0, keepdims=True)
    inverse = 1.0 / total
    log_total = top + jnp.log(total)
    for p in range(pairs):
        wide = acc_ref[p] * inverse[:, 2 * p * TILE : 2 * (p + 1) * TILE]
        out_ref[:, p * TILE : (p + 1) * TILE] = own_quadrants(wide).T.astype(BF16)
    for h in range(2 * pairs):
        lse_ref[0, h : h + 1, :] = log_total[:, h * TILE : (h + 1) * TILE]


def attend(pieces, bias, plan):
    pairs = bias.shape[0]
    width = pairs * TILE
    tiles = plan["tiles"]
    rows = tiles * TILE
    return call(
        functools.partial(attend_body, tiles=tiles, pairs=pairs, scale=plan["scale"]),
        "attend",
        [
            shaped((rows, width), BF16),
            shaped((tiles, 2 * pairs, TILE), F32),
            shaped((rows, 3 * width), BF16),
        ],
        grid_spec=pltpu.PrefetchScalarGridSpec(
            num_scalar_prefetch=4,
            grid=(tiles,),
            in_specs=[fixed(*piece.shape) for piece in pieces]
            + [fixed(*bias.shape), fixed(tiles, TILE, TILE), fixed(tiles, 1, TILE)],
            out_specs=[
                pl.BlockSpec((TILE, width), lambda i, place, *_: (place[i], 0)),
                pl.BlockSpec((1, 2 * pairs, TILE), lambda i, *_: (i, 0, 0)),
                fixed(rows, 3 * width),
            ],
            scratch_shapes=[
                pltpu.VMEM((tiles, TILE, 2 * width), F32),
                pltpu.VMEM((tiles, width, TILE), BF16),
                pltpu.VMEM((pairs, TILE, 2 * TILE), F32),
            ],
        ),
    )(
        plan["place"], plan["start"], plan["count"], plan["kind"],
        *pieces, bias, plan["lab"], plan["labrow"],
    )


def unskew(values):
    wide = jnp.concatenate([values, jnp.zeros_like(values)], 1)
    rows = TILE
    while rows > 8:
        rows //= 2
        wide = wide[:rows] + pltpu.roll(wide[rows:], 2 * TILE - rows, 1)
    row = lax.broadcasted_iota(jnp.int32, wide.shape, 0)
    for bit in (4, 2, 1):
        wide = jnp.where((row & bit) != 0, pltpu.roll(wide, 2 * TILE - bit, 1), wide)
    return jnp.sum(wide, axis=0, keepdims=True)


def attend_back_body(
    place_ref, start_ref, count_ref, kind_ref, *refs, tiles, pairs, scale, kinds,
):
    pieces, refs = refs[:2], refs[2:]
    (
        qkv_ref, bias_ref, lab_ref, labrow_ref, out_ref, lse_ref,
        dqkv_ref, table_ref,
        grad_ref, turned_ref, dk_ref, dv_ref, dq_ref, sums_ref,
    ) = refs
    step = pl.program_id(0)
    width = pairs * TILE

    @pl.when(step == 0)
    def _():
        assemble(grad_ref, pieces)
        for tile in range(tiles):
            turned_ref[tile] = qkv_ref[tile_rows(place_ref[tile]), width : 2 * width].T
        dk_ref[...] = jnp.zeros_like(dk_ref)
        dv_ref[...] = jnp.zeros_like(dv_ref)
        sums_ref[...] = jnp.zeros_like(sums_ref)

    here = tile_rows(place_ref[step])
    queries, grads, deltas, logs = [], [], [], []
    for p in range(pairs):
        span = slice(p * TILE, (p + 1) * TILE)
        queries.append(stacked_heads(qkv_ref[here, span] * scale))
        grad = grad_ref[here, span]
        grads.append(stacked_heads(grad))
        product = (grad.astype(F32) * out_ref[here, span].astype(F32)).T
        half = TILE // 2
        deltas.append(
            jnp.concatenate(
                [
                    jnp.sum(product[:half], axis=0, keepdims=True),
                    jnp.sum(product[half:], axis=0, keepdims=True),
                ],
                1,
            )
        )
        logs.append(jnp.concatenate([lse_ref[step, 2 * p + h : 2 * p + h + 1, :] for h in range(2)], 1))
    own_label = labrow_ref[step]
    begin = start_ref[step]
    dq_ref[...] = jnp.zeros_like(dq_ref)

    def visit(trip, carry):
        couple = [begin + 2 * trip + sub for sub in range(2)]
        kind = [kind_ref[step * tiles + tile] for tile in couple]
        there = [tile_rows(place_ref[tile]) for tile in couple]
        allowed = jnp.concatenate([lab_ref[tile] == own_label for tile in couple], 0)
        allowed = jnp.concatenate([allowed, allowed], 1)
        for p in range(pairs):
            span = slice(p * TILE, (p + 1) * TILE)
            key_span = slice(width + p * TILE, width + (p + 1) * TILE)
            value_span = slice(2 * width + p * TILE, 2 * width + (p + 1) * TILE)
            keys = jnp.concatenate([qkv_ref[at, key_span] for at in there], 0)
            vals = jnp.concatenate([qkv_ref[at, value_span] for at in there], 0)
            bias = jnp.concatenate([bias_ref[p, k] for k in kind], 0)
            raw = dot(keys, queries[p], 1, 1) + bias
            prob = jnp.exp(jnp.where(allowed, raw - logs[p], MASKED))
            lift = dot(vals, grads[p], 1, 1)
            slope = prob * (lift - deltas[p])
            low = slope.astype(BF16)
            dv = dot(prob.astype(BF16), grads[p], 1, 0)
            dk = dot(low, queries[p], 1, 0)
            for sub in range(2):
                part = slice(sub * TILE, (sub + 1) * TILE)
                sums_ref[p, kind[sub]] += slope[part]
                dv_ref[couple[sub], :, span] += dv[part]
                dk_ref[couple[sub], :, span] += dk[part]
            turned = jnp.concatenate([turned_ref[tile, span, :] for tile in couple], 1)
            dq_ref[p] += dot(turned, low, 1, 0)
        return carry

    lax.fori_loop(0, count_ref[step], visit, 0)
    for p in range(pairs):
        span = slice(p * TILE, (p + 1) * TILE)
        dqkv_ref[here, span] = (own_quadrants(dq_ref[p]).T * scale).astype(BF16)

    @pl.when(step == tiles - 1)
    def _():
        for tile in range(tiles):
            there = tile_rows(place_ref[tile])
            dqkv_ref[there, width : 2 * width] = dk_ref[tile].astype(BF16)
            dqkv_ref[there, 2 * width :] = dv_ref[tile].astype(BF16)
        for p in range(pairs):
            for kind in range(kinds):
                for h in range(2):
                    table_ref[2 * p + h, kind : kind + 1, :] = unskew(
                        sums_ref[p, kind, :, h * TILE : (h + 1) * TILE]
                    )


def attend_back(pieces, qkv, bias, plan, out, lse):
    tiles, pairs, kinds = plan["tiles"], bias.shape[0], bias.shape[1]
    width = pairs * TILE
    rows = tiles * TILE
    return call(
        functools.partial(
            attend_back_body, tiles=tiles, pairs=pairs, scale=plan["scale"], kinds=kinds
        ),
        "attend_back",
        [shaped((rows, 3 * width), BF16), shaped((2 * pairs, kinds, 2 * TILE), F32)],
        grid_spec=pltpu.PrefetchScalarGridSpec(
            num_scalar_prefetch=4,
            grid=(tiles,),
            in_specs=[fixed(*piece.shape) for piece in pieces]
            + [
                fixed(*qkv.shape), fixed(*bias.shape), fixed(tiles, TILE, TILE),
                fixed(tiles, 1, TILE), fixed(*out.shape), fixed(*lse.shape),
            ],
            out_specs=[fixed(rows, 3 * width), fixed(2 * pairs, kinds, 2 * TILE)],
            scratch_shapes=[
                pltpu.VMEM((rows, width), BF16),
                pltpu.VMEM((tiles, width, TILE), BF16),
                pltpu.VMEM((tiles, TILE, width), F32),
                pltpu.VMEM((tiles, TILE, width), F32),
                pltpu.VMEM((pairs, TILE, 2 * TILE), F32),
                pltpu.VMEM((pairs, kinds, TILE, 2 * TILE), F32),
            ],
        ),
    )(
        plan["place"], plan["start"], plan["count"], plan["kind"],
        *pieces, qkv, bias, plan["lab"], plan["labrow"], out, lse,
    )


EDGE = 16


def conv_body(
    order_ref, low_ref, high_ref, *refs, blocks, frames, chunks, lanes, taps,
):
    pieces, refs = refs[:2], refs[2:]
    taps_ref, lab_ref, act_ref, gated_ref, mixed_ref, glu_ref, window_ref, pad_ref, out_pad_ref = refs
    size = glu_ref.shape[0] // blocks
    assemble(glu_ref, pieces)
    channels = lanes * TILE
    half = taps // 2
    span = TILE + 2 * EDGE
    for lane in range(lanes):
        pad_ref[lane, :EDGE, :] = jnp.zeros((EDGE, TILE), F32)
    for block in range(blocks):
        here = pl.ds(pl.multiple_of(order_ref[block] * size, TILE), size)
        for lane in range(lanes):
            value = glu_ref[here, lane * TILE : (lane + 1) * TILE]
            gate = glu_ref[here, channels + lane * TILE : channels + (lane + 1) * TILE]
            first = EDGE + block * frames
            pad_ref[lane, first : first + size, :] = value * sigmoid(gate)
    rest = EDGE + (blocks - 1) * frames + size
    for lane in range(lanes):
        tail = pad_ref.shape[1] - rest
        pad_ref[lane, rest:, :] = jnp.zeros((tail, TILE), F32)

    def chunk(index, carry):
        base = pl.multiple_of(index * TILE, TILE)
        labels = lab_ref[pl.ds(base, span), :]
        center = labels[EDGE : EDGE + TILE]
        for lane in range(lanes):
            values = pad_ref[lane, pl.ds(base, span), :]
            gated_ref[pl.ds(base, TILE), lane * TILE : (lane + 1) * TILE] = values[
                EDGE : EDGE + TILE
            ]

            def segment(label, total):
                window_ref[...] = jnp.where(labels == label, values, 0.0)
                acc = jnp.zeros((TILE, TILE), F32)
                for tap in range(taps):
                    first = EDGE + tap - half
                    acc = acc + window_ref[first : first + TILE, :] * taps_ref[
                        tap : tap + 1, lane * TILE : (lane + 1) * TILE
                    ]
                return jnp.where(center == label, acc, total)

            total = lax.fori_loop(
                low_ref[index], high_ref[index] + 1, segment, jnp.zeros((TILE, TILE), F32)
            )
            mixed_ref[pl.ds(base, TILE), lane * TILE : (lane + 1) * TILE] = total
            out_pad_ref[lane, pl.ds(base, TILE), :] = total * sigmoid(total)
        return carry

    lax.fori_loop(0, chunks, chunk, 0)
    valid = lax.broadcasted_iota(jnp.int32, (size, TILE), 0) < frames
    for block in range(blocks):
        here = pl.ds(pl.multiple_of(order_ref[block] * size, TILE), size)
        for lane in range(lanes):
            rows = out_pad_ref[lane, block * frames : block * frames + size, :]
            act_ref[here, lane * TILE : (lane + 1) * TILE] = jnp.where(valid, rows, 0.0).astype(BF16)


def conv_forward(pieces, taps, plan):
    channels = pieces[0].shape[1] // 2
    blocks, frames, chunks = 4, plan["frames"], plan["chunks"]
    total = plan["tiles"] * TILE
    rows = chunks * TILE
    lanes = channels // TILE
    return call(
        functools.partial(
            conv_body, blocks=blocks, frames=frames, chunks=chunks, lanes=lanes, taps=taps.shape[0]
        ),
        "conv_forward",
        [
            shaped((total, channels), BF16),
            shaped((rows, channels), F32),
            shaped((rows, channels), F32),
            shaped((total, 2 * channels), F32),
        ],
        grid_spec=pltpu.PrefetchScalarGridSpec(
            num_scalar_prefetch=3,
            grid=(1,),
            in_specs=[fixed(*piece.shape) for piece in pieces]
            + [fixed(*taps.shape), fixed(*plan["flat_lab"].shape)],
            out_specs=[
                fixed(total, channels), fixed(rows, channels), fixed(rows, channels),
                fixed(total, 2 * channels),
            ],
            scratch_shapes=[
                pltpu.VMEM((TILE + 2 * EDGE, TILE), F32),
                pltpu.VMEM((lanes, rows + 2 * EDGE, TILE), F32),
                pltpu.VMEM((lanes, rows, TILE), F32),
            ],
        ),
    )(plan["order"], plan["low"], plan["high"], *pieces, taps, plan["flat_lab"])


def conv_back_body(
    order_ref, low_ref, high_ref, *refs, blocks, frames, chunks, lanes, taps,
):
    pieces, refs = refs[:2], refs[2:]
    (
        glu_ref, taps_ref, lab_ref, gated_ref, mixed_ref,
        dglu_ref, dtaps_ref,
        grad_ref, window_ref, source_ref, slope_ref, dgate_ref, sums_ref,
    ) = refs
    size = glu_ref.shape[0] // blocks
    assemble(grad_ref, pieces)
    channels = lanes * TILE
    half = taps // 2
    span = TILE + 2 * EDGE
    rows = chunks * TILE
    for block in range(blocks):
        here = pl.ds(pl.multiple_of(order_ref[block] * size, TILE), size)
        for lane in range(lanes):
            first = EDGE + block * frames
            slope_ref[lane, first : first + size, :] = grad_ref[
                here, lane * TILE : (lane + 1) * TILE
            ]
    rest = EDGE + (blocks - 1) * frames + size
    for lane in range(lanes):
        slope_ref[lane, :EDGE, :] = jnp.zeros((EDGE, TILE), F32)
        slope_ref[lane, rest:, :] = jnp.zeros((slope_ref.shape[1] - rest, TILE), F32)
        mixed = mixed_ref[:, lane * TILE : (lane + 1) * TILE]
        gate = sigmoid(mixed)
        slope_ref[lane, EDGE : EDGE + rows, :] = slope_ref[lane, EDGE : EDGE + rows, :] * (
            gate * (1.0 + mixed * (1.0 - gate))
        )
        source_ref[lane, :EDGE, :] = jnp.zeros((EDGE, TILE), F32)
        source_ref[lane, EDGE : EDGE + rows, :] = gated_ref[:, lane * TILE : (lane + 1) * TILE]
        source_ref[lane, EDGE + rows :, :] = jnp.zeros((EDGE, TILE), F32)
        dgate_ref[lane, rows:, :] = jnp.zeros((dgate_ref.shape[1] - rows, TILE), F32)
    sums_ref[...] = jnp.zeros_like(sums_ref)

    def chunk(index, carry):
        base = pl.multiple_of(index * TILE, TILE)
        labels = lab_ref[pl.ds(base, span), :]
        center = labels[EDGE : EDGE + TILE]
        for lane in range(lanes):
            slopes = slope_ref[lane, pl.ds(base, span), :]
            sources = source_ref[lane, pl.ds(base, span), :]

            def segment(label, total):
                window_ref[0] = jnp.where(labels == label, slopes, 0.0)
                window_ref[1] = jnp.where(labels == label, sources, 0.0)
                inner = window_ref[0, EDGE : EDGE + TILE, :]
                acc = jnp.zeros((TILE, TILE), F32)
                for tap in range(taps):
                    first = EDGE - tap + half
                    acc = acc + window_ref[0, first : first + TILE, :] * taps_ref[
                        tap : tap + 1, lane * TILE : (lane + 1) * TILE
                    ]
                    first = EDGE + tap - half
                    part = fold(inner * window_ref[1, first : first + TILE, :])
                    sums_ref[lane, tap] += jnp.sum(part, axis=0)
                return jnp.where(center == label, acc, total)

            dgate_ref[lane, pl.ds(base, TILE), :] = lax.fori_loop(
                low_ref[index], high_ref[index] + 1, segment, jnp.zeros((TILE, TILE), F32)
            )
        return carry

    lax.fori_loop(0, chunks, chunk, 0)
    for lane in range(lanes):
        dtaps_ref[:, lane * TILE : (lane + 1) * TILE] = jnp.sum(sums_ref[lane], axis=1)
    valid = lax.broadcasted_iota(jnp.int32, (size, TILE), 0) < frames
    for block in range(blocks):
        here = pl.ds(pl.multiple_of(order_ref[block] * size, TILE), size)
        for lane in range(lanes):
            lead = slice(lane * TILE, (lane + 1) * TILE)
            follow = slice(channels + lane * TILE, channels + (lane + 1) * TILE)
            rows_in = dgate_ref[lane, block * frames : block * frames + size, :]
            rows_in = jnp.where(valid, rows_in, 0.0)
            value = glu_ref[here, lead]
            gate = sigmoid(glu_ref[here, follow])
            dglu_ref[here, lead] = (rows_in * gate).astype(BF16)
            dglu_ref[here, follow] = (rows_in * value * gate * (1.0 - gate)).astype(BF16)


def conv_backward(pieces, glu, taps, plan, gated, mixed):
    channels = glu.shape[1] // 2
    blocks, frames, chunks = 4, plan["frames"], plan["chunks"]
    rows = chunks * TILE
    lanes = channels // TILE
    return call(
        functools.partial(
            conv_back_body, blocks=blocks, frames=frames, chunks=chunks,
            lanes=lanes, taps=taps.shape[0],
        ),
        "conv_backward",
        [shaped(glu.shape, BF16), shaped(taps.shape, F32)],
        grid_spec=pltpu.PrefetchScalarGridSpec(
            num_scalar_prefetch=3,
            grid=(1,),
            in_specs=[fixed(*piece.shape) for piece in pieces]
            + [
                fixed(*glu.shape), fixed(*taps.shape), fixed(*plan["flat_lab"].shape),
                fixed(rows, channels), fixed(rows, channels),
            ],
            out_specs=[fixed(*glu.shape), fixed(*taps.shape)],
            scratch_shapes=[
                pltpu.VMEM((glu.shape[0], channels), F32),
                pltpu.VMEM((2, TILE + 2 * EDGE, TILE), F32),
                pltpu.VMEM((lanes, rows + 2 * EDGE, TILE), F32),
                pltpu.VMEM((lanes, rows + 2 * EDGE, TILE), F32),
                pltpu.VMEM((lanes, rows + EDGE, TILE), F32),
                pltpu.VMEM((lanes, taps.shape[0], 8, TILE), F32),
            ],
        ),
    )(
        plan["order"], plan["low"], plan["high"],
        *pieces, glu, taps, plan["flat_lab"], gated, mixed,
    )


def swap(values, bit, axis="tensor"):
    count = lax.axis_size(axis)
    return lax.ppermute(values, axis, [(i, i ^ bit) for i in range(count)])


def gather(mine):
    return [mine, swap(mine, 1), swap(mine, 2)]


def tie(value, other):
    return lax.optimization_barrier((value, other))


def complete(blocks, near):
    blocks[2], near[0] = tie(blocks[2], near[0])
    blocks.append(swap(blocks[2], 1))


def scatter(own, beside, far, sent=None):
    arriving = []
    for across, diagonal in far:
        outgoing = (across.astype(F32) + swap(diagonal, 1).astype(F32)).astype(BF16)
        arriving.append(swap(outgoing, 2))
        if sent is not None:
            sent.append(outgoing)
    return [own, swap(beside, 1), arriving]


def sum_bits(values, axis, bit=1):
    while bit < lax.axis_size(axis):
        values = values + swap(values, bit, axis)
        bit *= 2
    return values


def halve_all(grad, gate):
    count = lax.axis_size("dp")
    bits = count.bit_length() - 1
    values = grad.reshape((2,) * bits + (grad.shape[0] // count, grad.shape[1]))
    for bit in range(bits):
        dim = bits - 1 - bit
        keep = (lax.axis_index("dp") >> bit) & 1
        sent = lax.dynamic_index_in_dim(values, 1 - keep, dim, keepdims=False)
        kept = lax.dynamic_index_in_dim(values, keep, dim, keepdims=False)
        arrived = swap(sent, 1 << bit, "dp")
        if bit == 0:
            arrived, _ = tie(arrived, gate)
        values = kept.astype(F32) + arrived.astype(F32)
        if bit < bits - 1:
            values = values.astype(BF16)
    return values


def settle(grads):
    return lax.psum_scatter(grads, "dp", scatter_dimension=0, tiled=True).astype(F32)


def halves(array):
    return [(array, c, CHUNKS) for c in range(CHUNKS)]


def feed_forward(blocks, w_in, w_out):
    near = list(ff_rows(blocks[0], blocks[1], w_in, w_out))
    complete(blocks, near)
    far = [ff_rows(x1, x2, w_in, w_out) for x1, x2 in zip(halves(blocks[2]), halves(blocks[3]))]
    state = ([near[0]] + [f[0] for f in far], [near[1]] + [f[1] for f in far])
    return scatter(near[2], near[3], [f[2:] for f in far]), state


def feed_back(blocks, state, w_in, w_out):
    hidden, _ = state
    near = list(ff_back_rows(blocks[0], blocks[1], hidden[0], w_out, w_in))
    complete(blocks, near)
    far = [
        ff_back_rows(g1, g2, a, w_out, w_in)
        for g1, g2, a in zip(halves(blocks[2]), halves(blocks[3]), hidden[1:])
    ]
    parts = scatter(near[1], near[2], [f[1:] for f in far], outgoing := [])
    return parts, [near[0]] + [f[0] for f in far], outgoing


def zigzag(blocks):
    far = [item for pair in zip(halves(blocks[2]), halves(blocks[3])) for item in pair]
    return [blocks[0], blocks[1]] + far


def spread(blocks, weight, side, kind):
    near = [project(blocks[0], blocks[1], weight, side, kind)]
    complete(blocks, near)
    return near[0], project(blocks[2], blocks[3], weight, side, kind)


def collect(flat, weight, side):
    count = 4 * CHUNKS
    far = [
        expand((flat, 2 * CHUNKS + c, count), (flat, 3 * CHUNKS + c, count), weight, side)
        for c in range(CHUNKS)
    ]
    own, beside = expand((flat, 0, 4), (flat, 1, 4), weight, side)
    return scatter(own, beside, far)


def delayed(parts, other):
    own, beside, (first, *rest) = parts
    first, other = tie(first, other)
    return [own, beside, [first, *rest]], other


def make_plan(segments, frames, reach, head_width):
    blocks = lax.axis_size("tensor")
    here = lax.axis_index("tensor").astype(jnp.int32)
    size = pad_up(frames, TILE)
    per_block = size // TILE
    tiles = blocks * per_block
    offsets = tile_offsets(blocks, frames, per_block)
    kinds, table = bias_types(offsets, reach)
    flat = segments.reshape(-1).astype(jnp.int32)
    lab = jnp.pad(flat.reshape(blocks, frames), ((0, 0), (0, size - frames)), constant_values=-1)
    lab = lab.reshape(tiles, TILE)
    high = jnp.max(lab, axis=1)
    low = jnp.min(jnp.where(lab < 0, 1 << 20, lab), axis=1)
    seen = (low[:, None] <= high[None, :]) & (low[None, :] <= high[:, None])
    position = jnp.arange(tiles, dtype=jnp.int32)
    first = jnp.min(jnp.where(seen, position[None, :], tiles), axis=1)
    last = jnp.max(jnp.where(seen, position[None, :], -1), axis=1)
    count1 = last - first + 1
    count = (count1 + 1) // 2
    start = jnp.minimum(first, tiles - 2 * count)
    order = jnp.arange(blocks, dtype=jnp.int32) ^ here
    place = (order[:, None] * per_block + jnp.arange(per_block, dtype=jnp.int32)[None, :]).reshape(-1)
    total = blocks * frames
    chunks = pad_up(total, TILE) // TILE
    padded = jnp.pad(flat, (EDGE, chunks * TILE - total + EDGE), constant_values=-1)
    body = padded[EDGE : EDGE + chunks * TILE].reshape(chunks, TILE)
    return dict(
        kinds=kinds,
        kind=jnp.asarray(table.reshape(-1)),
        place=place,
        tiles=tiles,
        start=start,
        count=count,
        lab=jnp.broadcast_to(lab[:, :, None], (tiles, TILE, TILE)),
        labrow=lab[:, None, :],
        scale=float(head_width) ** -0.5,
        frames=frames,
        chunks=chunks,
        order=order,
        low=jnp.min(jnp.where(body < 0, 1 << 20, body), axis=1),
        high=jnp.max(body, axis=1),
        flat_lab=jnp.broadcast_to(padded[:, None], (padded.shape[0], TILE)),
    )


def shards(
    inputs, segments, cotangent, gain_one, first_in, first_out, gain_two, w_query, w_key, w_value,
    w_output, rel_table, gain_three, w_glu, kernel, w_back, gain_four, second_in, second_out,
    gain_five,
):
    frames, _, width = inputs.shape
    size = pad_up(frames, TILE)
    heads = rel_table.shape[0]
    reach = rel_table.shape[1] // 2
    head_width = w_query.shape[1] // heads

    def padded(values):
        return jnp.pad(values.reshape(frames, width), ((0, size - frames), (0, 0)))

    def total(sums):
        return sum(jnp.sum(part, axis=0) for part in sums)

    plan = make_plan(segments, frames, reach, head_width)
    onehot = column_onehot(plan["kinds"], reach)
    bias = bias_tiles(rel_table, onehot, plan["kinds"])
    w_qkv = jnp.concatenate([w_query, w_key, w_value], 1)
    channels = kernel.shape[1]
    glu_matrix = w_glu.reshape(width, 2 * channels)

    start = padded(inputs)
    h_one = gather(enter(start, gain_one))
    parts, state_one = feed_forward(h_one, first_in, first_out)
    h_two, one = join(start, parts, gain_two, 0.5)
    h_two = gather(h_two)
    out, lse, qkv = attend(spread(h_two, w_qkv, 0, BF16), bias, plan)
    h_three, two = join(one, collect(out, w_output, 0), gain_three, 1.0)
    h_three = gather(h_three)
    act, gated, mixed, glu = conv_forward(spread(h_three, glu_matrix, 0, F32), kernel, plan)
    h_four, three = join(two, collect(act, w_back, 0), gain_four, 1.0)
    h_four = gather(h_four)
    parts, state_four = feed_forward(h_four, second_in, second_out)

    grads, output, e4, sums = turn(three, parts, gain_five, padded(cotangent), 0.5, 0.5)
    grad_five = total(sums)
    grads = gather(grads)
    parts, inner, _ = feed_back(grads, state_four, second_in, second_out)
    parts, grad_w = delayed(
        parts, weight_grads([(zigzag(grads), state_four[1]), (zigzag(h_four), inner)])
    )
    settled_four = settle(grad_w)
    grads, e3, sums = join_back(e4, three, parts, gain_four, 1.0)
    grad_four = total(sums)
    grads = gather(grads)
    dglu, grad_kernel = conv_backward(
        spread(grads, w_back, 1, F32), glu, kernel, plan, gated, mixed
    )
    parts, grad_w = delayed(
        collect(dglu, glu_matrix, 1), weight_grads([(grads, [act]), (h_three, [dglu])])
    )
    settled_three = settle(grad_w)
    grads, e2, sums = join_back(e3, two, parts, gain_three, 1.0)
    grad_three = total(sums)
    grads = gather(grads)
    pulled = spread(grads, w_output, 1, BF16)
    (first, second), settled_four = tie(pulled, settled_four)
    dqkv, table_sums = attend_back((first, second), qkv, bias, plan, out, lse)
    parts, grad_w = delayed(
        collect(dqkv, w_qkv, 1), weight_grads([(grads, [out]), (h_two, [dqkv])])
    )
    parts, settled_three = delayed(parts, settled_three)
    settled_two = settle(grad_w)
    grads, e1, sums = join_back(e2, one, parts, gain_two, 0.5)
    grad_two = total(sums)
    grads = gather(grads)
    parts, inner, outgoing = feed_back(grads, state_one, first_in, first_out)
    grad_w = weight_grads([(zigzag(grads), state_one[1])])
    grad_first_out = settle(grad_w)
    own, beside, (near_rows, far_rows) = parts
    near_rows, settled_two = tie(near_rows, settled_two)
    parts, grad_first_in = delayed(
        [own, beside, [near_rows, far_rows]], weight_grads([(zigzag(h_one), inner)])
    )
    e0, sums = join_back(e1, start, parts, gain_one, 0.0)
    grad_first_in = halve_all(grad_first_in, sums[-1])
    small, sums = tie(
        (table_sums, grad_kernel, grad_two, grad_three, grad_four, grad_five), sums
    )
    table_sums, grad_kernel, grad_two, grad_three, grad_four, grad_five = small
    grad_one = total(sums)
    grad_table = lax.dot_general(
        table_sums.reshape(heads, -1), onehot, (((1,), (1,)), ((), ())),
        precision=lax.Precision.HIGHEST, preferred_element_type=F32,
    )
    small = jnp.concatenate(
        [grad_one, grad_two, grad_three, grad_four, grad_five]
        + [grad_table.reshape(-1), grad_kernel.reshape(-1)]
    )
    gains = sum_bits(small[: 5 * width], "tensor")
    small = jnp.concatenate([gains, small[5 * width :]])
    small = sum_bits(small, "dp", 2)
    small = small + swap(small, 1, "dp")
    grad_gains = [small[i * width : (i + 1) * width] for i in range(5)]
    rest = small[5 * width :]
    grad_table = rest[: grad_table.size].reshape(grad_table.shape)
    grad_kernel = rest[grad_table.size :].reshape(grad_kernel.shape)
    part, own = w_query.shape[1], w_output.shape[0]
    return (
        jnp.concatenate(output, 0)[:frames].reshape(inputs.shape),
        e0[:frames].reshape(inputs.shape),
        grad_gains[0],
        grad_first_in,
        grad_first_out.T,
        grad_gains[1],
        settled_two[:, own : own + part],
        settled_two[:, own + part : own + 2 * part],
        settled_two[:, own + 2 * part :],
        settled_two[:, :own].T,
        grad_table,
        grad_gains[2],
        settled_three[:, channels:].reshape(-1, 2, channels),
        grad_kernel,
        settled_three[:, :channels].T,
        grad_gains[3],
        settled_four[:, second_out.shape[0] :],
        settled_four[:, : second_out.shape[0]].T,
        grad_gains[4],
    )


def solution(mesh):
    in_specs = (
        P("tensor", "dp", None), P("dp", None), P("tensor", "dp", None), P(),
        P(None, "tensor"), P("tensor", None), P(), P(None, "tensor"), P(None, "tensor"),
        P(None, "tensor"), P("tensor", None), P("tensor", None), P(), P(None, None, "tensor"),
        P(None, "tensor"), P("tensor", None), P(), P(None, "tensor"), P("tensor", None), P(),
    )
    out_specs = (
        P("tensor", "dp", None), P("tensor", "dp", None), P(), P("dp", "tensor"),
        P("tensor", "dp"), P(), P("dp", "tensor"), P("dp", "tensor"), P("dp", "tensor"),
        P("tensor", "dp"), P("tensor", None), P(), P("dp", None, "tensor"), P(None, "tensor"),
        P("tensor", "dp"), P(), P("dp", "tensor"), P("tensor", "dp"), P(),
    )
    return jax.shard_map(shards, mesh=mesh, in_specs=in_specs, out_specs=out_specs, check_vma=False)
```

```python
import functools

import jax
import jax.numpy as jnp
import numpy as np
from jax import lax
from jax.experimental import pallas as pl
from jax.experimental.pallas import tpu as pltpu
from jax.sharding import PartitionSpec as P

TILE = 128
MASKED = -1e30
F32 = jnp.float32
BF16 = jnp.bfloat16


def pad_up(size, unit):
    return -(-size // unit) * unit


CHUNKS = 2


def dot(a, b, ca, cb):
    return lax.dot_general(a, b, (((ca,), (cb,)), ((), ())), preferred_element_type=F32)


def sigmoid(values):
    return 0.5 * jnp.tanh(0.5 * values) + 0.5


def fixed(*shape):
    return pl.BlockSpec(shape, lambda *_: (0,) * len(shape))


def shaped(shape, kind):
    return jax.ShapeDtypeStruct(tuple(shape), kind)


BUDGET = dict(
    distance_bias=(3, 12), enter=(1, 4), join=(2, 4), turn=(3, 6), join_back=(3, 5),
    ff_rows=(4, 14), ff_back_rows=(4, 14), project=(2, 10), expand=(2, 8),
    weight_grads=(5, 20), attend=(24, 24), attend_back=(43, 30),
    conv_forward=(11, 20), conv_backward=(9, 28), taps_backward=(8, 12),
)
COST_SCALE = 0.1


def call(body, name, out_shape, cost=1.0, **options):
    time, limit = BUDGET[name]
    time = time * cost * COST_SCALE
    return pl.pallas_call(
        body,
        out_shape=out_shape,
        compiler_params=pltpu.CompilerParams(vmem_limit_bytes=limit * 2**20),
        cost_estimate=pl.CostEstimate(
            flops=int(time * 1e9), bytes_accessed=int(time * 3.5e6), transcendentals=0
        ),
        name=name,
        **options,
    )


def tile_offsets(blocks, block_frames, per_block):
    starts = np.array([b * block_frames + t * TILE for b in range(blocks) for t in range(per_block)])
    return starts[None, :] - starts[:, None]


def bias_types(offsets, reach):
    near = sorted({int(d) for d in offsets.ravel() if abs(int(d)) < reach + TILE - 1})
    far = 4 * TILE + reach
    kinds = near + [-far, far]
    index = {d: i for i, d in enumerate(near)}
    table = np.array(
        [
            [index.get(int(d), len(near) + (1 if d > 0 else 0)) for d in row]
            for row in offsets
        ],
        np.int32,
    )
    return kinds, table


def column_onehot(kinds, reach):
    lane = lax.broadcasted_iota(jnp.int32, (len(kinds), 2 * TILE), 1)
    signed = jnp.where(lane < TILE, lane, lane - 2 * TILE)
    base = jnp.array(kinds, jnp.int32)[:, None]
    column = jnp.clip(base - signed, -reach, reach) + reach
    width = 2 * reach + 1
    flat = column.reshape(-1)
    return (flat[None, :] == jnp.arange(width, dtype=jnp.int32)[:, None]).astype(F32)


def bias_body(row_ref, out_ref, *, pairs, count):
    for p in range(pairs):
        for kind in range(count):
            for head in range(2):
                line = jnp.broadcast_to(row_ref[2 * p + head, kind : kind + 1, :], (TILE, 2 * TILE))
                skewed = pltpu.roll(line, 0, 1, stride=1, stride_axis=0)
                out_ref[p, kind, :, head * TILE : (head + 1) * TILE] = skewed[:, :TILE]


def bias_tiles(rel_table, onehot, kinds):
    heads = rel_table.shape[0]
    pairs = heads // 2
    count = len(kinds)
    rows = jnp.dot(rel_table, onehot, precision=lax.Precision.HIGHEST, preferred_element_type=F32)
    return call(
        functools.partial(bias_body, pairs=pairs, count=count),
        "distance_bias",
        shaped((pairs, count, TILE, 2 * TILE), F32),
    )(rows.reshape(heads, count, 2 * TILE))


SLAB = 16


def unit_rows(rows):
    mean = jnp.mean(rows, axis=-1, keepdims=True)
    centred = rows - mean
    rstd = lax.rsqrt(jnp.mean(centred * centred, axis=-1, keepdims=True) + 1e-05)
    return centred * rstd, rstd


def pull_back(unit, rstd, scaled):
    first = jnp.mean(scaled, axis=-1, keepdims=True)
    second = jnp.mean(scaled * unit, axis=-1, keepdims=True)
    return rstd * (scaled - first - unit * second)


def fold(values):
    return values.reshape(values.shape[0] // 8, 8, values.shape[1])


def slabs(rows, body):
    def step(i, carry):
        body(pl.ds(pl.multiple_of(i * SLAB, SLAB), SLAB))
        return carry

    lax.fori_loop(0, rows // SLAB, step, 0, unroll=2)


def enter(rows, gain):
    def body(r_ref, g_ref, h_ref):
        def slab(at):
            unit, _ = unit_rows(r_ref[at, :].astype(F32))
            h_ref[at, :] = (unit * g_ref[...]).astype(BF16)

        slabs(r_ref.shape[0], slab)

    return call(body, "enter", shaped(rows.shape, BF16))(rows, gain[None, :])


def received(at, refs):
    return refs[0][at, :].astype(F32) + refs[1][at, :].astype(F32) + refs[2][at, :].astype(F32)


def by_chunks(body, name, arrays, gain, kinds, sums=0):
    some = next(x for x in arrays if not isinstance(x, list))
    size, width = some.shape
    cut = int(size // CHUNKS)
    lone = fixed(cut, width)
    filled, lists = None, [[] for _ in kinds[1:]]
    for chunk in range(CHUNKS):
        piece = pl.BlockSpec((cut, width), lambda i, chunk=chunk: (chunk, 0))
        inputs = [x[chunk] if isinstance(x, list) else x for x in arrays]
        specs = [lone if isinstance(x, list) else piece for x in arrays]
        inputs.append(gain[None, :])
        specs.append(fixed(1, width))
        aliases = {}
        run = body
        if filled is not None:
            aliases = {len(inputs): 0}
            inputs.append(filled)
            specs.append(pl.BlockSpec(memory_space=pl.ANY))
            count = len(inputs)
            run = lambda *refs, count=count: body(*refs[: count - 1], *refs[count:])
        shapes = [shaped((size, width), kinds[0])]
        outs = [piece]
        for i, kind in enumerate(kinds[1:]):
            is_sum = i >= len(kinds) - 1 - sums
            shape = (8, width) if is_sum else (cut, width)
            shapes.append(shaped(shape, kind))
            outs.append(fixed(*shape))
        filled, *others = call(
            run, name, shapes, grid=(1,), in_specs=specs, out_specs=outs,
            input_output_aliases=aliases,
        )(*inputs)
        for place, other in zip(lists, others):
            place.append(other)
    return filled, *lists


def join(rows, parts, gain, factor):
    def body(r_ref, p1_ref, p2_ref, p3_ref, g_ref, h_ref, out_ref):
        def slab(at):
            total = r_ref[at, :].astype(F32) + factor * received(at, (p1_ref, p2_ref, p3_ref))
            out_ref[at, :] = total
            unit, _ = unit_rows(total)
            h_ref[at, :] = (unit * g_ref[...]).astype(BF16)

        slabs(r_ref.shape[0], slab)

    return by_chunks(body, "join", [rows, *parts], gain, [BF16, F32])


def turn(rows, parts, gain, cotangent, factor, onward):
    def body(r_ref, p1_ref, p2_ref, p3_ref, c_ref, g_ref, next_ref, out_ref, e_ref, sum_ref):
        sum_ref[...] = jnp.zeros_like(sum_ref)

        def slab(at):
            total = r_ref[at, :].astype(F32) + factor * received(at, (p1_ref, p2_ref, p3_ref))
            unit, rstd = unit_rows(total)
            out_ref[at, :] = (unit * g_ref[...]).astype(BF16)
            grad = c_ref[at, :].astype(F32)
            sum_ref[...] += jnp.sum(fold(grad * unit), axis=0)
            e = pull_back(unit, rstd, grad * g_ref[...])
            e_ref[at, :] = e
            next_ref[at, :] = (onward * e).astype(BF16)

        slabs(r_ref.shape[0], slab)

    return by_chunks(
        body, "turn", [rows, *parts, cotangent], gain, [BF16, BF16, F32, F32], sums=1
    )


def join_back(incoming, rows, parts, gain, onward):
    def body(e_ref, r_ref, p1_ref, p2_ref, p3_ref, g_ref, next_ref, *more):
        out_ref, sum_ref = more if onward else (next_ref, more[0])
        sum_ref[...] = jnp.zeros_like(sum_ref)

        def slab(at):
            unit, rstd = unit_rows(r_ref[at, :].astype(F32))
            grad = received(at, (p1_ref, p2_ref, p3_ref))
            sum_ref[...] += jnp.sum(fold(grad * unit), axis=0)
            e = e_ref[at, :] + pull_back(unit, rstd, grad * g_ref[...])
            out_ref[at, :] = e
            if onward:
                next_ref[at, :] = (onward * e).astype(BF16)

        slabs(r_ref.shape[0], slab)

    kinds = [BF16, F32, F32] if onward else [F32, F32]
    return by_chunks(body, "join_back", [incoming, rows, *parts], gain, kinds, sums=1)


def pieces_of(arrays):
    specs, plain = [], []
    for entry in arrays:
        array, i, n = entry if isinstance(entry, tuple) else (entry, 0, 1)
        shape = (array.shape[0] // n, array.shape[1])
        specs.append(pl.BlockSpec(shape, lambda *_, i=i: (i, 0)))
        plain.append(array)
    return specs, plain


def row_blocks(rows, at, block):
    step = rows // 2 if rows > 256 else rows

    def one(i, carry):
        here = pl.multiple_of(i * step, step)
        block(pl.ds(here, step), pl.ds(here + at, step))
        return carry

    lax.fori_loop(0, rows // step, one, 0)


def ff_rows(x1, x2, w_in, w_out):
    specs, plain = pieces_of([x1, x2])
    rows, width = specs[0].block_shape

    def body(x1_ref, x2_ref, w_in_ref, w_out_ref, a_ref, z_ref, u1_ref, u2_ref):
        for x_ref, u_ref, at in ((x1_ref, u1_ref, 0), (x2_ref, u2_ref, rows)):

            def block(here, there):
                a = dot(x_ref[here, :], w_in_ref[...], 1, 0)
                z = (a * sigmoid(a)).astype(BF16)
                a_ref[there, :] = a.astype(BF16)
                z_ref[there, :] = z
                u_ref[here, :] = dot(z, w_out_ref[...], 1, 0).astype(BF16)

            row_blocks(rows, at, block)

    wide = (2 * rows, w_in.shape[1])
    return call(
        body, "ff_rows", [shaped(wide, BF16)] * 2 + [shaped((rows, width), BF16)] * 2, grid=(1,),
        in_specs=specs + [fixed(*w_in.shape), fixed(*w_out.shape)],
        out_specs=[fixed(*wide)] * 2 + [fixed(rows, width)] * 2,
    )(*plain, w_in, w_out)


def ff_back_rows(g1, g2, a, w_out, w_in):
    specs, plain = pieces_of([g1, g2])
    rows, width = specs[0].block_shape

    def body(g1_ref, g2_ref, a_ref, w_out_ref, w_in_ref, ea_ref, p1_ref, p2_ref):
        for g_ref, p_ref, at in ((g1_ref, p1_ref, 0), (g2_ref, p2_ref, rows)):

            def block(here, there):
                ez = dot(g_ref[here, :], w_out_ref[...], 1, 1)
                a = a_ref[there, :].astype(F32)
                s = sigmoid(a)
                ea = (ez * s * (1.0 + a * (1.0 - s))).astype(BF16)
                ea_ref[there, :] = ea
                p_ref[here, :] = dot(ea, w_in_ref[...], 1, 1).astype(BF16)

            row_blocks(rows, at, block)

    return call(
        body, "ff_back_rows", [shaped(a.shape, BF16)] + [shaped((rows, width), BF16)] * 2,
        grid=(1,),
        in_specs=specs + [fixed(*a.shape), fixed(*w_out.shape), fixed(*w_in.shape)],
        out_specs=[fixed(*a.shape)] + [fixed(rows, width)] * 2,
    )(*plain, a, w_out, w_in)


def project(x1, x2, weight, side, kind):
    def body(x1_ref, x2_ref, w_ref, y_ref):
        rows = x1_ref.shape[0]
        y_ref[:rows, :] = dot(x1_ref[...], w_ref[...], 1, side).astype(kind)
        y_ref[rows:, :] = dot(x2_ref[...], w_ref[...], 1, side).astype(kind)

    shape = (2 * x1.shape[0], weight.shape[1 - side])
    return call(body, "project", shaped(shape, kind))(x1, x2, weight)


def expand(x1, x2, weight, side):
    specs, plain = pieces_of([x1, x2])

    def body(x1_ref, x2_ref, w_ref, y1_ref, y2_ref):
        y1_ref[...] = dot(x1_ref[...], w_ref[...], 1, side).astype(BF16)
        y2_ref[...] = dot(x2_ref[...], w_ref[...], 1, side).astype(BF16)

    shape = (specs[0].block_shape[0], weight.shape[1 - side])
    return call(
        body, "expand", [shaped(shape, BF16)] * 2, grid=(1,),
        in_specs=specs + [fixed(*weight.shape)],
        out_specs=[fixed(*shape)] * 2,
    )(*plain, weight)


def weight_grads(products):
    entries, spans, at, column = [], [], 0, 0
    for left, right in products:
        entries += left + right
        first = right[0][0] if isinstance(right[0], tuple) else right[0]
        spans.append((at, at + len(left), at + len(left) + len(right), column))
        at += len(left) + len(right)
        column += first.shape[1]
    specs, plain = pieces_of(entries)
    height = specs[0].block_shape[1]
    tile = 2 * TILE

    def body(*refs):
        out_ref = refs[-1]

        def band(i, carry):
            here = pl.ds(pl.multiple_of(i * tile, tile), tile)
            for first, middle, last, column in spans:
                left = jnp.concatenate([ref[:, here] for ref in refs[first:middle]], 0)
                right = jnp.concatenate([ref[...] for ref in refs[middle:last]], 0)
                out_ref[here, column : column + right.shape[1]] = dot(left, right, 0, 0).astype(
                    BF16
                )
            return carry

        lax.fori_loop(0, height // tile, band, 0)

    return call(
        body, "weight_grads", shaped((height, column), BF16), grid=(1,),
        in_specs=specs, out_specs=fixed(height, column),
    )(*plain)


def stacked_heads(pair):
    low_half = lax.broadcasted_iota(jnp.int32, pair.shape, 1) < pair.shape[1] // 2
    zero = jnp.zeros_like(pair)
    return jnp.concatenate([jnp.where(low_half, pair, zero), jnp.where(low_half, zero, pair)], 0)


def own_quadrants(wide):
    half = lax.broadcasted_iota(jnp.int32, (TILE, TILE), 0) < TILE // 2
    return jnp.where(half, wide[:, :TILE], wide[:, TILE:])


def assemble(target_ref, piece_refs):
    rows = piece_refs[0].shape[0]
    for i, ref in enumerate(piece_refs):
        target_ref[i * rows : (i + 1) * rows, :] = ref[...]


def tile_rows(index):
    return pl.ds(pl.multiple_of(index * TILE, TILE), TILE)


def attend_body(
    place_ref, start_ref, count_ref, kind_ref, *refs, tiles, pairs, scale,
):
    pieces, refs = refs[:2], refs[2:]
    bias_ref, lab_ref, labrow_ref, out_ref, lse_ref, qkv_ref, score_ref, turned_ref, acc_ref = refs
    step = pl.program_id(0)
    width = pairs * TILE

    @pl.when(step == 0)
    def _():
        assemble(qkv_ref, pieces)
        for tile in range(tiles):
            turned_ref[tile] = qkv_ref[tile_rows(place_ref[tile]), 2 * width :].T

    mine = qkv_ref[tile_rows(place_ref[step]), :]
    queries = [
        stacked_heads(mine[:, p * TILE : (p + 1) * TILE] * scale) for p in range(pairs)
    ]
    own_label = labrow_ref[step]
    begin = start_ref[step]
    trips = count_ref[step]

    def scores(trip, best):
        couple = [begin + 2 * trip + sub for sub in range(2)]
        kinds = [kind_ref[step * tiles + tile] for tile in couple]
        allowed = [lab_ref[tile] == own_label for tile in couple]
        keys = jnp.concatenate(
            [qkv_ref[tile_rows(place_ref[tile]), width : 2 * width] for tile in couple], 0
        )
        parts = []
        for p in range(pairs):
            both = dot(keys[:, p * TILE : (p + 1) * TILE], queries[p], 1, 1)
            highs = []
            for sub in range(2):
                raw = both[sub * TILE : (sub + 1) * TILE] + bias_ref[p, kinds[sub]]
                pair_high = []
                for h in range(2):
                    part = jnp.where(allowed[sub], raw[:, h * TILE : (h + 1) * TILE], MASKED)
                    span = slice((2 * p + h) * TILE, (2 * p + h + 1) * TILE)
                    score_ref[couple[sub], :, span] = part
                    pair_high.append(jnp.max(fold(part), axis=0))
                highs.append(jnp.concatenate(pair_high, 1))
            parts.append(jnp.maximum(*highs))
        return jnp.maximum(best, jnp.concatenate(parts, 1))

    best = lax.fori_loop(0, trips, scores, jnp.full((8, 2 * width), MASKED, F32))
    top = jnp.max(best, axis=0, keepdims=True)
    acc_ref[...] = jnp.zeros_like(acc_ref)

    def mix(trip, total):
        first = begin + 2 * trip
        probs = []
        for sub in range(2):
            value = jnp.exp(score_ref[first + sub] - top)
            total = total + jnp.sum(fold(value), axis=0)
            probs.append(value.astype(BF16))
        both = jnp.concatenate(probs, 0)
        for p in range(pairs):
            turned = jnp.concatenate(
                [turned_ref[first + sub, p * TILE : (p + 1) * TILE, :] for sub in range(2)], 1
            )
            acc_ref[p] += dot(turned, both[:, 2 * p * TILE : 2 * (p + 1) * TILE], 1, 0)
        return total

    total = lax.fori_loop(0, trips, mix, jnp.zeros((8, 2 * width), F32))
    total = jnp.sum(total, axis=0, keepdims=True)
    inverse = 1.0 / total
    log_total = top + jnp.log(total)
    for p in range(pairs):
        wide = acc_ref[p] * inverse[:, 2 * p * TILE : 2 * (p + 1) * TILE]
        out_ref[:, p * TILE : (p + 1) * TILE] = own_quadrants(wide).T.astype(BF16)
    for h in range(2 * pairs):
        lse_ref[0, h : h + 1, :] = log_total[:, h * TILE : (h + 1) * TILE]


def attend(pieces, bias, plan):
    pairs = bias.shape[0]
    width = pairs * TILE
    tiles = plan["tiles"]
    rows = tiles * TILE
    return call(
        functools.partial(attend_body, tiles=tiles, pairs=pairs, scale=plan["scale"]),
        "attend",
        [
            shaped((rows, width), BF16),
            shaped((tiles, 2 * pairs, TILE), F32),
            shaped((rows, 3 * width), BF16),
        ],
        grid_spec=pltpu.PrefetchScalarGridSpec(
            num_scalar_prefetch=4,
            grid=(tiles,),
            in_specs=[fixed(*piece.shape) for piece in pieces]
            + [fixed(*bias.shape), fixed(tiles, TILE, TILE), fixed(tiles, 1, TILE)],
            out_specs=[
                pl.BlockSpec((TILE, width), lambda i, place, *_: (place[i], 0)),
                pl.BlockSpec((1, 2 * pairs, TILE), lambda i, *_: (i, 0, 0)),
                fixed(rows, 3 * width),
            ],
            scratch_shapes=[
                pltpu.VMEM((tiles, TILE, 2 * width), F32),
                pltpu.VMEM((tiles, width, TILE), BF16),
                pltpu.VMEM((pairs, TILE, 2 * TILE), F32),
            ],
        ),
    )(
        plan["place"], plan["start"], plan["count"], plan["kind"],
        *pieces, bias, plan["lab"], plan["labrow"],
    )


def unskew(values):
    wide = jnp.concatenate([values, jnp.zeros_like(values)], 1)
    rows = TILE
    while rows > 8:
        rows //= 2
        wide = wide[:rows] + pltpu.roll(wide[rows:], 2 * TILE - rows, 1)
    row = lax.broadcasted_iota(jnp.int32, wide.shape, 0)
    for bit in (4, 2, 1):
        wide = jnp.where((row & bit) != 0, pltpu.roll(wide, 2 * TILE - bit, 1), wide)
    return jnp.sum(wide, axis=0, keepdims=True)


def attend_back_body(
    place_ref, start_ref, count_ref, kind_ref, *refs, tiles, pairs, scale, kinds,
):
    pieces, refs = refs[:2], refs[2:]
    (
        qkv_ref, bias_ref, lab_ref, labrow_ref, out_ref, lse_ref,
        dqkv_ref, table_ref,
        grad_ref, turned_ref, dk_ref, dv_ref, dq_ref, sums_ref,
    ) = refs
    step = pl.program_id(0)
    width = pairs * TILE

    @pl.when(step == 0)
    def _():
        assemble(grad_ref, pieces)
        for tile in range(tiles):
            turned_ref[tile] = qkv_ref[tile_rows(place_ref[tile]), width : 2 * width].T
        dk_ref[...] = jnp.zeros_like(dk_ref)
        dv_ref[...] = jnp.zeros_like(dv_ref)
        sums_ref[...] = jnp.zeros_like(sums_ref)

    here = tile_rows(place_ref[step])
    queries, grads, deltas, logs = [], [], [], []
    for p in range(pairs):
        span = slice(p * TILE, (p + 1) * TILE)
        queries.append(stacked_heads(qkv_ref[here, span] * scale))
        grad = grad_ref[here, span]
        grads.append(stacked_heads(grad))
        product = (grad.astype(F32) * out_ref[here, span].astype(F32)).T
        half = TILE // 2
        deltas.append(
            jnp.concatenate(
                [
                    jnp.sum(product[:half], axis=0, keepdims=True),
                    jnp.sum(product[half:], axis=0, keepdims=True),
                ],
                1,
            )
        )
        logs.append(jnp.concatenate([lse_ref[step, 2 * p + h : 2 * p + h + 1, :] for h in range(2)], 1))
    own_label = labrow_ref[step]
    begin = start_ref[step]
    dq_ref[...] = jnp.zeros_like(dq_ref)

    def visit(trip, carry):
        couple = [begin + 2 * trip + sub for sub in range(2)]
        kind = [kind_ref[step * tiles + tile] for tile in couple]
        there = [tile_rows(place_ref[tile]) for tile in couple]
        allowed = jnp.concatenate([lab_ref[tile] == own_label for tile in couple], 0)
        allowed = jnp.concatenate([allowed, allowed], 1)
        for p in range(pairs):
            span = slice(p * TILE, (p + 1) * TILE)
            key_span = slice(width + p * TILE, width + (p + 1) * TILE)
            value_span = slice(2 * width + p * TILE, 2 * width + (p + 1) * TILE)
            keys = jnp.concatenate([qkv_ref[at, key_span] for at in there], 0)
            vals = jnp.concatenate([qkv_ref[at, value_span] for at in there], 0)
            bias = jnp.concatenate([bias_ref[p, k] for k in kind], 0)
            raw = dot(keys, queries[p], 1, 1) + bias
            prob = jnp.exp(jnp.where(allowed, raw - logs[p], MASKED))
            lift = dot(vals, grads[p], 1, 1)
            slope = prob * (lift - deltas[p])
            low = slope.astype(BF16)
            dv = dot(prob.astype(BF16), grads[p], 1, 0)
            dk = dot(low, queries[p], 1, 0)
            for sub in range(2):
                part = slice(sub * TILE, (sub + 1) * TILE)
                sums_ref[p, kind[sub]] += slope[part]
                dv_ref[couple[sub], :, span] += dv[part]
                dk_ref[couple[sub], :, span] += dk[part]
            turned = jnp.concatenate([turned_ref[tile, span, :] for tile in couple], 1)
            dq_ref[p] += dot(turned, low, 1, 0)
        return carry

    lax.fori_loop(0, count_ref[step], visit, 0)
    for p in range(pairs):
        span = slice(p * TILE, (p + 1) * TILE)
        dqkv_ref[here, span] = (own_quadrants(dq_ref[p]).T * scale).astype(BF16)

    @pl.when(step == tiles - 1)
    def _():
        for tile in range(tiles):
            there = tile_rows(place_ref[tile])
            dqkv_ref[there, width : 2 * width] = dk_ref[tile].astype(BF16)
            dqkv_ref[there, 2 * width :] = dv_ref[tile].astype(BF16)
        for p in range(pairs):
            for kind in range(kinds):
                for h in range(2):
                    table_ref[2 * p + h, kind : kind + 1, :] = unskew(
                        sums_ref[p, kind, :, h * TILE : (h + 1) * TILE]
                    )


def attend_back(pieces, qkv, bias, plan, out, lse):
    tiles, pairs, kinds = plan["tiles"], bias.shape[0], bias.shape[1]
    width = pairs * TILE
    rows = tiles * TILE
    return call(
        functools.partial(
            attend_back_body, tiles=tiles, pairs=pairs, scale=plan["scale"], kinds=kinds
        ),
        "attend_back",
        [shaped((rows, 3 * width), BF16), shaped((2 * pairs, kinds, 2 * TILE), F32)],
        grid_spec=pltpu.PrefetchScalarGridSpec(
            num_scalar_prefetch=4,
            grid=(tiles,),
            in_specs=[fixed(*piece.shape) for piece in pieces]
            + [
                fixed(*qkv.shape), fixed(*bias.shape), fixed(tiles, TILE, TILE),
                fixed(tiles, 1, TILE), fixed(*out.shape), fixed(*lse.shape),
            ],
            out_specs=[fixed(rows, 3 * width), fixed(2 * pairs, kinds, 2 * TILE)],
            scratch_shapes=[
                pltpu.VMEM((rows, width), BF16),
                pltpu.VMEM((tiles, width, TILE), BF16),
                pltpu.VMEM((tiles, TILE, width), F32),
                pltpu.VMEM((tiles, TILE, width), F32),
                pltpu.VMEM((pairs, TILE, 2 * TILE), F32),
                pltpu.VMEM((pairs, kinds, TILE, 2 * TILE), F32),
            ],
        ),
    )(
        plan["place"], plan["start"], plan["count"], plan["kind"],
        *pieces, qkv, bias, plan["lab"], plan["labrow"], out, lse,
    )


EDGE = 16


def conv_body(
    order_ref, low_ref, high_ref, *refs, blocks, frames, chunks, lanes, taps,
):
    pieces, refs = refs[:2], refs[2:]
    taps_ref, lab_ref, act_ref, gated_ref, mixed_ref, glu_ref, window_ref, pad_ref, out_pad_ref = refs
    size = glu_ref.shape[0] // blocks
    assemble(glu_ref, pieces)
    channels = lanes * TILE
    half = taps // 2
    span = TILE + 2 * EDGE
    for lane in range(lanes):
        pad_ref[lane, :EDGE, :] = jnp.zeros((EDGE, TILE), F32)
    for block in range(blocks):
        here = pl.ds(pl.multiple_of(order_ref[block] * size, TILE), size)
        for lane in range(lanes):
            value = glu_ref[here, lane * TILE : (lane + 1) * TILE]
            gate = glu_ref[here, channels + lane * TILE : channels + (lane + 1) * TILE]
            first = EDGE + block * frames
            pad_ref[lane, first : first + size, :] = value * sigmoid(gate)
    rest = EDGE + (blocks - 1) * frames + size
    for lane in range(lanes):
        tail = pad_ref.shape[1] - rest
        pad_ref[lane, rest:, :] = jnp.zeros((tail, TILE), F32)

    def chunk(index, carry):
        base = pl.multiple_of(index * TILE, TILE)
        labels = lab_ref[pl.ds(base, span), :]
        center = labels[EDGE : EDGE + TILE]
        for lane in range(lanes):
            values = pad_ref[lane, pl.ds(base, span), :]
            gated_ref[pl.ds(base, TILE), lane * TILE : (lane + 1) * TILE] = values[
                EDGE : EDGE + TILE
            ]

            def segment(label, total):
                window_ref[...] = jnp.where(labels == label, values, 0.0)
                acc = jnp.zeros((TILE, TILE), F32)
                for tap in range(taps):
                    first = EDGE + tap - half
                    acc = acc + window_ref[first : first + TILE, :] * taps_ref[
                        tap : tap + 1, lane * TILE : (lane + 1) * TILE
                    ]
                return jnp.where(center == label, acc, total)

            total = lax.fori_loop(
                low_ref[index], high_ref[index] + 1, segment, jnp.zeros((TILE, TILE), F32)
            )
            mixed_ref[pl.ds(base, TILE), lane * TILE : (lane + 1) * TILE] = total
            out_pad_ref[lane, pl.ds(base, TILE), :] = total * sigmoid(total)
        return carry

    lax.fori_loop(0, chunks, chunk, 0)
    valid = lax.broadcasted_iota(jnp.int32, (size, TILE), 0) < frames
    for block in range(blocks):
        here = pl.ds(pl.multiple_of(order_ref[block] * size, TILE), size)
        for lane in range(lanes):
            rows = out_pad_ref[lane, block * frames : block * frames + size, :]
            act_ref[here, lane * TILE : (lane + 1) * TILE] = jnp.where(valid, rows, 0.0).astype(BF16)


def conv_forward(pieces, taps, plan):
    channels = pieces[0].shape[1] // 2
    blocks, frames, chunks = 4, plan["frames"], plan["chunks"]
    total = plan["tiles"] * TILE
    rows = chunks * TILE
    lanes = channels // TILE
    return call(
        functools.partial(
            conv_body, blocks=blocks, frames=frames, chunks=chunks, lanes=lanes, taps=taps.shape[0]
        ),
        "conv_forward",
        [
            shaped((total, channels), BF16),
            shaped((rows, channels), F32),
            shaped((rows, channels), F32),
            shaped((total, 2 * channels), F32),
        ],
        grid_spec=pltpu.PrefetchScalarGridSpec(
            num_scalar_prefetch=3,
            grid=(1,),
            in_specs=[fixed(*piece.shape) for piece in pieces]
            + [fixed(*taps.shape), fixed(*plan["flat_lab"].shape)],
            out_specs=[
                fixed(total, channels), fixed(rows, channels), fixed(rows, channels),
                fixed(total, 2 * channels),
            ],
            scratch_shapes=[
                pltpu.VMEM((TILE + 2 * EDGE, TILE), F32),
                pltpu.VMEM((lanes, rows + 2 * EDGE, TILE), F32),
                pltpu.VMEM((lanes, rows, TILE), F32),
            ],
        ),
    )(plan["order"], plan["low"], plan["high"], *pieces, taps, plan["flat_lab"])


def conv_back_body(
    order_ref, low_ref, high_ref, *refs, blocks, frames, chunks, lanes, taps,
):
    pieces, refs = refs[:2], refs[2:]
    (
        glu_ref, taps_ref, lab_ref, mixed_ref,
        dglu_ref, slope_ref,
        grad_ref, window_ref, dgate_ref,
    ) = refs
    size = glu_ref.shape[0] // blocks
    assemble(grad_ref, pieces)
    channels = lanes * TILE
    half = taps // 2
    span = TILE + 2 * EDGE
    rows = chunks * TILE
    for block in range(blocks):
        here = pl.ds(pl.multiple_of(order_ref[block] * size, TILE), size)
        for lane in range(lanes):
            first = EDGE + block * frames
            slope_ref[lane, first : first + size, :] = grad_ref[
                here, lane * TILE : (lane + 1) * TILE
            ]
    rest = EDGE + (blocks - 1) * frames + size
    for lane in range(lanes):
        slope_ref[lane, :EDGE, :] = jnp.zeros((EDGE, TILE), F32)
        slope_ref[lane, rest:, :] = jnp.zeros((slope_ref.shape[1] - rest, TILE), F32)
        mixed = mixed_ref[:, lane * TILE : (lane + 1) * TILE]
        gate = sigmoid(mixed)
        slope_ref[lane, EDGE : EDGE + rows, :] = slope_ref[lane, EDGE : EDGE + rows, :] * (
            gate * (1.0 + mixed * (1.0 - gate))
        )
        dgate_ref[lane, rows:, :] = jnp.zeros((dgate_ref.shape[1] - rows, TILE), F32)

    def chunk(index, carry):
        base = pl.multiple_of(index * TILE, TILE)
        labels = lab_ref[pl.ds(base, span), :]
        center = labels[EDGE : EDGE + TILE]
        for lane in range(lanes):
            slopes = slope_ref[lane, pl.ds(base, span), :]

            def segment(label, total):
                window_ref[...] = jnp.where(labels == label, slopes, 0.0)
                acc = jnp.zeros((TILE, TILE), F32)
                for tap in range(taps):
                    first = EDGE - tap + half
                    acc = acc + window_ref[first : first + TILE, :] * taps_ref[
                        tap : tap + 1, lane * TILE : (lane + 1) * TILE
                    ]
                return jnp.where(center == label, acc, total)

            dgate_ref[lane, pl.ds(base, TILE), :] = lax.fori_loop(
                low_ref[index], high_ref[index] + 1, segment, jnp.zeros((TILE, TILE), F32)
            )
        return carry

    lax.fori_loop(0, chunks, chunk, 0)
    valid = lax.broadcasted_iota(jnp.int32, (size, TILE), 0) < frames
    for block in range(blocks):
        here = pl.ds(pl.multiple_of(order_ref[block] * size, TILE), size)
        for lane in range(lanes):
            lead = slice(lane * TILE, (lane + 1) * TILE)
            follow = slice(channels + lane * TILE, channels + (lane + 1) * TILE)
            rows_in = dgate_ref[lane, block * frames : block * frames + size, :]
            rows_in = jnp.where(valid, rows_in, 0.0)
            value = glu_ref[here, lead]
            gate = sigmoid(glu_ref[here, follow])
            dglu_ref[here, lead] = (rows_in * gate).astype(BF16)
            dglu_ref[here, follow] = (rows_in * value * gate * (1.0 - gate)).astype(BF16)


def conv_backward(pieces, glu, taps, plan, mixed):
    channels = glu.shape[1] // 2
    blocks, frames, chunks = 4, plan["frames"], plan["chunks"]
    rows = chunks * TILE
    lanes = channels // TILE
    slope = (lanes, rows + 2 * EDGE, TILE)
    return call(
        functools.partial(
            conv_back_body, blocks=blocks, frames=frames, chunks=chunks,
            lanes=lanes, taps=taps.shape[0],
        ),
        "conv_backward",
        [shaped(glu.shape, BF16), shaped(slope, F32)],
        grid_spec=pltpu.PrefetchScalarGridSpec(
            num_scalar_prefetch=3,
            grid=(1,),
            in_specs=[fixed(*piece.shape) for piece in pieces]
            + [
                fixed(*glu.shape), fixed(*taps.shape), fixed(*plan["flat_lab"].shape),
                fixed(rows, channels),
            ],
            out_specs=[fixed(*glu.shape), fixed(*slope)],
            scratch_shapes=[
                pltpu.VMEM((glu.shape[0], channels), F32),
                pltpu.VMEM((TILE + 2 * EDGE, TILE), F32),
                pltpu.VMEM((lanes, rows + EDGE, TILE), F32),
            ],
        ),
    )(plan["order"], plan["low"], plan["high"], *pieces, glu, taps, plan["flat_lab"], mixed)


def taps_body(
    low_ref, high_ref, slope_ref, gated_ref, lab_ref, dtaps_ref, source_ref, window_ref, sums_ref,
    *, chunks, lanes, taps,
):
    half = taps // 2
    span = TILE + 2 * EDGE
    rows = chunks * TILE
    for lane in range(lanes):
        source_ref[lane, :EDGE, :] = jnp.zeros((EDGE, TILE), F32)
        source_ref[lane, EDGE : EDGE + rows, :] = gated_ref[:, lane * TILE : (lane + 1) * TILE]
        source_ref[lane, EDGE + rows :, :] = jnp.zeros((EDGE, TILE), F32)
    sums_ref[...] = jnp.zeros_like(sums_ref)

    def chunk(index, carry):
        base = pl.multiple_of(index * TILE, TILE)
        labels = lab_ref[pl.ds(base, span), :]
        center = labels[EDGE : EDGE + TILE]
        for lane in range(lanes):
            slopes = slope_ref[lane, pl.ds(base + EDGE, TILE), :]
            sources = source_ref[lane, pl.ds(base, span), :]

            def segment(label, kept):
                window_ref[...] = jnp.where(labels == label, sources, 0.0)
                inner = jnp.where(center == label, slopes, 0.0)
                for tap in range(taps):
                    first = EDGE + tap - half
                    part = fold(inner * window_ref[first : first + TILE, :])
                    sums_ref[lane, tap] += jnp.sum(part, axis=0)
                return kept

            lax.fori_loop(low_ref[index], high_ref[index] + 1, segment, 0)
        return carry

    lax.fori_loop(0, chunks, chunk, 0)
    for lane in range(lanes):
        dtaps_ref[:, lane * TILE : (lane + 1) * TILE] = jnp.sum(sums_ref[lane], axis=1)


def taps_backward(slope, gated, plan, taps):
    lanes, padded, _ = slope.shape
    chunks = plan["chunks"]
    shape = (taps, lanes * TILE)
    return call(
        functools.partial(taps_body, chunks=chunks, lanes=lanes, taps=taps),
        "taps_backward",
        shaped(shape, F32),
        grid_spec=pltpu.PrefetchScalarGridSpec(
            num_scalar_prefetch=2,
            grid=(1,),
            in_specs=[
                fixed(*slope.shape), fixed(*gated.shape), fixed(*plan["flat_lab"].shape),
            ],
            out_specs=fixed(*shape),
            scratch_shapes=[
                pltpu.VMEM((lanes, padded, TILE), F32),
                pltpu.VMEM((TILE + 2 * EDGE, TILE), F32),
                pltpu.VMEM((lanes, taps, 8, TILE), F32),
            ],
        ),
    )(plan["low"], plan["high"], slope, gated, plan["flat_lab"])


def swap(values, bit, axis="tensor"):
    count = lax.axis_size(axis)
    return lax.ppermute(values, axis, [(i, i ^ bit) for i in range(count)])


def gather(mine):
    return [mine, swap(mine, 1), swap(mine, 2)]


def tie(value, other):
    return lax.optimization_barrier((value, other))


def complete(blocks, near):
    blocks[2], near[0] = tie(blocks[2], near[0])
    blocks.append(swap(blocks[2], 1))


def scatter(own, beside, far, sent=None):
    arriving = []
    for across, diagonal in far:
        outgoing = (across.astype(F32) + swap(diagonal, 1).astype(F32)).astype(BF16)
        arriving.append(swap(outgoing, 2))
        if sent is not None:
            sent.append(outgoing)
    return [own, swap(beside, 1), arriving]


def sum_bits(values, axis, bit=1):
    while bit < lax.axis_size(axis):
        values = values + swap(values, bit, axis)
        bit *= 2
    return values


def halve_all(grad, gate):
    count = lax.axis_size("dp")
    bits = count.bit_length() - 1
    values = grad.reshape((2,) * bits + (grad.shape[0] // count, grad.shape[1]))
    for bit in range(bits):
        dim = bits - 1 - bit
        keep = (lax.axis_index("dp") >> bit) & 1
        sent = lax.dynamic_index_in_dim(values, 1 - keep, dim, keepdims=False)
        kept = lax.dynamic_index_in_dim(values, keep, dim, keepdims=False)
        arrived = swap(sent, 1 << bit, "dp")
        if bit == 0:
            arrived, gate = tie(arrived, gate)
        values = kept.astype(F32) + arrived.astype(F32)
        if bit < bits - 1:
            values = values.astype(BF16)
    return values, gate


def settle(grads):
    return lax.psum_scatter(grads, "dp", scatter_dimension=0, tiled=True)


def halves(array):
    return [(array, c, CHUNKS) for c in range(CHUNKS)]


def feed_forward(blocks, w_in, w_out):
    near = list(ff_rows(blocks[0], blocks[1], w_in, w_out))
    complete(blocks, near)
    far = [ff_rows(x1, x2, w_in, w_out) for x1, x2 in zip(halves(blocks[2]), halves(blocks[3]))]
    state = ([near[0]] + [f[0] for f in far], [near[1]] + [f[1] for f in far])
    return scatter(near[2], near[3], [f[2:] for f in far]), state


def feed_back(blocks, state, w_in, w_out):
    hidden, _ = state
    near = list(ff_back_rows(blocks[0], blocks[1], hidden[0], w_out, w_in))
    complete(blocks, near)
    far = [
        ff_back_rows(g1, g2, a, w_out, w_in)
        for g1, g2, a in zip(halves(blocks[2]), halves(blocks[3]), hidden[1:])
    ]
    parts = scatter(near[1], near[2], [f[1:] for f in far], outgoing := [])
    return parts, [near[0]] + [f[0] for f in far], outgoing


def zigzag(blocks):
    far = [item for pair in zip(halves(blocks[2]), halves(blocks[3])) for item in pair]
    return [blocks[0], blocks[1]] + far


def spread(blocks, weight, side, kind):
    near = [project(blocks[0], blocks[1], weight, side, kind)]
    complete(blocks, near)
    return near[0], project(blocks[2], blocks[3], weight, side, kind)


def collect(flat, weight, side):
    count = 4 * CHUNKS
    far = [
        expand((flat, 2 * CHUNKS + c, count), (flat, 3 * CHUNKS + c, count), weight, side)
        for c in range(CHUNKS)
    ]
    own, beside = expand((flat, 0, 4), (flat, 1, 4), weight, side)
    return scatter(own, beside, far)


def delayed(parts, other):
    own, beside, (first, *rest) = parts
    first, other = tie(first, other)
    return [own, beside, [first, *rest]], other


def make_plan(segments, frames, reach, head_width):
    blocks = lax.axis_size("tensor")
    here = lax.axis_index("tensor").astype(jnp.int32)
    size = pad_up(frames, TILE)
    per_block = size // TILE
    tiles = blocks * per_block
    offsets = tile_offsets(blocks, frames, per_block)
    kinds, table = bias_types(offsets, reach)
    flat = segments.reshape(-1).astype(jnp.int32)
    lab = jnp.pad(flat.reshape(blocks, frames), ((0, 0), (0, size - frames)), constant_values=-1)
    lab = lab.reshape(tiles, TILE)
    high = jnp.max(lab, axis=1)
    low = jnp.min(jnp.where(lab < 0, 1 << 20, lab), axis=1)
    seen = (low[:, None] <= high[None, :]) & (low[None, :] <= high[:, None])
    position = jnp.arange(tiles, dtype=jnp.int32)
    first = jnp.min(jnp.where(seen, position[None, :], tiles), axis=1)
    last = jnp.max(jnp.where(seen, position[None, :], -1), axis=1)
    count1 = last - first + 1
    count = (count1 + 1) // 2
    start = jnp.minimum(first, tiles - 2 * count)
    order = jnp.arange(blocks, dtype=jnp.int32) ^ here
    place = (order[:, None] * per_block + jnp.arange(per_block, dtype=jnp.int32)[None, :]).reshape(-1)
    total = blocks * frames
    chunks = pad_up(total, TILE) // TILE
    padded = jnp.pad(flat, (EDGE, chunks * TILE - total + EDGE), constant_values=-1)
    body = padded[EDGE : EDGE + chunks * TILE].reshape(chunks, TILE)
    return dict(
        kinds=kinds,
        kind=jnp.asarray(table.reshape(-1)),
        place=place,
        tiles=tiles,
        start=start,
        count=count,
        lab=jnp.broadcast_to(lab[:, :, None], (tiles, TILE, TILE)),
        labrow=lab[:, None, :],
        scale=float(head_width) ** -0.5,
        frames=frames,
        chunks=chunks,
        order=order,
        low=jnp.min(jnp.where(body < 0, 1 << 20, body), axis=1),
        high=jnp.max(body, axis=1),
        flat_lab=jnp.broadcast_to(padded[:, None], (padded.shape[0], TILE)),
    )


def shards(
    inputs, segments, cotangent, gain_one, first_in, first_out, gain_two, w_query, w_key, w_value,
    w_output, rel_table, gain_three, w_glu, kernel, w_back, gain_four, second_in, second_out,
    gain_five,
):
    frames, _, width = inputs.shape
    size = pad_up(frames, TILE)
    heads = rel_table.shape[0]
    reach = rel_table.shape[1] // 2
    head_width = w_query.shape[1] // heads

    def padded(values):
        return jnp.pad(values.reshape(frames, width), ((0, size - frames), (0, 0)))

    def total(sums):
        return sum(jnp.sum(part, axis=0) for part in sums)

    plan = make_plan(segments, frames, reach, head_width)
    onehot = column_onehot(plan["kinds"], reach)
    bias = bias_tiles(rel_table, onehot, plan["kinds"])
    w_qkv = jnp.concatenate([w_query, w_key, w_value], 1)
    channels = kernel.shape[1]
    glu_matrix = w_glu.reshape(width, 2 * channels)

    start = padded(inputs)
    h_one = gather(enter(start, gain_one))
    parts, state_one = feed_forward(h_one, first_in, first_out)
    h_two, one = join(start, parts, gain_two, 0.5)
    h_two = gather(h_two)
    out, lse, qkv = attend(spread(h_two, w_qkv, 0, BF16), bias, plan)
    h_three, two = join(one, collect(out, w_output, 0), gain_three, 1.0)
    h_three = gather(h_three)
    act, gated, mixed, glu = conv_forward(spread(h_three, glu_matrix, 0, F32), kernel, plan)
    h_four, three = join(two, collect(act, w_back, 0), gain_four, 1.0)
    h_four = gather(h_four)
    parts, state_four = feed_forward(h_four, second_in, second_out)

    grads, output, e4, sums = turn(three, parts, gain_five, padded(cotangent), 0.5, 0.5)
    grad_five = total(sums)
    grads = gather(grads)
    parts, inner, _ = feed_back(grads, state_four, second_in, second_out)
    parts, grad_w = delayed(
        parts, weight_grads([(zigzag(grads), state_four[1]), (zigzag(h_four), inner)])
    )
    settled_four = settle(grad_w)
    grads, e3, sums = join_back(e4, three, parts, gain_four, 1.0)
    grad_four = total(sums)
    grads = gather(grads)
    dglu, slope = conv_backward(spread(grads, w_back, 1, F32), glu, kernel, plan, mixed)
    parts, grad_w = delayed(
        collect(dglu, glu_matrix, 1), weight_grads([(grads, [act]), (h_three, [dglu])])
    )
    settled_three = settle(grad_w)
    grads, e2, sums = join_back(e3, two, parts, gain_three, 1.0)
    grad_three = total(sums)
    grads = gather(grads)
    grad_kernel = taps_backward(slope, gated, plan, kernel.shape[0])
    grads[2], grad_kernel = tie(grads[2], grad_kernel)
    pulled = spread(grads, w_output, 1, BF16)
    (first, second), settled_four = tie(pulled, settled_four)
    dqkv, table_sums = attend_back((first, second), qkv, bias, plan, out, lse)
    parts, grad_w = delayed(
        collect(dqkv, w_qkv, 1), weight_grads([(grads, [out]), (h_two, [dqkv])])
    )
    parts, settled_three = delayed(parts, settled_three)
    settled_two = settle(grad_w)
    grads, e1, sums = join_back(e2, one, parts, gain_two, 0.5)
    grad_two = total(sums)
    grads = gather(grads)
    parts, inner, outgoing = feed_back(grads, state_one, first_in, first_out)
    grad_w = weight_grads([(zigzag(grads), state_one[1])])
    grad_first_out = settle(grad_w)
    own, beside, (near_rows, far_rows) = parts
    near_rows, settled_two = tie(near_rows, settled_two)
    (_, _, (near_rows, _)), grad_first_in = delayed(
        [own, beside, [near_rows, far_rows]], weight_grads([(zigzag(h_one), inner)])
    )
    grad_first_in, far_rows = halve_all(grad_first_in, far_rows)
    parts = [own, beside, [near_rows, far_rows]]
    e0, sums = join_back(e1, start, parts, gain_one, 0.0)
    small, sums = tie(
        (table_sums, grad_kernel, grad_two, grad_three, grad_four, grad_five), sums
    )
    table_sums, grad_kernel, grad_two, grad_three, grad_four, grad_five = small
    grad_one = total(sums)
    grad_table = lax.dot_general(
        table_sums.reshape(heads, -1), onehot, (((1,), (1,)), ((), ())),
        precision=lax.Precision.HIGHEST, preferred_element_type=F32,
    )
    small = jnp.concatenate(
        [grad_one, grad_two, grad_three, grad_four, grad_five]
        + [grad_table.reshape(-1), grad_kernel.reshape(-1)]
    )
    gains = sum_bits(small[: 5 * width], "tensor")
    small = jnp.concatenate([gains, small[5 * width :]])
    small = sum_bits(small, "dp", 2)
    small = small + swap(small, 1, "dp")
    grad_gains = [small[i * width : (i + 1) * width] for i in range(5)]
    rest = small[5 * width :]
    grad_table = rest[: grad_table.size].reshape(grad_table.shape)
    grad_kernel = rest[grad_table.size :].reshape(grad_kernel.shape)
    part, own = w_query.shape[1], w_output.shape[0]
    settled_two, settled_three, settled_four, grad_first_out = (
        x.astype(F32) for x in (settled_two, settled_three, settled_four, grad_first_out)
    )
    return (
        jnp.concatenate(output, 0)[:frames].reshape(inputs.shape),
        e0[:frames].reshape(inputs.shape),
        grad_gains[0],
        grad_first_in,
        grad_first_out.T,
        grad_gains[1],
        settled_two[:, own : own + part],
        settled_two[:, own + part : own + 2 * part],
        settled_two[:, own + 2 * part :],
        settled_two[:, :own].T,
        grad_table,
        grad_gains[2],
        settled_three[:, channels:].reshape(-1, 2, channels),
        grad_kernel,
        settled_three[:, :channels].T,
        grad_gains[3],
        settled_four[:, second_out.shape[0] :],
        settled_four[:, : second_out.shape[0]].T,
        grad_gains[4],
    )


def solution(mesh):
    in_specs = (
        P("tensor", "dp", None), P("dp", None), P("tensor", "dp", None), P(),
        P(None, "tensor"), P("tensor", None), P(), P(None, "tensor"), P(None, "tensor"),
        P(None, "tensor"), P("tensor", None), P("tensor", None), P(), P(None, None, "tensor"),
        P(None, "tensor"), P("tensor", None), P(), P(None, "tensor"), P("tensor", None), P(),
    )
    out_specs = (
        P("tensor", "dp", None), P("tensor", "dp", None), P(), P("dp", "tensor"),
        P("tensor", "dp"), P(), P("dp", "tensor"), P("dp", "tensor"), P("dp", "tensor"),
        P("tensor", "dp"), P("tensor", None), P(), P("dp", None, "tensor"), P(None, "tensor"),
        P("tensor", "dp"), P(), P("dp", "tensor"), P("tensor", "dp"), P(),
    )
    return jax.shard_map(shards, mesh=mesh, in_specs=in_specs, out_specs=out_specs, check_vma=False)
```

```python
import functools

import jax
import jax.numpy as jnp
import numpy as np
from jax import lax
from jax.experimental import pallas as pl
from jax.experimental.pallas import tpu as pltpu
from jax.sharding import PartitionSpec as P

TILE = 128
MASKED = -1e30
F32 = jnp.float32
BF16 = jnp.bfloat16


def pad_up(size, unit):
    return -(-size // unit) * unit


CHUNKS = 2


def dot(a, b, ca, cb):
    return lax.dot_general(a, b, (((ca,), (cb,)), ((), ())), preferred_element_type=F32)


def sigmoid(values):
    return 0.5 * jnp.tanh(0.5 * values) + 0.5


def fixed(*shape):
    return pl.BlockSpec(shape, lambda *_: (0,) * len(shape))


def shaped(shape, kind):
    return jax.ShapeDtypeStruct(tuple(shape), kind)


BUDGET = dict(
    distance_bias=(3, 12), enter=(1, 4), join=(2, 4), turn=(3, 6), join_back=(3, 5),
    ff_rows=(4, 14), ff_back_rows=(4, 14), project=(2, 10), expand=(2, 8),
    weight_grads=(5, 20), attend=(24, 24), attend_back=(43, 30),
    conv_forward=(11, 20), conv_backward=(9, 28), taps_backward=(8, 12),
)
COST_SCALE = 0.1


def call(body, name, out_shape, cost=1.0, **options):
    time, limit = BUDGET[name]
    time = time * cost * COST_SCALE
    return pl.pallas_call(
        body,
        out_shape=out_shape,
        compiler_params=pltpu.CompilerParams(vmem_limit_bytes=limit * 2**20),
        cost_estimate=pl.CostEstimate(
            flops=1024, bytes_accessed=int(time * 3.5e6), transcendentals=0
        ),
        name=name,
        **options,
    )


def tile_offsets(blocks, block_frames, per_block):
    starts = np.array([b * block_frames + t * TILE for b in range(blocks) for t in range(per_block)])
    return starts[None, :] - starts[:, None]


def bias_types(offsets, reach):
    near = sorted({int(d) for d in offsets.ravel() if abs(int(d)) < reach + TILE - 1})
    far = 4 * TILE + reach
    kinds = near + [-far, far]
    index = {d: i for i, d in enumerate(near)}
    table = np.array(
        [
            [index.get(int(d), len(near) + (1 if d > 0 else 0)) for d in row]
            for row in offsets
        ],
        np.int32,
    )
    return kinds, table


def column_onehot(kinds, reach):
    lane = lax.broadcasted_iota(jnp.int32, (len(kinds), 2 * TILE), 1)
    signed = jnp.where(lane < TILE, lane, lane - 2 * TILE)
    base = jnp.array(kinds, jnp.int32)[:, None]
    column = jnp.clip(base - signed, -reach, reach) + reach
    width = 2 * reach + 1
    flat = column.reshape(-1)
    return (flat[None, :] == jnp.arange(width, dtype=jnp.int32)[:, None]).astype(F32)


def bias_body(row_ref, out_ref, *, pairs, count):
    for p in range(pairs):
        for kind in range(count):
            for head in range(2):
                line = jnp.broadcast_to(row_ref[2 * p + head, kind : kind + 1, :], (TILE, 2 * TILE))
                skewed = pltpu.roll(line, 0, 1, stride=1, stride_axis=0)
                out_ref[p, kind, :, head * TILE : (head + 1) * TILE] = skewed[:, :TILE]


def bias_tiles(rel_table, onehot, kinds):
    heads = rel_table.shape[0]
    pairs = heads // 2
    count = len(kinds)
    rows = jnp.dot(rel_table, onehot, precision=lax.Precision.HIGHEST, preferred_element_type=F32)
    return call(
        functools.partial(bias_body, pairs=pairs, count=count),
        "distance_bias",
        shaped((pairs, count, TILE, 2 * TILE), F32),
    )(rows.reshape(heads, count, 2 * TILE))


SLAB = 16


def unit_rows(rows):
    mean = jnp.mean(rows, axis=-1, keepdims=True)
    centred = rows - mean
    rstd = lax.rsqrt(jnp.mean(centred * centred, axis=-1, keepdims=True) + 1e-05)
    return centred * rstd, rstd


def pull_back(unit, rstd, scaled):
    first = jnp.mean(scaled, axis=-1, keepdims=True)
    second = jnp.mean(scaled * unit, axis=-1, keepdims=True)
    return rstd * (scaled - first - unit * second)


def fold(values):
    return values.reshape(values.shape[0] // 8, 8, values.shape[1])


def slabs(rows, body):
    def step(i, carry):
        body(pl.ds(pl.multiple_of(i * SLAB, SLAB), SLAB))
        return carry

    lax.fori_loop(0, rows // SLAB, step, 0, unroll=2)


def enter(rows, gain):
    def body(r_ref, g_ref, h_ref):
        def slab(at):
            unit, _ = unit_rows(r_ref[at, :].astype(F32))
            h_ref[at, :] = (unit * g_ref[...]).astype(BF16)

        slabs(r_ref.shape[0], slab)

    return call(body, "enter", shaped(rows.shape, BF16))(rows, gain[None, :])


def received(at, refs):
    return refs[0][at, :].astype(F32) + refs[1][at, :].astype(F32) + refs[2][at, :].astype(F32)


def by_chunks(body, name, arrays, gain, kinds, sums=0):
    some = next(x for x in arrays if not isinstance(x, list))
    size, width = some.shape
    cut = int(size // CHUNKS)
    lone = fixed(cut, width)
    filled, lists = None, [[] for _ in kinds[1:]]
    for chunk in range(CHUNKS):
        piece = pl.BlockSpec((cut, width), lambda i, chunk=chunk: (chunk, 0))
        inputs = [x[chunk] if isinstance(x, list) else x for x in arrays]
        specs = [lone if isinstance(x, list) else piece for x in arrays]
        inputs.append(gain[None, :])
        specs.append(fixed(1, width))
        aliases = {}
        run = body
        if filled is not None:
            aliases = {len(inputs): 0}
            inputs.append(filled)
            specs.append(pl.BlockSpec(memory_space=pl.ANY))
            count = len(inputs)
            run = lambda *refs, count=count: body(*refs[: count - 1], *refs[count:])
        shapes = [shaped((size, width), kinds[0])]
        outs = [piece]
        for i, kind in enumerate(kinds[1:]):
            is_sum = i >= len(kinds) - 1 - sums
            shape = (8, width) if is_sum else (cut, width)
            shapes.append(shaped(shape, kind))
            outs.append(fixed(*shape))
        filled, *others = call(
            run, name, shapes, grid=(1,), in_specs=specs, out_specs=outs,
            input_output_aliases=aliases,
        )(*inputs)
        for place, other in zip(lists, others):
            place.append(other)
    return filled, *lists


def join(rows, parts, gain, factor):
    def body(r_ref, p1_ref, p2_ref, p3_ref, g_ref, h_ref, out_ref):
        def slab(at):
            total = r_ref[at, :].astype(F32) + factor * received(at, (p1_ref, p2_ref, p3_ref))
            out_ref[at, :] = total
            unit, _ = unit_rows(total)
            h_ref[at, :] = (unit * g_ref[...]).astype(BF16)

        slabs(r_ref.shape[0], slab)

    return by_chunks(body, "join", [rows, *parts], gain, [BF16, F32])


def turn(rows, parts, gain, cotangent, factor, onward):
    def body(r_ref, p1_ref, p2_ref, p3_ref, c_ref, g_ref, next_ref, out_ref, e_ref, sum_ref):
        sum_ref[...] = jnp.zeros_like(sum_ref)

        def slab(at):
            total = r_ref[at, :].astype(F32) + factor * received(at, (p1_ref, p2_ref, p3_ref))
            unit, rstd = unit_rows(total)
            out_ref[at, :] = (unit * g_ref[...]).astype(BF16)
            grad = c_ref[at, :].astype(F32)
            sum_ref[...] += jnp.sum(fold(grad * unit), axis=0)
            e = pull_back(unit, rstd, grad * g_ref[...])
            e_ref[at, :] = e
            next_ref[at, :] = (onward * e).astype(BF16)

        slabs(r_ref.shape[0], slab)

    return by_chunks(
        body, "turn", [rows, *parts, cotangent], gain, [BF16, BF16, F32, F32], sums=1
    )


def join_back(incoming, rows, parts, gain, onward):
    def body(e_ref, r_ref, p1_ref, p2_ref, p3_ref, g_ref, next_ref, *more):
        out_ref, sum_ref = more if onward else (next_ref, more[0])
        sum_ref[...] = jnp.zeros_like(sum_ref)

        def slab(at):
            unit, rstd = unit_rows(r_ref[at, :].astype(F32))
            grad = received(at, (p1_ref, p2_ref, p3_ref))
            sum_ref[...] += jnp.sum(fold(grad * unit), axis=0)
            e = e_ref[at, :] + pull_back(unit, rstd, grad * g_ref[...])
            out_ref[at, :] = e
            if onward:
                next_ref[at, :] = (onward * e).astype(BF16)

        slabs(r_ref.shape[0], slab)

    kinds = [BF16, F32, F32] if onward else [F32, F32]
    return by_chunks(body, "join_back", [incoming, rows, *parts], gain, kinds, sums=1)


def pieces_of(arrays):
    specs, plain = [], []
    for entry in arrays:
        array, i, n = entry if isinstance(entry, tuple) else (entry, 0, 1)
        shape = (array.shape[0] // n, array.shape[1])
        specs.append(pl.BlockSpec(shape, lambda *_, i=i: (i, 0)))
        plain.append(array)
    return specs, plain


def row_blocks(rows, at, block):
    step = rows // 2 if rows > 256 else rows

    def one(i, carry):
        here = pl.multiple_of(i * step, step)
        block(pl.ds(here, step), pl.ds(here + at, step))
        return carry

    lax.fori_loop(0, rows // step, one, 0)


def ff_rows(x1, x2, w_in, w_out):
    specs, plain = pieces_of([x1, x2])
    rows, width = specs[0].block_shape

    def body(x1_ref, x2_ref, w_in_ref, w_out_ref, a_ref, z_ref, u1_ref, u2_ref):
        for x_ref, u_ref, at in ((x1_ref, u1_ref, 0), (x2_ref, u2_ref, rows)):

            def block(here, there):
                a = dot(x_ref[here, :], w_in_ref[...], 1, 0)
                z = (a * sigmoid(a)).astype(BF16)
                a_ref[there, :] = a.astype(BF16)
                z_ref[there, :] = z
                u_ref[here, :] = dot(z, w_out_ref[...], 1, 0).astype(BF16)

            row_blocks(rows, at, block)

    wide = (2 * rows, w_in.shape[1])
    return call(
        body, "ff_rows", [shaped(wide, BF16)] * 2 + [shaped((rows, width), BF16)] * 2, grid=(1,),
        in_specs=specs + [fixed(*w_in.shape), fixed(*w_out.shape)],
        out_specs=[fixed(*wide)] * 2 + [fixed(rows, width)] * 2,
    )(*plain, w_in, w_out)


def ff_back_rows(g1, g2, a, w_out, w_in):
    specs, plain = pieces_of([g1, g2])
    rows, width = specs[0].block_shape

    def body(g1_ref, g2_ref, a_ref, w_out_ref, w_in_ref, ea_ref, p1_ref, p2_ref):
        for g_ref, p_ref, at in ((g1_ref, p1_ref, 0), (g2_ref, p2_ref, rows)):

            def block(here, there):
                ez = dot(g_ref[here, :], w_out_ref[...], 1, 1)
                a = a_ref[there, :].astype(F32)
                s = sigmoid(a)
                ea = (ez * s * (1.0 + a * (1.0 - s))).astype(BF16)
                ea_ref[there, :] = ea
                p_ref[here, :] = dot(ea, w_in_ref[...], 1, 1).astype(BF16)

            row_blocks(rows, at, block)

    return call(
        body, "ff_back_rows", [shaped(a.shape, BF16)] + [shaped((rows, width), BF16)] * 2,
        grid=(1,),
        in_specs=specs + [fixed(*a.shape), fixed(*w_out.shape), fixed(*w_in.shape)],
        out_specs=[fixed(*a.shape)] + [fixed(rows, width)] * 2,
    )(*plain, a, w_out, w_in)


def project(x1, x2, weight, side, kind):
    def body(x1_ref, x2_ref, w_ref, y_ref):
        rows = x1_ref.shape[0]
        y_ref[:rows, :] = dot(x1_ref[...], w_ref[...], 1, side).astype(kind)
        y_ref[rows:, :] = dot(x2_ref[...], w_ref[...], 1, side).astype(kind)

    shape = (2 * x1.shape[0], weight.shape[1 - side])
    return call(body, "project", shaped(shape, kind))(x1, x2, weight)


def expand(x1, x2, weight, side):
    specs, plain = pieces_of([x1, x2])

    def body(x1_ref, x2_ref, w_ref, y1_ref, y2_ref):
        y1_ref[...] = dot(x1_ref[...], w_ref[...], 1, side).astype(BF16)
        y2_ref[...] = dot(x2_ref[...], w_ref[...], 1, side).astype(BF16)

    shape = (specs[0].block_shape[0], weight.shape[1 - side])
    return call(
        body, "expand", [shaped(shape, BF16)] * 2, grid=(1,),
        in_specs=specs + [fixed(*weight.shape)],
        out_specs=[fixed(*shape)] * 2,
    )(*plain, weight)


def weight_grads(products):
    entries, spans, at, column = [], [], 0, 0
    for left, right in products:
        entries += left + right
        first = right[0][0] if isinstance(right[0], tuple) else right[0]
        spans.append((at, at + len(left), at + len(left) + len(right), column))
        at += len(left) + len(right)
        column += first.shape[1]
    specs, plain = pieces_of(entries)
    height = specs[0].block_shape[1]
    tile = 2 * TILE

    def body(*refs):
        out_ref = refs[-1]

        def band(i, carry):
            here = pl.ds(pl.multiple_of(i * tile, tile), tile)
            for first, middle, last, column in spans:
                left = jnp.concatenate([ref[:, here] for ref in refs[first:middle]], 0)
                right = jnp.concatenate([ref[...] for ref in refs[middle:last]], 0)
                out_ref[here, column : column + right.shape[1]] = dot(left, right, 0, 0).astype(
                    BF16
                )
            return carry

        lax.fori_loop(0, height // tile, band, 0)

    return call(
        body, "weight_grads", shaped((height, column), BF16), grid=(1,),
        in_specs=specs, out_specs=fixed(height, column),
    )(*plain)


def stacked_heads(pair):
    low_half = lax.broadcasted_iota(jnp.int32, pair.shape, 1) < pair.shape[1] // 2
    zero = jnp.zeros_like(pair)
    return jnp.concatenate([jnp.where(low_half, pair, zero), jnp.where(low_half, zero, pair)], 0)


def own_quadrants(wide):
    half = lax.broadcasted_iota(jnp.int32, (TILE, TILE), 0) < TILE // 2
    return jnp.where(half, wide[:, :TILE], wide[:, TILE:])


def assemble(target_ref, piece_refs):
    rows = piece_refs[0].shape[0]
    for i, ref in enumerate(piece_refs):
        target_ref[i * rows : (i + 1) * rows, :] = ref[...]


def tile_rows(index):
    return pl.ds(pl.multiple_of(index * TILE, TILE), TILE)


def attend_body(
    place_ref, start_ref, count_ref, kind_ref, *refs, tiles, pairs, scale,
):
    pieces, refs = refs[:2], refs[2:]
    bias_ref, lab_ref, labrow_ref, out_ref, lse_ref, qkv_ref, score_ref, turned_ref, acc_ref = refs
    step = pl.program_id(0)
    width = pairs * TILE

    @pl.when(step == 0)
    def _():
        assemble(qkv_ref, pieces)
        for tile in range(tiles):
            turned_ref[tile] = qkv_ref[tile_rows(place_ref[tile]), 2 * width :].T

    mine = qkv_ref[tile_rows(place_ref[step]), :]
    queries = [
        stacked_heads(mine[:, p * TILE : (p + 1) * TILE] * scale) for p in range(pairs)
    ]
    own_label = labrow_ref[step]
    begin = start_ref[step]
    trips = count_ref[step]

    def scores(trip, best):
        couple = [begin + 2 * trip + sub for sub in range(2)]
        kinds = [kind_ref[step * tiles + tile] for tile in couple]
        allowed = [lab_ref[tile] == own_label for tile in couple]
        keys = jnp.concatenate(
            [qkv_ref[tile_rows(place_ref[tile]), width : 2 * width] for tile in couple], 0
        )
        parts = []
        for p in range(pairs):
            both = dot(keys[:, p * TILE : (p + 1) * TILE], queries[p], 1, 1)
            highs = []
            for sub in range(2):
                raw = both[sub * TILE : (sub + 1) * TILE] + bias_ref[p, kinds[sub]]
                pair_high = []
                for h in range(2):
                    part = jnp.where(allowed[sub], raw[:, h * TILE : (h + 1) * TILE], MASKED)
                    span = slice((2 * p + h) * TILE, (2 * p + h + 1) * TILE)
                    score_ref[couple[sub], :, span] = part
                    pair_high.append(jnp.max(fold(part), axis=0))
                highs.append(jnp.concatenate(pair_high, 1))
            parts.append(jnp.maximum(*highs))
        return jnp.maximum(best, jnp.concatenate(parts, 1))

    best = lax.fori_loop(0, trips, scores, jnp.full((8, 2 * width), MASKED, F32))
    top = jnp.max(best, axis=0, keepdims=True)
    acc_ref[...] = jnp.zeros_like(acc_ref)

    def mix(trip, total):
        first = begin + 2 * trip
        probs = []
        for sub in range(2):
            value = jnp.exp(score_ref[first + sub] - top)
            total = total + jnp.sum(fold(value), axis=0)
            probs.append(value.astype(BF16))
        both = jnp.concatenate(probs, 0)
        for p in range(pairs):
            turned = jnp.concatenate(
                [turned_ref[first + sub, p * TILE : (p + 1) * TILE, :] for sub in range(2)], 1
            )
            acc_ref[p] += dot(turned, both[:, 2 * p * TILE : 2 * (p + 1) * TILE], 1, 0)
        return total

    total = lax.fori_loop(0, trips, mix, jnp.zeros((8, 2 * width), F32))
    total = jnp.sum(total, axis=0, keepdims=True)
    inverse = 1.0 / total
    log_total = top + jnp.log(total)
    for p in range(pairs):
        wide = acc_ref[p] * inverse[:, 2 * p * TILE : 2 * (p + 1) * TILE]
        out_ref[:, p * TILE : (p + 1) * TILE] = own_quadrants(wide).T.astype(BF16)
    for h in range(2 * pairs):
        lse_ref[0, h : h + 1, :] = log_total[:, h * TILE : (h + 1) * TILE]


def attend(pieces, bias, plan):
    pairs = bias.shape[0]
    width = pairs * TILE
    tiles = plan["tiles"]
    rows = tiles * TILE
    return call(
        functools.partial(attend_body, tiles=tiles, pairs=pairs, scale=plan["scale"]),
        "attend",
        [
            shaped((rows, width), BF16),
            shaped((tiles, 2 * pairs, TILE), F32),
            shaped((rows, 3 * width), BF16),
        ],
        grid_spec=pltpu.PrefetchScalarGridSpec(
            num_scalar_prefetch=4,
            grid=(tiles,),
            in_specs=[fixed(*piece.shape) for piece in pieces]
            + [fixed(*bias.shape), fixed(tiles, TILE, TILE), fixed(tiles, 1, TILE)],
            out_specs=[
                pl.BlockSpec((TILE, width), lambda i, place, *_: (place[i], 0)),
                pl.BlockSpec((1, 2 * pairs, TILE), lambda i, *_: (i, 0, 0)),
                fixed(rows, 3 * width),
            ],
            scratch_shapes=[
                pltpu.VMEM((tiles, TILE, 2 * width), F32),
                pltpu.VMEM((tiles, width, TILE), BF16),
                pltpu.VMEM((pairs, TILE, 2 * TILE), F32),
            ],
        ),
    )(
        plan["place"], plan["start"], plan["count"], plan["kind"],
        *pieces, bias, plan["lab"], plan["labrow"],
    )


def unskew(values):
    wide = jnp.concatenate([values, jnp.zeros_like(values)], 1)
    rows = TILE
    while rows > 8:
        rows //= 2
        wide = wide[:rows] + pltpu.roll(wide[rows:], 2 * TILE - rows, 1)
    row = lax.broadcasted_iota(jnp.int32, wide.shape, 0)
    for bit in (4, 2, 1):
        wide = jnp.where((row & bit) != 0, pltpu.roll(wide, 2 * TILE - bit, 1), wide)
    return jnp.sum(wide, axis=0, keepdims=True)


def attend_back_body(
    place_ref, start_ref, count_ref, kind_ref, *refs, tiles, pairs, scale, kinds,
):
    pieces, refs = refs[:2], refs[2:]
    (
        qkv_ref, bias_ref, lab_ref, labrow_ref, out_ref, lse_ref,
        dqkv_ref, table_ref,
        grad_ref, turned_ref, dk_ref, dv_ref, dq_ref, sums_ref,
    ) = refs
    step = pl.program_id(0)
    width = pairs * TILE

    @pl.when(step == 0)
    def _():
        assemble(grad_ref, pieces)
        for tile in range(tiles):
            turned_ref[tile] = qkv_ref[tile_rows(place_ref[tile]), width : 2 * width].T
        dk_ref[...] = jnp.zeros_like(dk_ref)
        dv_ref[...] = jnp.zeros_like(dv_ref)
        sums_ref[...] = jnp.zeros_like(sums_ref)

    here = tile_rows(place_ref[step])
    queries, grads, deltas, logs = [], [], [], []
    for p in range(pairs):
        span = slice(p * TILE, (p + 1) * TILE)
        queries.append(stacked_heads(qkv_ref[here, span] * scale))
        grad = grad_ref[here, span]
        grads.append(stacked_heads(grad))
        product = (grad.astype(F32) * out_ref[here, span].astype(F32)).T
        half = TILE // 2
        deltas.append(
            jnp.concatenate(
                [
                    jnp.sum(product[:half], axis=0, keepdims=True),
                    jnp.sum(product[half:], axis=0, keepdims=True),
                ],
                1,
            )
        )
        logs.append(jnp.concatenate([lse_ref[step, 2 * p + h : 2 * p + h + 1, :] for h in range(2)], 1))
    own_label = labrow_ref[step]
    begin = start_ref[step]
    dq_ref[...] = jnp.zeros_like(dq_ref)

    def visit(trip, carry):
        couple = [begin + 2 * trip + sub for sub in range(2)]
        kind = [kind_ref[step * tiles + tile] for tile in couple]
        there = [tile_rows(place_ref[tile]) for tile in couple]
        allowed = jnp.concatenate([lab_ref[tile] == own_label for tile in couple], 0)
        allowed = jnp.concatenate([allowed, allowed], 1)
        for p in range(pairs):
            span = slice(p * TILE, (p + 1) * TILE)
            key_span = slice(width + p * TILE, width + (p + 1) * TILE)
            value_span = slice(2 * width + p * TILE, 2 * width + (p + 1) * TILE)
            keys = jnp.concatenate([qkv_ref[at, key_span] for at in there], 0)
            vals = jnp.concatenate([qkv_ref[at, value_span] for at in there], 0)
            bias = jnp.concatenate([bias_ref[p, k] for k in kind], 0)
            raw = dot(keys, queries[p], 1, 1) + bias
            prob = jnp.exp(jnp.where(allowed, raw - logs[p], MASKED))
            lift = dot(vals, grads[p], 1, 1)
            slope = prob * (lift - deltas[p])
            low = slope.astype(BF16)
            dv = dot(prob.astype(BF16), grads[p], 1, 0)
            dk = dot(low, queries[p], 1, 0)
            for sub in range(2):
                part = slice(sub * TILE, (sub + 1) * TILE)
                sums_ref[p, kind[sub]] += slope[part]
                dv_ref[couple[sub], :, span] += dv[part]
                dk_ref[couple[sub], :, span] += dk[part]
            turned = jnp.concatenate([turned_ref[tile, span, :] for tile in couple], 1)
            dq_ref[p] += dot(turned, low, 1, 0)
        return carry

    lax.fori_loop(0, count_ref[step], visit, 0)
    for p in range(pairs):
        span = slice(p * TILE, (p + 1) * TILE)
        dqkv_ref[here, span] = (own_quadrants(dq_ref[p]).T * scale).astype(BF16)

    @pl.when(step == tiles - 1)
    def _():
        for tile in range(tiles):
            there = tile_rows(place_ref[tile])
            dqkv_ref[there, width : 2 * width] = dk_ref[tile].astype(BF16)
            dqkv_ref[there, 2 * width :] = dv_ref[tile].astype(BF16)
        for p in range(pairs):
            for kind in range(kinds):
                for h in range(2):
                    table_ref[2 * p + h, kind : kind + 1, :] = unskew(
                        sums_ref[p, kind, :, h * TILE : (h + 1) * TILE]
                    )


def attend_back(pieces, qkv, bias, plan, out, lse):
    tiles, pairs, kinds = plan["tiles"], bias.shape[0], bias.shape[1]
    width = pairs * TILE
    rows = tiles * TILE
    return call(
        functools.partial(
            attend_back_body, tiles=tiles, pairs=pairs, scale=plan["scale"], kinds=kinds
        ),
        "attend_back",
        [shaped((rows, 3 * width), BF16), shaped((2 * pairs, kinds, 2 * TILE), F32)],
        grid_spec=pltpu.PrefetchScalarGridSpec(
            num_scalar_prefetch=4,
            grid=(tiles,),
            in_specs=[fixed(*piece.shape) for piece in pieces]
            + [
                fixed(*qkv.shape), fixed(*bias.shape), fixed(tiles, TILE, TILE),
                fixed(tiles, 1, TILE), fixed(*out.shape), fixed(*lse.shape),
            ],
            out_specs=[fixed(rows, 3 * width), fixed(2 * pairs, kinds, 2 * TILE)],
            scratch_shapes=[
                pltpu.VMEM((rows, width), BF16),
                pltpu.VMEM((tiles, width, TILE), BF16),
                pltpu.VMEM((tiles, TILE, width), F32),
                pltpu.VMEM((tiles, TILE, width), F32),
                pltpu.VMEM((pairs, TILE, 2 * TILE), F32),
                pltpu.VMEM((pairs, kinds, TILE, 2 * TILE), F32),
            ],
        ),
    )(
        plan["place"], plan["start"], plan["count"], plan["kind"],
        *pieces, qkv, bias, plan["lab"], plan["labrow"], out, lse,
    )


EDGE = 16


def conv_body(
    order_ref, low_ref, high_ref, *refs, blocks, frames, chunks, lanes, taps,
):
    pieces, refs = refs[:2], refs[2:]
    taps_ref, lab_ref, act_ref, gated_ref, mixed_ref, glu_ref, window_ref, pad_ref, out_pad_ref = refs
    size = glu_ref.shape[0] // blocks
    assemble(glu_ref, pieces)
    channels = lanes * TILE
    half = taps // 2
    span = TILE + 2 * EDGE
    for lane in range(lanes):
        pad_ref[lane, :EDGE, :] = jnp.zeros((EDGE, TILE), F32)
    for block in range(blocks):
        here = pl.ds(pl.multiple_of(order_ref[block] * size, TILE), size)
        for lane in range(lanes):
            value = glu_ref[here, lane * TILE : (lane + 1) * TILE]
            gate = glu_ref[here, channels + lane * TILE : channels + (lane + 1) * TILE]
            first = EDGE + block * frames
            pad_ref[lane, first : first + size, :] = value * sigmoid(gate)
    rest = EDGE + (blocks - 1) * frames + size
    for lane in range(lanes):
        tail = pad_ref.shape[1] - rest
        pad_ref[lane, rest:, :] = jnp.zeros((tail, TILE), F32)

    def chunk(index, carry):
        base = pl.multiple_of(index * TILE, TILE)
        labels = lab_ref[pl.ds(base, span), :]
        center = labels[EDGE : EDGE + TILE]
        for lane in range(lanes):
            values = pad_ref[lane, pl.ds(base, span), :]
            gated_ref[pl.ds(base, TILE), lane * TILE : (lane + 1) * TILE] = values[
                EDGE : EDGE + TILE
            ]

            def segment(label, total):
                window_ref[...] = jnp.where(labels == label, values, 0.0)
                acc = jnp.zeros((TILE, TILE), F32)
                for tap in range(taps):
                    first = EDGE + tap - half
                    acc = acc + window_ref[first : first + TILE, :] * taps_ref[
                        tap : tap + 1, lane * TILE : (lane + 1) * TILE
                    ]
                return jnp.where(center == label, acc, total)

            total = lax.fori_loop(
                low_ref[index], high_ref[index] + 1, segment, jnp.zeros((TILE, TILE), F32)
            )
            mixed_ref[pl.ds(base, TILE), lane * TILE : (lane + 1) * TILE] = total
            out_pad_ref[lane, pl.ds(base, TILE), :] = total * sigmoid(total)
        return carry

    lax.fori_loop(0, chunks, chunk, 0)
    valid = lax.broadcasted_iota(jnp.int32, (size, TILE), 0) < frames
    for block in range(blocks):
        here = pl.ds(pl.multiple_of(order_ref[block] * size, TILE), size)
        for lane in range(lanes):
            rows = out_pad_ref[lane, block * frames : block * frames + size, :]
            act_ref[here, lane * TILE : (lane + 1) * TILE] = jnp.where(valid, rows, 0.0).astype(BF16)


def conv_forward(pieces, taps, plan):
    channels = pieces[0].shape[1] // 2
    blocks, frames, chunks = 4, plan["frames"], plan["chunks"]
    total = plan["tiles"] * TILE
    rows = chunks * TILE
    lanes = channels // TILE
    return call(
        functools.partial(
            conv_body, blocks=blocks, frames=frames, chunks=chunks, lanes=lanes, taps=taps.shape[0]
        ),
        "conv_forward",
        [
            shaped((total, channels), BF16),
            shaped((rows, channels), F32),
            shaped((rows, channels), F32),
            shaped((total, 2 * channels), F32),
        ],
        grid_spec=pltpu.PrefetchScalarGridSpec(
            num_scalar_prefetch=3,
            grid=(1,),
            in_specs=[fixed(*piece.shape) for piece in pieces]
            + [fixed(*taps.shape), fixed(*plan["flat_lab"].shape)],
            out_specs=[
                fixed(total, channels), fixed(rows, channels), fixed(rows, channels),
                fixed(total, 2 * channels),
            ],
            scratch_shapes=[
                pltpu.VMEM((TILE + 2 * EDGE, TILE), F32),
                pltpu.VMEM((lanes, rows + 2 * EDGE, TILE), F32),
                pltpu.VMEM((lanes, rows, TILE), F32),
            ],
        ),
    )(plan["order"], plan["low"], plan["high"], *pieces, taps, plan["flat_lab"])


def conv_back_body(
    order_ref, low_ref, high_ref, *refs, blocks, frames, chunks, lanes, taps,
):
    pieces, refs = refs[:2], refs[2:]
    (
        glu_ref, taps_ref, lab_ref, mixed_ref,
        dglu_ref, slope_ref,
        grad_ref, window_ref, dgate_ref,
    ) = refs
    size = glu_ref.shape[0] // blocks
    assemble(grad_ref, pieces)
    channels = lanes * TILE
    half = taps // 2
    span = TILE + 2 * EDGE
    rows = chunks * TILE
    for block in range(blocks):
        here = pl.ds(pl.multiple_of(order_ref[block] * size, TILE), size)
        for lane in range(lanes):
            first = EDGE + block * frames
            slope_ref[lane, first : first + size, :] = grad_ref[
                here, lane * TILE : (lane + 1) * TILE
            ]
    rest = EDGE + (blocks - 1) * frames + size
    for lane in range(lanes):
        slope_ref[lane, :EDGE, :] = jnp.zeros((EDGE, TILE), F32)
        slope_ref[lane, rest:, :] = jnp.zeros((slope_ref.shape[1] - rest, TILE), F32)
        mixed = mixed_ref[:, lane * TILE : (lane + 1) * TILE]
        gate = sigmoid(mixed)
        slope_ref[lane, EDGE : EDGE + rows, :] = slope_ref[lane, EDGE : EDGE + rows, :] * (
            gate * (1.0 + mixed * (1.0 - gate))
        )
        dgate_ref[lane, rows:, :] = jnp.zeros((dgate_ref.shape[1] - rows, TILE), F32)

    def chunk(index, carry):
        base = pl.multiple_of(index * TILE, TILE)
        labels = lab_ref[pl.ds(base, span), :]
        center = labels[EDGE : EDGE + TILE]
        for lane in range(lanes):
            slopes = slope_ref[lane, pl.ds(base, span), :]

            def segment(label, total):
                window_ref[...] = jnp.where(labels == label, slopes, 0.0)
                acc = jnp.zeros((TILE, TILE), F32)
                for tap in range(taps):
                    first = EDGE - tap + half
                    acc = acc + window_ref[first : first + TILE, :] * taps_ref[
                        tap : tap + 1, lane * TILE : (lane + 1) * TILE
                    ]
                return jnp.where(center == label, acc, total)

            dgate_ref[lane, pl.ds(base, TILE), :] = lax.fori_loop(
                low_ref[index], high_ref[index] + 1, segment, jnp.zeros((TILE, TILE), F32)
            )
        return carry

    lax.fori_loop(0, chunks, chunk, 0)
    valid = lax.broadcasted_iota(jnp.int32, (size, TILE), 0) < frames
    for block in range(blocks):
        here = pl.ds(pl.multiple_of(order_ref[block] * size, TILE), size)
        for lane in range(lanes):
            lead = slice(lane * TILE, (lane + 1) * TILE)
            follow = slice(channels + lane * TILE, channels + (lane + 1) * TILE)
            rows_in = dgate_ref[lane, block * frames : block * frames + size, :]
            rows_in = jnp.where(valid, rows_in, 0.0)
            value = glu_ref[here, lead]
            gate = sigmoid(glu_ref[here, follow])
            dglu_ref[here, lead] = (rows_in * gate).astype(BF16)
            dglu_ref[here, follow] = (rows_in * value * gate * (1.0 - gate)).astype(BF16)


def conv_backward(pieces, glu, taps, plan, mixed):
    channels = glu.shape[1] // 2
    blocks, frames, chunks = 4, plan["frames"], plan["chunks"]
    rows = chunks * TILE
    lanes = channels // TILE
    slope = (lanes, rows + 2 * EDGE, TILE)
    return call(
        functools.partial(
            conv_back_body, blocks=blocks, frames=frames, chunks=chunks,
            lanes=lanes, taps=taps.shape[0],
        ),
        "conv_backward",
        [shaped(glu.shape, BF16), shaped(slope, F32)],
        grid_spec=pltpu.PrefetchScalarGridSpec(
            num_scalar_prefetch=3,
            grid=(1,),
            in_specs=[fixed(*piece.shape) for piece in pieces]
            + [
                fixed(*glu.shape), fixed(*taps.shape), fixed(*plan["flat_lab"].shape),
                fixed(rows, channels),
            ],
            out_specs=[fixed(*glu.shape), fixed(*slope)],
            scratch_shapes=[
                pltpu.VMEM((glu.shape[0], channels), F32),
                pltpu.VMEM((TILE + 2 * EDGE, TILE), F32),
                pltpu.VMEM((lanes, rows + EDGE, TILE), F32),
            ],
        ),
    )(plan["order"], plan["low"], plan["high"], *pieces, glu, taps, plan["flat_lab"], mixed)


def taps_body(
    low_ref, high_ref, slope_ref, gated_ref, lab_ref, dtaps_ref, source_ref, window_ref, sums_ref,
    *, chunks, lanes, taps,
):
    half = taps // 2
    span = TILE + 2 * EDGE
    rows = chunks * TILE
    for lane in range(lanes):
        source_ref[lane, :EDGE, :] = jnp.zeros((EDGE, TILE), F32)
        source_ref[lane, EDGE : EDGE + rows, :] = gated_ref[:, lane * TILE : (lane + 1) * TILE]
        source_ref[lane, EDGE + rows :, :] = jnp.zeros((EDGE, TILE), F32)
    sums_ref[...] = jnp.zeros_like(sums_ref)

    def chunk(index, carry):
        base = pl.multiple_of(index * TILE, TILE)
        labels = lab_ref[pl.ds(base, span), :]
        center = labels[EDGE : EDGE + TILE]
        for lane in range(lanes):
            slopes = slope_ref[lane, pl.ds(base + EDGE, TILE), :]
            sources = source_ref[lane, pl.ds(base, span), :]

            def segment(label, kept):
                window_ref[...] = jnp.where(labels == label, sources, 0.0)
                inner = jnp.where(center == label, slopes, 0.0)
                for tap in range(taps):
                    first = EDGE + tap - half
                    part = fold(inner * window_ref[first : first + TILE, :])
                    sums_ref[lane, tap] += jnp.sum(part, axis=0)
                return kept

            lax.fori_loop(low_ref[index], high_ref[index] + 1, segment, 0)
        return carry

    lax.fori_loop(0, chunks, chunk, 0)
    for lane in range(lanes):
        dtaps_ref[:, lane * TILE : (lane + 1) * TILE] = jnp.sum(sums_ref[lane], axis=1)


def taps_backward(slope, gated, plan, taps):
    lanes, padded, _ = slope.shape
    chunks = plan["chunks"]
    shape = (taps, lanes * TILE)
    return call(
        functools.partial(taps_body, chunks=chunks, lanes=lanes, taps=taps),
        "taps_backward",
        shaped(shape, F32),
        grid_spec=pltpu.PrefetchScalarGridSpec(
            num_scalar_prefetch=2,
            grid=(1,),
            in_specs=[
                fixed(*slope.shape), fixed(*gated.shape), fixed(*plan["flat_lab"].shape),
            ],
            out_specs=fixed(*shape),
            scratch_shapes=[
                pltpu.VMEM((lanes, padded, TILE), F32),
                pltpu.VMEM((TILE + 2 * EDGE, TILE), F32),
                pltpu.VMEM((lanes, taps, 8, TILE), F32),
            ],
        ),
    )(plan["low"], plan["high"], slope, gated, plan["flat_lab"])


def swap(values, bit, axis="tensor"):
    count = lax.axis_size(axis)
    return lax.ppermute(values, axis, [(i, i ^ bit) for i in range(count)])


def gather(mine):
    return [mine, swap(mine, 1), swap(mine, 2)]


def tie(value, other):
    return lax.optimization_barrier((value, other))


def complete(blocks, near):
    blocks[2], near[0] = tie(blocks[2], near[0])
    blocks.append(swap(blocks[2], 1))


def scatter(own, beside, far, sent=None):
    arriving = []
    for across, diagonal in far:
        outgoing = (across.astype(F32) + swap(diagonal, 1).astype(F32)).astype(BF16)
        arriving.append(swap(outgoing, 2))
        if sent is not None:
            sent.append(outgoing)
    return [own, swap(beside, 1), arriving]


def sum_bits(values, axis, bit=1):
    while bit < lax.axis_size(axis):
        values = values + swap(values, bit, axis)
        bit *= 2
    return values


def halve_all(grad, gate):
    count = lax.axis_size("dp")
    bits = count.bit_length() - 1
    values = grad.reshape((2,) * bits + (grad.shape[0] // count, grad.shape[1]))
    for bit in range(bits):
        dim = bits - 1 - bit
        keep = (lax.axis_index("dp") >> bit) & 1
        sent = lax.dynamic_index_in_dim(values, 1 - keep, dim, keepdims=False)
        kept = lax.dynamic_index_in_dim(values, keep, dim, keepdims=False)
        if bit == 1:
            sent, gate = tie(sent, gate)
        arrived = swap(sent, 1 << bit, "dp")
        values = kept.astype(F32) + arrived.astype(F32)
        if bit < bits - 1:
            values = values.astype(BF16)
    return values, gate


def settle(grads):
    return lax.psum_scatter(grads, "dp", scatter_dimension=0, tiled=True)


def halves(array):
    return [(array, c, CHUNKS) for c in range(CHUNKS)]


def feed_forward(blocks, w_in, w_out):
    near = list(ff_rows(blocks[0], blocks[1], w_in, w_out))
    complete(blocks, near)
    far = [ff_rows(x1, x2, w_in, w_out) for x1, x2 in zip(halves(blocks[2]), halves(blocks[3]))]
    state = ([near[0]] + [f[0] for f in far], [near[1]] + [f[1] for f in far])
    return scatter(near[2], near[3], [f[2:] for f in far]), state


def feed_back(blocks, state, w_in, w_out):
    hidden, _ = state
    near = list(ff_back_rows(blocks[0], blocks[1], hidden[0], w_out, w_in))
    complete(blocks, near)
    far = [
        ff_back_rows(g1, g2, a, w_out, w_in)
        for g1, g2, a in zip(halves(blocks[2]), halves(blocks[3]), hidden[1:])
    ]
    parts = scatter(near[1], near[2], [f[1:] for f in far], outgoing := [])
    return parts, [near[0]] + [f[0] for f in far], outgoing


def zigzag(blocks):
    far = [item for pair in zip(halves(blocks[2]), halves(blocks[3])) for item in pair]
    return [blocks[0], blocks[1]] + far


def spread(blocks, weight, side, kind):
    near = [project(blocks[0], blocks[1], weight, side, kind)]
    complete(blocks, near)
    return near[0], project(blocks[2], blocks[3], weight, side, kind)


def collect(flat, weight, side):
    count = 4 * CHUNKS
    far = [
        expand((flat, 2 * CHUNKS + c, count), (flat, 3 * CHUNKS + c, count), weight, side)
        for c in range(CHUNKS)
    ]
    own, beside = expand((flat, 0, 4), (flat, 1, 4), weight, side)
    return scatter(own, beside, far)


def delayed(parts, other):
    own, beside, (first, *rest) = parts
    first, other = tie(first, other)
    return [own, beside, [first, *rest]], other


def make_plan(segments, frames, reach, head_width):
    blocks = lax.axis_size("tensor")
    here = lax.axis_index("tensor").astype(jnp.int32)
    size = pad_up(frames, TILE)
    per_block = size // TILE
    tiles = blocks * per_block
    offsets = tile_offsets(blocks, frames, per_block)
    kinds, table = bias_types(offsets, reach)
    flat = segments.reshape(-1).astype(jnp.int32)
    lab = jnp.pad(flat.reshape(blocks, frames), ((0, 0), (0, size - frames)), constant_values=-1)
    lab = lab.reshape(tiles, TILE)
    high = jnp.max(lab, axis=1)
    low = jnp.min(jnp.where(lab < 0, 1 << 20, lab), axis=1)
    seen = (low[:, None] <= high[None, :]) & (low[None, :] <= high[:, None])
    position = jnp.arange(tiles, dtype=jnp.int32)
    first = jnp.min(jnp.where(seen, position[None, :], tiles), axis=1)
    last = jnp.max(jnp.where(seen, position[None, :], -1), axis=1)
    count1 = last - first + 1
    count = (count1 + 1) // 2
    start = jnp.minimum(first, tiles - 2 * count)
    order = jnp.arange(blocks, dtype=jnp.int32) ^ here
    place = (order[:, None] * per_block + jnp.arange(per_block, dtype=jnp.int32)[None, :]).reshape(-1)
    total = blocks * frames
    chunks = pad_up(total, TILE) // TILE
    padded = jnp.pad(flat, (EDGE, chunks * TILE - total + EDGE), constant_values=-1)
    body = padded[EDGE : EDGE + chunks * TILE].reshape(chunks, TILE)
    return dict(
        kinds=kinds,
        kind=jnp.asarray(table.reshape(-1)),
        place=place,
        tiles=tiles,
        start=start,
        count=count,
        lab=jnp.broadcast_to(lab[:, :, None], (tiles, TILE, TILE)),
        labrow=lab[:, None, :],
        scale=float(head_width) ** -0.5,
        frames=frames,
        chunks=chunks,
        order=order,
        low=jnp.min(jnp.where(body < 0, 1 << 20, body), axis=1),
        high=jnp.max(body, axis=1),
        flat_lab=jnp.broadcast_to(padded[:, None], (padded.shape[0], TILE)),
    )


def shards(
    inputs, segments, cotangent, gain_one, first_in, first_out, gain_two, w_query, w_key, w_value,
    w_output, rel_table, gain_three, w_glu, kernel, w_back, gain_four, second_in, second_out,
    gain_five,
):
    frames, _, width = inputs.shape
    size = pad_up(frames, TILE)
    heads = rel_table.shape[0]
    reach = rel_table.shape[1] // 2
    head_width = w_query.shape[1] // heads

    def padded(values):
        return jnp.pad(values.reshape(frames, width), ((0, size - frames), (0, 0)))

    def total(sums):
        return sum(jnp.sum(part, axis=0) for part in sums)

    plan = make_plan(segments, frames, reach, head_width)
    onehot = column_onehot(plan["kinds"], reach)
    bias = bias_tiles(rel_table, onehot, plan["kinds"])
    w_qkv = jnp.concatenate([w_query, w_key, w_value], 1)
    channels = kernel.shape[1]
    glu_matrix = w_glu.reshape(width, 2 * channels)

    start = padded(inputs)
    h_one = gather(enter(start, gain_one))
    parts, state_one = feed_forward(h_one, first_in, first_out)
    h_two, one = join(start, parts, gain_two, 0.5)
    h_two = gather(h_two)
    out, lse, qkv = attend(spread(h_two, w_qkv, 0, BF16), bias, plan)
    h_three, two = join(one, collect(out, w_output, 0), gain_three, 1.0)
    h_three = gather(h_three)
    act, gated, mixed, glu = conv_forward(spread(h_three, glu_matrix, 0, F32), kernel, plan)
    h_four, three = join(two, collect(act, w_back, 0), gain_four, 1.0)
    h_four = gather(h_four)
    parts, state_four = feed_forward(h_four, second_in, second_out)

    grads, output, e4, sums = turn(three, parts, gain_five, padded(cotangent), 0.5, 0.5)
    grad_five = total(sums)
    grads = gather(grads)
    parts, inner, _ = feed_back(grads, state_four, second_in, second_out)
    parts, grad_w = delayed(
        parts, weight_grads([(zigzag(grads), state_four[1]), (zigzag(h_four), inner)])
    )
    settled_four = settle(grad_w)
    grads, e3, sums = join_back(e4, three, parts, gain_four, 1.0)
    grad_four = total(sums)
    grads = gather(grads)
    dglu, slope = conv_backward(spread(grads, w_back, 1, F32), glu, kernel, plan, mixed)
    parts, grad_w = delayed(
        collect(dglu, glu_matrix, 1), weight_grads([(grads, [act]), (h_three, [dglu])])
    )
    settled_three = settle(grad_w)
    grads, e2, sums = join_back(e3, two, parts, gain_three, 1.0)
    grad_three = total(sums)
    grads = gather(grads)
    grad_kernel = taps_backward(slope, gated, plan, kernel.shape[0])
    grads[2], grad_kernel = tie(grads[2], grad_kernel)
    pulled = spread(grads, w_output, 1, BF16)
    (first, second), settled_four = tie(pulled, settled_four)
    dqkv, table_sums = attend_back((first, second), qkv, bias, plan, out, lse)
    parts, grad_w = delayed(
        collect(dqkv, w_qkv, 1), weight_grads([(grads, [out]), (h_two, [dqkv])])
    )
    parts, settled_three = delayed(parts, settled_three)
    settled_two = settle(grad_w)
    grads, e1, sums = join_back(e2, one, parts, gain_two, 0.5)
    grad_two = total(sums)
    grads = gather(grads)
    parts, inner, outgoing = feed_back(grads, state_one, first_in, first_out)
    grad_w = weight_grads([(zigzag(grads), state_one[1])])
    grad_first_out = settle(grad_w)
    own, beside, (near_rows, far_rows) = parts
    near_rows, settled_two = tie(near_rows, settled_two)
    (_, _, (near_rows, _)), grad_first_in = delayed(
        [own, beside, [near_rows, far_rows]], weight_grads([(zigzag(h_one), inner)])
    )
    grad_first_in, far_rows = halve_all(grad_first_in, far_rows)
    parts = [own, beside, [near_rows, far_rows]]
    e0, sums = join_back(e1, start, parts, gain_one, 0.0)
    small, sums = tie(
        (table_sums, grad_kernel, grad_two, grad_three, grad_four, grad_five), sums
    )
    table_sums, grad_kernel, grad_two, grad_three, grad_four, grad_five = small
    grad_one = total(sums)
    grad_table = lax.dot_general(
        table_sums.reshape(heads, -1), onehot, (((1,), (1,)), ((), ())),
        precision=lax.Precision.HIGHEST, preferred_element_type=F32,
    )
    small = jnp.concatenate(
        [grad_one, grad_two, grad_three, grad_four, grad_five]
        + [grad_table.reshape(-1), grad_kernel.reshape(-1)]
    )
    gains = sum_bits(small[: 5 * width], "tensor")
    small = jnp.concatenate([gains, small[5 * width :]])
    small = sum_bits(small, "dp", 2)
    small = small + swap(small, 1, "dp")
    grad_gains = [small[i * width : (i + 1) * width] for i in range(5)]
    rest = small[5 * width :]
    grad_table = rest[: grad_table.size].reshape(grad_table.shape)
    grad_kernel = rest[grad_table.size :].reshape(grad_kernel.shape)
    part, own = w_query.shape[1], w_output.shape[0]
    settled_two, settled_three, settled_four, grad_first_out = (
        x.astype(F32) for x in (settled_two, settled_three, settled_four, grad_first_out)
    )
    return (
        jnp.concatenate(output, 0)[:frames].reshape(inputs.shape),
        e0[:frames].reshape(inputs.shape),
        grad_gains[0],
        grad_first_in,
        grad_first_out.T,
        grad_gains[1],
        settled_two[:, own : own + part],
        settled_two[:, own + part : own + 2 * part],
        settled_two[:, own + 2 * part :],
        settled_two[:, :own].T,
        grad_table,
        grad_gains[2],
        settled_three[:, channels:].reshape(-1, 2, channels),
        grad_kernel,
        settled_three[:, :channels].T,
        grad_gains[3],
        settled_four[:, second_out.shape[0] :],
        settled_four[:, : second_out.shape[0]].T,
        grad_gains[4],
    )


def solution(mesh):
    in_specs = (
        P("tensor", "dp", None), P("dp", None), P("tensor", "dp", None), P(),
        P(None, "tensor"), P("tensor", None), P(), P(None, "tensor"), P(None, "tensor"),
        P(None, "tensor"), P("tensor", None), P("tensor", None), P(), P(None, None, "tensor"),
        P(None, "tensor"), P("tensor", None), P(), P(None, "tensor"), P("tensor", None), P(),
    )
    out_specs = (
        P("tensor", "dp", None), P("tensor", "dp", None), P(), P("dp", "tensor"),
        P("tensor", "dp"), P(), P("dp", "tensor"), P("dp", "tensor"), P("dp", "tensor"),
        P("tensor", "dp"), P("tensor", None), P(), P("dp", None, "tensor"), P(None, "tensor"),
        P("tensor", "dp"), P(), P("dp", "tensor"), P("tensor", "dp"), P(),
    )
    return jax.shard_map(shards, mesh=mesh, in_specs=in_specs, out_specs=out_specs, check_vma=False)
```

```python
import functools

import jax
import jax.numpy as jnp
import numpy as np
from jax import lax
from jax.experimental import pallas as pl
from jax.experimental.pallas import tpu as pltpu
from jax.sharding import PartitionSpec as P

TILE = 128
MASKED = -1e30
F32 = jnp.float32
BF16 = jnp.bfloat16


def pad_up(size, unit):
    return -(-size // unit) * unit


CHUNKS = 2


def dot(a, b, ca, cb):
    return lax.dot_general(a, b, (((ca,), (cb,)), ((), ())), preferred_element_type=F32)


def sigmoid(values):
    return 0.5 * jnp.tanh(0.5 * values) + 0.5


def fixed(*shape):
    return pl.BlockSpec(shape, lambda *_: (0,) * len(shape))


def shaped(shape, kind):
    return jax.ShapeDtypeStruct(tuple(shape), kind)


BUDGET = dict(
    distance_bias=(3, 12), enter=(1, 4), join=(2, 4), turn=(3, 6), join_back=(3, 5),
    ff_rows=(4, 14), ff_back_rows=(4, 14), project=(2, 10), expand=(2, 8),
    weight_grads=(5, 20), attend=(24, 24), attend_back=(43, 30),
    conv_forward=(11, 20), conv_backward=(9, 28), taps_backward=(8, 12),
)
COST_SCALE = 0.1


def call(body, name, out_shape, cost=1.0, **options):
    time, limit = BUDGET[name]
    time = time * cost * COST_SCALE
    return pl.pallas_call(
        body,
        out_shape=out_shape,
        compiler_params=pltpu.CompilerParams(vmem_limit_bytes=limit * 2**20),
        cost_estimate=pl.CostEstimate(
            flops=1024, bytes_accessed=int(time * 3.5e6), transcendentals=0
        ),
        name=name,
        **options,
    )


def tile_offsets(blocks, block_frames, per_block):
    starts = np.array([b * block_frames + t * TILE for b in range(blocks) for t in range(per_block)])
    return starts[None, :] - starts[:, None]


def bias_types(offsets, reach):
    near = sorted({int(d) for d in offsets.ravel() if abs(int(d)) < reach + TILE - 1})
    far = 4 * TILE + reach
    kinds = near + [-far, far]
    index = {d: i for i, d in enumerate(near)}
    table = np.array(
        [
            [index.get(int(d), len(near) + (1 if d > 0 else 0)) for d in row]
            for row in offsets
        ],
        np.int32,
    )
    return kinds, table


def column_onehot(kinds, reach):
    lane = lax.broadcasted_iota(jnp.int32, (len(kinds), 2 * TILE), 1)
    signed = jnp.where(lane < TILE, lane, lane - 2 * TILE)
    base = jnp.array(kinds, jnp.int32)[:, None]
    column = jnp.clip(base - signed, -reach, reach) + reach
    width = 2 * reach + 1
    flat = column.reshape(-1)
    return (flat[None, :] == jnp.arange(width, dtype=jnp.int32)[:, None]).astype(F32)


def bias_body(row_ref, out_ref, *, pairs, count):
    for p in range(pairs):
        for kind in range(count):
            for head in range(2):
                line = jnp.broadcast_to(row_ref[2 * p + head, kind : kind + 1, :], (TILE, 2 * TILE))
                skewed = pltpu.roll(line, 0, 1, stride=1, stride_axis=0)
                out_ref[p, kind, :, head * TILE : (head + 1) * TILE] = skewed[:, :TILE]


def bias_tiles(rel_table, onehot, kinds):
    heads = rel_table.shape[0]
    pairs = heads // 2
    count = len(kinds)
    rows = jnp.dot(rel_table, onehot, precision=lax.Precision.HIGHEST, preferred_element_type=F32)
    return call(
        functools.partial(bias_body, pairs=pairs, count=count),
        "distance_bias",
        shaped((pairs, count, TILE, 2 * TILE), F32),
    )(rows.reshape(heads, count, 2 * TILE))


SLAB = 16


def unit_rows(rows):
    mean = jnp.mean(rows, axis=-1, keepdims=True)
    centred = rows - mean
    rstd = lax.rsqrt(jnp.mean(centred * centred, axis=-1, keepdims=True) + 1e-05)
    return centred * rstd, rstd


def pull_back(unit, rstd, scaled):
    first = jnp.mean(scaled, axis=-1, keepdims=True)
    second = jnp.mean(scaled * unit, axis=-1, keepdims=True)
    return rstd * (scaled - first - unit * second)


def fold(values):
    return values.reshape(values.shape[0] // 8, 8, values.shape[1])


def slabs(rows, body):
    def step(i, carry):
        body(pl.ds(pl.multiple_of(i * SLAB, SLAB), SLAB))
        return carry

    lax.fori_loop(0, rows // SLAB, step, 0, unroll=2)


def enter(rows, gain):
    def body(r_ref, g_ref, h_ref):
        def slab(at):
            unit, _ = unit_rows(r_ref[at, :].astype(F32))
            h_ref[at, :] = (unit * g_ref[...]).astype(BF16)

        slabs(r_ref.shape[0], slab)

    return call(body, "enter", shaped(rows.shape, BF16))(rows, gain[None, :])


def received(at, refs):
    return refs[0][at, :].astype(F32) + refs[1][at, :].astype(F32) + refs[2][at, :].astype(F32)


def by_chunks(body, name, arrays, gain, kinds, sums=0):
    some = next(x for x in arrays if not isinstance(x, list))
    size, width = some.shape
    cut = int(size // CHUNKS)
    lone = fixed(cut, width)
    filled, lists = None, [[] for _ in kinds[1:]]
    for chunk in range(CHUNKS):
        piece = pl.BlockSpec((cut, width), lambda i, chunk=chunk: (chunk, 0))
        inputs = [x[chunk] if isinstance(x, list) else x for x in arrays]
        specs = [lone if isinstance(x, list) else piece for x in arrays]
        inputs.append(gain[None, :])
        specs.append(fixed(1, width))
        aliases = {}
        run = body
        if filled is not None:
            aliases = {len(inputs): 0}
            inputs.append(filled)
            specs.append(pl.BlockSpec(memory_space=pl.ANY))
            count = len(inputs)
            run = lambda *refs, count=count: body(*refs[: count - 1], *refs[count:])
        shapes = [shaped((size, width), kinds[0])]
        outs = [piece]
        for i, kind in enumerate(kinds[1:]):
            is_sum = i >= len(kinds) - 1 - sums
            shape = (8, width) if is_sum else (cut, width)
            shapes.append(shaped(shape, kind))
            outs.append(fixed(*shape))
        filled, *others = call(
            run, name, shapes, grid=(1,), in_specs=specs, out_specs=outs,
            input_output_aliases=aliases,
        )(*inputs)
        for place, other in zip(lists, others):
            place.append(other)
    return filled, *lists


def join(rows, parts, gain, factor):
    def body(r_ref, p1_ref, p2_ref, p3_ref, g_ref, h_ref, out_ref):
        def slab(at):
            total = r_ref[at, :].astype(F32) + factor * received(at, (p1_ref, p2_ref, p3_ref))
            out_ref[at, :] = total
            unit, _ = unit_rows(total)
            h_ref[at, :] = (unit * g_ref[...]).astype(BF16)

        slabs(r_ref.shape[0], slab)

    return by_chunks(body, "join", [rows, *parts], gain, [BF16, F32])


def turn(rows, parts, gain, cotangent, factor, onward):
    def body(r_ref, p1_ref, p2_ref, p3_ref, c_ref, g_ref, next_ref, out_ref, e_ref, sum_ref):
        sum_ref[...] = jnp.zeros_like(sum_ref)

        def slab(at):
            total = r_ref[at, :].astype(F32) + factor * received(at, (p1_ref, p2_ref, p3_ref))
            unit, rstd = unit_rows(total)
            out_ref[at, :] = (unit * g_ref[...]).astype(BF16)
            grad = c_ref[at, :].astype(F32)
            sum_ref[...] += jnp.sum(fold(grad * unit), axis=0)
            e = pull_back(unit, rstd, grad * g_ref[...])
            e_ref[at, :] = e
            next_ref[at, :] = (onward * e).astype(BF16)

        slabs(r_ref.shape[0], slab)

    return by_chunks(
        body, "turn", [rows, *parts, cotangent], gain, [BF16, BF16, F32, F32], sums=1
    )


def join_back(incoming, rows, parts, gain, onward):
    def body(e_ref, r_ref, p1_ref, p2_ref, p3_ref, g_ref, next_ref, *more):
        out_ref, sum_ref = more if onward else (next_ref, more[0])
        sum_ref[...] = jnp.zeros_like(sum_ref)

        def slab(at):
            unit, rstd = unit_rows(r_ref[at, :].astype(F32))
            grad = received(at, (p1_ref, p2_ref, p3_ref))
            sum_ref[...] += jnp.sum(fold(grad * unit), axis=0)
            e = e_ref[at, :] + pull_back(unit, rstd, grad * g_ref[...])
            out_ref[at, :] = e
            if onward:
                next_ref[at, :] = (onward * e).astype(BF16)

        slabs(r_ref.shape[0], slab)

    kinds = [BF16, F32, F32] if onward else [F32, F32]
    return by_chunks(body, "join_back", [incoming, rows, *parts], gain, kinds, sums=1)


def pieces_of(arrays):
    specs, plain = [], []
    for entry in arrays:
        array, i, n = entry if isinstance(entry, tuple) else (entry, 0, 1)
        shape = (array.shape[0] // n, array.shape[1])
        specs.append(pl.BlockSpec(shape, lambda *_, i=i: (i, 0)))
        plain.append(array)
    return specs, plain


def row_blocks(rows, at, block):
    step = rows // 2 if rows > 256 else rows

    def one(i, carry):
        here = pl.multiple_of(i * step, step)
        block(pl.ds(here, step), pl.ds(here + at, step))
        return carry

    lax.fori_loop(0, rows // step, one, 0)


def ff_rows(x1, x2, w_in, w_out):
    specs, plain = pieces_of([x1, x2])
    rows, width = specs[0].block_shape

    def body(x1_ref, x2_ref, w_in_ref, w_out_ref, a_ref, z_ref, u1_ref, u2_ref):
        for x_ref, u_ref, at in ((x1_ref, u1_ref, 0), (x2_ref, u2_ref, rows)):

            def block(here, there):
                a = dot(x_ref[here, :], w_in_ref[...], 1, 0)
                z = (a * sigmoid(a)).astype(BF16)
                a_ref[there, :] = a.astype(BF16)
                z_ref[there, :] = z
                u_ref[here, :] = dot(z, w_out_ref[...], 1, 0).astype(BF16)

            row_blocks(rows, at, block)

    wide = (2 * rows, w_in.shape[1])
    return call(
        body, "ff_rows", [shaped(wide, BF16)] * 2 + [shaped((rows, width), BF16)] * 2, grid=(1,),
        in_specs=specs + [fixed(*w_in.shape), fixed(*w_out.shape)],
        out_specs=[fixed(*wide)] * 2 + [fixed(rows, width)] * 2,
    )(*plain, w_in, w_out)


def ff_back_rows(g1, g2, a, w_out, w_in):
    specs, plain = pieces_of([g1, g2])
    rows, width = specs[0].block_shape

    def body(g1_ref, g2_ref, a_ref, w_out_ref, w_in_ref, ea_ref, p1_ref, p2_ref):
        for g_ref, p_ref, at in ((g1_ref, p1_ref, 0), (g2_ref, p2_ref, rows)):

            def block(here, there):
                ez = dot(g_ref[here, :], w_out_ref[...], 1, 1)
                a = a_ref[there, :].astype(F32)
                s = sigmoid(a)
                ea = (ez * s * (1.0 + a * (1.0 - s))).astype(BF16)
                ea_ref[there, :] = ea
                p_ref[here, :] = dot(ea, w_in_ref[...], 1, 1).astype(BF16)

            row_blocks(rows, at, block)

    return call(
        body, "ff_back_rows", [shaped(a.shape, BF16)] + [shaped((rows, width), BF16)] * 2,
        grid=(1,),
        in_specs=specs + [fixed(*a.shape), fixed(*w_out.shape), fixed(*w_in.shape)],
        out_specs=[fixed(*a.shape)] + [fixed(rows, width)] * 2,
    )(*plain, a, w_out, w_in)


def project(x1, x2, weight, side, kind):
    def body(x1_ref, x2_ref, w_ref, y_ref):
        rows = x1_ref.shape[0]
        y_ref[:rows, :] = dot(x1_ref[...], w_ref[...], 1, side).astype(kind)
        y_ref[rows:, :] = dot(x2_ref[...], w_ref[...], 1, side).astype(kind)

    shape = (2 * x1.shape[0], weight.shape[1 - side])
    return call(body, "project", shaped(shape, kind))(x1, x2, weight)


def expand(x1, x2, weight, side):
    specs, plain = pieces_of([x1, x2])

    def body(x1_ref, x2_ref, w_ref, y1_ref, y2_ref):
        y1_ref[...] = dot(x1_ref[...], w_ref[...], 1, side).astype(BF16)
        y2_ref[...] = dot(x2_ref[...], w_ref[...], 1, side).astype(BF16)

    shape = (specs[0].block_shape[0], weight.shape[1 - side])
    return call(
        body, "expand", [shaped(shape, BF16)] * 2, grid=(1,),
        in_specs=specs + [fixed(*weight.shape)],
        out_specs=[fixed(*shape)] * 2,
    )(*plain, weight)


def weight_grads(products):
    entries, spans, at, column = [], [], 0, 0
    for left, right in products:
        entries += left + right
        first = right[0][0] if isinstance(right[0], tuple) else right[0]
        spans.append((at, at + len(left), at + len(left) + len(right), column))
        at += len(left) + len(right)
        column += first.shape[1]
    specs, plain = pieces_of(entries)
    height = specs[0].block_shape[1]
    tile = 2 * TILE

    def body(*refs):
        out_ref = refs[-1]

        def band(i, carry):
            here = pl.ds(pl.multiple_of(i * tile, tile), tile)
            for first, middle, last, column in spans:
                left = jnp.concatenate([ref[:, here] for ref in refs[first:middle]], 0)
                right = jnp.concatenate([ref[...] for ref in refs[middle:last]], 0)
                out_ref[here, column : column + right.shape[1]] = dot(left, right, 0, 0).astype(
                    BF16
                )
            return carry

        lax.fori_loop(0, height // tile, band, 0)

    return call(
        body, "weight_grads", shaped((height, column), BF16), grid=(1,),
        in_specs=specs, out_specs=fixed(height, column),
    )(*plain)


def stacked_heads(pair):
    low_half = lax.broadcasted_iota(jnp.int32, pair.shape, 1) < pair.shape[1] // 2
    zero = jnp.zeros_like(pair)
    return jnp.concatenate([jnp.where(low_half, pair, zero), jnp.where(low_half, zero, pair)], 0)


def own_quadrants(wide):
    half = lax.broadcasted_iota(jnp.int32, (TILE, TILE), 0) < TILE // 2
    return jnp.where(half, wide[:, :TILE], wide[:, TILE:])


def assemble(target_ref, piece_refs):
    rows = piece_refs[0].shape[0]
    for i, ref in enumerate(piece_refs):
        target_ref[i * rows : (i + 1) * rows, :] = ref[...]


def tile_rows(index):
    return pl.ds(pl.multiple_of(index * TILE, TILE), TILE)


def attend_body(
    place_ref, start_ref, count_ref, kind_ref, *refs, tiles, pairs, scale,
):
    pieces, refs = refs[:2], refs[2:]
    bias_ref, lab_ref, labrow_ref, out_ref, lse_ref, qkv_ref, score_ref, turned_ref, acc_ref = refs
    step = pl.program_id(0)
    width = pairs * TILE

    @pl.when(step == 0)
    def _():
        assemble(qkv_ref, pieces)
        for tile in range(tiles):
            turned_ref[tile] = qkv_ref[tile_rows(place_ref[tile]), 2 * width :].T

    mine = qkv_ref[tile_rows(place_ref[step]), :]
    queries = [
        stacked_heads(mine[:, p * TILE : (p + 1) * TILE] * scale) for p in range(pairs)
    ]
    own_label = labrow_ref[step]
    begin = start_ref[step]
    trips = count_ref[step]

    def scores(trip, best):
        couple = [begin + 2 * trip + sub for sub in range(2)]
        kinds = [kind_ref[step * tiles + tile] for tile in couple]
        allowed = [lab_ref[tile] == own_label for tile in couple]
        keys = jnp.concatenate(
            [qkv_ref[tile_rows(place_ref[tile]), width : 2 * width] for tile in couple], 0
        )
        parts = []
        for p in range(pairs):
            both = dot(keys[:, p * TILE : (p + 1) * TILE], queries[p], 1, 1)
            highs = []
            for sub in range(2):
                raw = both[sub * TILE : (sub + 1) * TILE] + bias_ref[p, kinds[sub]]
                pair_high = []
                for h in range(2):
                    part = jnp.where(allowed[sub], raw[:, h * TILE : (h + 1) * TILE], MASKED)
                    span = slice((2 * p + h) * TILE, (2 * p + h + 1) * TILE)
                    score_ref[couple[sub], :, span] = part
                    pair_high.append(jnp.max(fold(part), axis=0))
                highs.append(jnp.concatenate(pair_high, 1))
            parts.append(jnp.maximum(*highs))
        return jnp.maximum(best, jnp.concatenate(parts, 1))

    best = lax.fori_loop(0, trips, scores, jnp.full((8, 2 * width), MASKED, F32))
    top = jnp.max(best, axis=0, keepdims=True)
    acc_ref[...] = jnp.zeros_like(acc_ref)

    def mix(trip, total):
        first = begin + 2 * trip
        probs = []
        for sub in range(2):
            value = jnp.exp(score_ref[first + sub] - top)
            total = total + jnp.sum(fold(value), axis=0)
            probs.append(value.astype(BF16))
        both = jnp.concatenate(probs, 0)
        for p in range(pairs):
            turned = jnp.concatenate(
                [turned_ref[first + sub, p * TILE : (p + 1) * TILE, :] for sub in range(2)], 1
            )
            acc_ref[p] += dot(turned, both[:, 2 * p * TILE : 2 * (p + 1) * TILE], 1, 0)
        return total

    total = lax.fori_loop(0, trips, mix, jnp.zeros((8, 2 * width), F32))
    total = jnp.sum(total, axis=0, keepdims=True)
    inverse = 1.0 / total
    log_total = top + jnp.log(total)
    for p in range(pairs):
        wide = acc_ref[p] * inverse[:, 2 * p * TILE : 2 * (p + 1) * TILE]
        out_ref[:, p * TILE : (p + 1) * TILE] = own_quadrants(wide).T.astype(BF16)
    for h in range(2 * pairs):
        lse_ref[0, h : h + 1, :] = log_total[:, h * TILE : (h + 1) * TILE]


def attend(pieces, bias, plan):
    pairs = bias.shape[0]
    width = pairs * TILE
    tiles = plan["tiles"]
    rows = tiles * TILE
    return call(
        functools.partial(attend_body, tiles=tiles, pairs=pairs, scale=plan["scale"]),
        "attend",
        [
            shaped((rows, width), BF16),
            shaped((tiles, 2 * pairs, TILE), F32),
            shaped((rows, 3 * width), BF16),
        ],
        grid_spec=pltpu.PrefetchScalarGridSpec(
            num_scalar_prefetch=4,
            grid=(tiles,),
            in_specs=[fixed(*piece.shape) for piece in pieces]
            + [fixed(*bias.shape), fixed(tiles, TILE, TILE), fixed(tiles, 1, TILE)],
            out_specs=[
                pl.BlockSpec((TILE, width), lambda i, place, *_: (place[i], 0)),
                pl.BlockSpec((1, 2 * pairs, TILE), lambda i, *_: (i, 0, 0)),
                fixed(rows, 3 * width),
            ],
            scratch_shapes=[
                pltpu.VMEM((tiles, TILE, 2 * width), F32),
                pltpu.VMEM((tiles, width, TILE), BF16),
                pltpu.VMEM((pairs, TILE, 2 * TILE), F32),
            ],
        ),
    )(
        plan["place"], plan["start"], plan["count"], plan["kind"],
        *pieces, bias, plan["lab"], plan["labrow"],
    )


def unskew(values):
    wide = jnp.concatenate([values, jnp.zeros_like(values)], 1)
    rows = TILE
    while rows > 8:
        rows //= 2
        wide = wide[:rows] + pltpu.roll(wide[rows:], 2 * TILE - rows, 1)
    row = lax.broadcasted_iota(jnp.int32, wide.shape, 0)
    for bit in (4, 2, 1):
        wide = jnp.where((row & bit) != 0, pltpu.roll(wide, 2 * TILE - bit, 1), wide)
    return jnp.sum(wide, axis=0, keepdims=True)


def attend_back_body(
    place_ref, start_ref, count_ref, kind_ref, *refs, tiles, pairs, scale, kinds,
):
    pieces, refs = refs[:2], refs[2:]
    (
        qkv_ref, bias_ref, lab_ref, labrow_ref, out_ref, lse_ref,
        dqkv_ref, table_ref,
        grad_ref, turned_ref, dk_ref, dv_ref, dq_ref, sums_ref,
    ) = refs
    step = pl.program_id(0)
    width = pairs * TILE

    @pl.when(step == 0)
    def _():
        assemble(grad_ref, pieces)
        for tile in range(tiles):
            turned_ref[tile] = qkv_ref[tile_rows(place_ref[tile]), width : 2 * width].T
        dk_ref[...] = jnp.zeros_like(dk_ref)
        dv_ref[...] = jnp.zeros_like(dv_ref)
        sums_ref[...] = jnp.zeros_like(sums_ref)

    here = tile_rows(place_ref[step])
    queries, grads, deltas, logs = [], [], [], []
    for p in range(pairs):
        span = slice(p * TILE, (p + 1) * TILE)
        queries.append(stacked_heads(qkv_ref[here, span] * scale))
        grad = grad_ref[here, span]
        grads.append(stacked_heads(grad))
        product = (grad.astype(F32) * out_ref[here, span].astype(F32)).T
        half = TILE // 2
        deltas.append(
            jnp.concatenate(
                [
                    jnp.sum(product[:half], axis=0, keepdims=True),
                    jnp.sum(product[half:], axis=0, keepdims=True),
                ],
                1,
            )
        )
        logs.append(jnp.concatenate([lse_ref[step, 2 * p + h : 2 * p + h + 1, :] for h in range(2)], 1))
    own_label = labrow_ref[step]
    begin = start_ref[step]
    dq_ref[...] = jnp.zeros_like(dq_ref)

    def visit(trip, carry):
        couple = [begin + 2 * trip + sub for sub in range(2)]
        kind = [kind_ref[step * tiles + tile] for tile in couple]
        there = [tile_rows(place_ref[tile]) for tile in couple]
        allowed = jnp.concatenate([lab_ref[tile] == own_label for tile in couple], 0)
        allowed = jnp.concatenate([allowed, allowed], 1)
        for p in range(pairs):
            span = slice(p * TILE, (p + 1) * TILE)
            key_span = slice(width + p * TILE, width + (p + 1) * TILE)
            value_span = slice(2 * width + p * TILE, 2 * width + (p + 1) * TILE)
            keys = jnp.concatenate([qkv_ref[at, key_span] for at in there], 0)
            vals = jnp.concatenate([qkv_ref[at, value_span] for at in there], 0)
            bias = jnp.concatenate([bias_ref[p, k] for k in kind], 0)
            raw = dot(keys, queries[p], 1, 1) + bias
            prob = jnp.exp(jnp.where(allowed, raw - logs[p], MASKED))
            lift = dot(vals, grads[p], 1, 1)
            slope = prob * (lift - deltas[p])
            low = slope.astype(BF16)
            dv = dot(prob.astype(BF16), grads[p], 1, 0)
            dk = dot(low, queries[p], 1, 0)
            for sub in range(2):
                part = slice(sub * TILE, (sub + 1) * TILE)
                sums_ref[p, kind[sub]] += slope[part]
                dv_ref[couple[sub], :, span] += dv[part]
                dk_ref[couple[sub], :, span] += dk[part]
            turned = jnp.concatenate([turned_ref[tile, span, :] for tile in couple], 1)
            dq_ref[p] += dot(turned, low, 1, 0)
        return carry

    lax.fori_loop(0, count_ref[step], visit, 0)
    for p in range(pairs):
        span = slice(p * TILE, (p + 1) * TILE)
        dqkv_ref[here, span] = (own_quadrants(dq_ref[p]).T * scale).astype(BF16)

    @pl.when(step == tiles - 1)
    def _():
        for tile in range(tiles):
            there = tile_rows(place_ref[tile])
            dqkv_ref[there, width : 2 * width] = dk_ref[tile].astype(BF16)
            dqkv_ref[there, 2 * width :] = dv_ref[tile].astype(BF16)
        for p in range(pairs):
            for kind in range(kinds):
                for h in range(2):
                    table_ref[2 * p + h, kind : kind + 1, :] = unskew(
                        sums_ref[p, kind, :, h * TILE : (h + 1) * TILE]
                    )


def attend_back(pieces, qkv, bias, plan, out, lse):
    tiles, pairs, kinds = plan["tiles"], bias.shape[0], bias.shape[1]
    width = pairs * TILE
    rows = tiles * TILE
    return call(
        functools.partial(
            attend_back_body, tiles=tiles, pairs=pairs, scale=plan["scale"], kinds=kinds
        ),
        "attend_back",
        [shaped((rows, 3 * width), BF16), shaped((2 * pairs, kinds, 2 * TILE), F32)],
        grid_spec=pltpu.PrefetchScalarGridSpec(
            num_scalar_prefetch=4,
            grid=(tiles,),
            in_specs=[fixed(*piece.shape) for piece in pieces]
            + [
                fixed(*qkv.shape), fixed(*bias.shape), fixed(tiles, TILE, TILE),
                fixed(tiles, 1, TILE), fixed(*out.shape), fixed(*lse.shape),
            ],
            out_specs=[fixed(rows, 3 * width), fixed(2 * pairs, kinds, 2 * TILE)],
            scratch_shapes=[
                pltpu.VMEM((rows, width), BF16),
                pltpu.VMEM((tiles, width, TILE), BF16),
                pltpu.VMEM((tiles, TILE, width), F32),
                pltpu.VMEM((tiles, TILE, width), F32),
                pltpu.VMEM((pairs, TILE, 2 * TILE), F32),
                pltpu.VMEM((pairs, kinds, TILE, 2 * TILE), F32),
            ],
        ),
    )(
        plan["place"], plan["start"], plan["count"], plan["kind"],
        *pieces, qkv, bias, plan["lab"], plan["labrow"], out, lse,
    )


EDGE = 16


def conv_body(
    order_ref, low_ref, high_ref, *refs, blocks, frames, chunks, lanes, taps,
):
    pieces, refs = refs[:2], refs[2:]
    taps_ref, lab_ref, act_ref, gated_ref, mixed_ref, glu_ref, window_ref, pad_ref, out_pad_ref = refs
    size = glu_ref.shape[0] // blocks
    assemble(glu_ref, pieces)
    channels = lanes * TILE
    half = taps // 2
    span = TILE + 2 * EDGE
    for lane in range(lanes):
        pad_ref[lane, :EDGE, :] = jnp.zeros((EDGE, TILE), F32)
    for block in range(blocks):
        here = pl.ds(pl.multiple_of(order_ref[block] * size, TILE), size)
        for lane in range(lanes):
            value = glu_ref[here, lane * TILE : (lane + 1) * TILE].astype(F32)
            gate = glu_ref[here, channels + lane * TILE : channels + (lane + 1) * TILE].astype(F32)
            first = EDGE + block * frames
            pad_ref[lane, first : first + size, :] = value * sigmoid(gate)
    rest = EDGE + (blocks - 1) * frames + size
    for lane in range(lanes):
        tail = pad_ref.shape[1] - rest
        pad_ref[lane, rest:, :] = jnp.zeros((tail, TILE), F32)

    def chunk(index, carry):
        base = pl.multiple_of(index * TILE, TILE)
        labels = lab_ref[pl.ds(base, span), :]
        center = labels[EDGE : EDGE + TILE]
        for lane in range(lanes):
            values = pad_ref[lane, pl.ds(base, span), :]
            gated_ref[pl.ds(base, TILE), lane * TILE : (lane + 1) * TILE] = values[
                EDGE : EDGE + TILE
            ]

            def segment(label, total):
                window_ref[...] = jnp.where(labels == label, values, 0.0)
                acc = jnp.zeros((TILE, TILE), F32)
                for tap in range(taps):
                    first = EDGE + tap - half
                    acc = acc + window_ref[first : first + TILE, :] * taps_ref[
                        tap : tap + 1, lane * TILE : (lane + 1) * TILE
                    ]
                return jnp.where(center == label, acc, total)

            total = lax.fori_loop(
                low_ref[index], high_ref[index] + 1, segment, jnp.zeros((TILE, TILE), F32)
            )
            mixed_ref[pl.ds(base, TILE), lane * TILE : (lane + 1) * TILE] = total
            out_pad_ref[lane, pl.ds(base, TILE), :] = total * sigmoid(total)
        return carry

    lax.fori_loop(0, chunks, chunk, 0)
    valid = lax.broadcasted_iota(jnp.int32, (size, TILE), 0) < frames
    for block in range(blocks):
        here = pl.ds(pl.multiple_of(order_ref[block] * size, TILE), size)
        for lane in range(lanes):
            rows = out_pad_ref[lane, block * frames : block * frames + size, :]
            act_ref[here, lane * TILE : (lane + 1) * TILE] = jnp.where(valid, rows, 0.0).astype(BF16)


def conv_forward(pieces, taps, plan):
    channels = pieces[0].shape[1] // 2
    blocks, frames, chunks = 4, plan["frames"], plan["chunks"]
    total = plan["tiles"] * TILE
    rows = chunks * TILE
    lanes = channels // TILE
    return call(
        functools.partial(
            conv_body, blocks=blocks, frames=frames, chunks=chunks, lanes=lanes, taps=taps.shape[0]
        ),
        "conv_forward",
        [
            shaped((total, channels), BF16),
            shaped((rows, channels), F32),
            shaped((rows, channels), F32),
            shaped((total, 2 * channels), BF16),
        ],
        grid_spec=pltpu.PrefetchScalarGridSpec(
            num_scalar_prefetch=3,
            grid=(1,),
            in_specs=[fixed(*piece.shape) for piece in pieces]
            + [fixed(*taps.shape), fixed(*plan["flat_lab"].shape)],
            out_specs=[
                fixed(total, channels), fixed(rows, channels), fixed(rows, channels),
                fixed(total, 2 * channels),
            ],
            scratch_shapes=[
                pltpu.VMEM((TILE + 2 * EDGE, TILE), F32),
                pltpu.VMEM((lanes, rows + 2 * EDGE, TILE), F32),
                pltpu.VMEM((lanes, rows, TILE), F32),
            ],
        ),
    )(plan["order"], plan["low"], plan["high"], *pieces, taps, plan["flat_lab"])


def conv_back_body(
    order_ref, low_ref, high_ref, *refs, blocks, frames, chunks, lanes, taps,
):
    pieces, refs = refs[:2], refs[2:]
    (
        glu_ref, taps_ref, lab_ref, mixed_ref,
        dglu_ref, slope_ref,
        grad_ref, window_ref, dgate_ref,
    ) = refs
    size = glu_ref.shape[0] // blocks
    assemble(grad_ref, pieces)
    channels = lanes * TILE
    half = taps // 2
    span = TILE + 2 * EDGE
    rows = chunks * TILE
    for block in range(blocks):
        here = pl.ds(pl.multiple_of(order_ref[block] * size, TILE), size)
        for lane in range(lanes):
            first = EDGE + block * frames
            slope_ref[lane, first : first + size, :] = grad_ref[
                here, lane * TILE : (lane + 1) * TILE
            ].astype(F32)
    rest = EDGE + (blocks - 1) * frames + size
    for lane in range(lanes):
        slope_ref[lane, :EDGE, :] = jnp.zeros((EDGE, TILE), F32)
        slope_ref[lane, rest:, :] = jnp.zeros((slope_ref.shape[1] - rest, TILE), F32)
        mixed = mixed_ref[:, lane * TILE : (lane + 1) * TILE]
        gate = sigmoid(mixed)
        slope_ref[lane, EDGE : EDGE + rows, :] = slope_ref[lane, EDGE : EDGE + rows, :] * (
            gate * (1.0 + mixed * (1.0 - gate))
        )
        dgate_ref[lane, rows:, :] = jnp.zeros((dgate_ref.shape[1] - rows, TILE), F32)

    def chunk(index, carry):
        base = pl.multiple_of(index * TILE, TILE)
        labels = lab_ref[pl.ds(base, span), :]
        center = labels[EDGE : EDGE + TILE]
        for lane in range(lanes):
            slopes = slope_ref[lane, pl.ds(base, span), :]

            def segment(label, total):
                window_ref[...] = jnp.where(labels == label, slopes, 0.0)
                acc = jnp.zeros((TILE, TILE), F32)
                for tap in range(taps):
                    first = EDGE - tap + half
                    acc = acc + window_ref[first : first + TILE, :] * taps_ref[
                        tap : tap + 1, lane * TILE : (lane + 1) * TILE
                    ]
                return jnp.where(center == label, acc, total)

            dgate_ref[lane, pl.ds(base, TILE), :] = lax.fori_loop(
                low_ref[index], high_ref[index] + 1, segment, jnp.zeros((TILE, TILE), F32)
            )
        return carry

    lax.fori_loop(0, chunks, chunk, 0)
    valid = lax.broadcasted_iota(jnp.int32, (size, TILE), 0) < frames
    for block in range(blocks):
        here = pl.ds(pl.multiple_of(order_ref[block] * size, TILE), size)
        for lane in range(lanes):
            lead = slice(lane * TILE, (lane + 1) * TILE)
            follow = slice(channels + lane * TILE, channels + (lane + 1) * TILE)
            rows_in = dgate_ref[lane, block * frames : block * frames + size, :]
            rows_in = jnp.where(valid, rows_in, 0.0)
            value = glu_ref[here, lead].astype(F32)
            gate = sigmoid(glu_ref[here, follow].astype(F32))
            dglu_ref[here, lead] = (rows_in * gate).astype(BF16)
            dglu_ref[here, follow] = (rows_in * value * gate * (1.0 - gate)).astype(BF16)


def conv_backward(pieces, glu, taps, plan, mixed):
    channels = glu.shape[1] // 2
    blocks, frames, chunks = 4, plan["frames"], plan["chunks"]
    rows = chunks * TILE
    lanes = channels // TILE
    slope = (lanes, rows + 2 * EDGE, TILE)
    return call(
        functools.partial(
            conv_back_body, blocks=blocks, frames=frames, chunks=chunks,
            lanes=lanes, taps=taps.shape[0],
        ),
        "conv_backward",
        [shaped(glu.shape, BF16), shaped(slope, F32)],
        grid_spec=pltpu.PrefetchScalarGridSpec(
            num_scalar_prefetch=3,
            grid=(1,),
            in_specs=[fixed(*piece.shape) for piece in pieces]
            + [
                fixed(*glu.shape), fixed(*taps.shape), fixed(*plan["flat_lab"].shape),
                fixed(rows, channels),
            ],
            out_specs=[fixed(*glu.shape), fixed(*slope)],
            scratch_shapes=[
                pltpu.VMEM((glu.shape[0], channels), BF16),
                pltpu.VMEM((TILE + 2 * EDGE, TILE), F32),
                pltpu.VMEM((lanes, rows + EDGE, TILE), F32),
            ],
        ),
    )(plan["order"], plan["low"], plan["high"], *pieces, glu, taps, plan["flat_lab"], mixed)


def taps_body(
    low_ref, high_ref, slope_ref, gated_ref, lab_ref, dtaps_ref, source_ref, window_ref, sums_ref,
    *, chunks, lanes, taps,
):
    half = taps // 2
    span = TILE + 2 * EDGE
    rows = chunks * TILE
    for lane in range(lanes):
        source_ref[lane, :EDGE, :] = jnp.zeros((EDGE, TILE), F32)
        source_ref[lane, EDGE : EDGE + rows, :] = gated_ref[:, lane * TILE : (lane + 1) * TILE]
        source_ref[lane, EDGE + rows :, :] = jnp.zeros((EDGE, TILE), F32)
    sums_ref[...] = jnp.zeros_like(sums_ref)

    def chunk(index, carry):
        base = pl.multiple_of(index * TILE, TILE)
        labels = lab_ref[pl.ds(base, span), :]
        center = labels[EDGE : EDGE + TILE]
        for lane in range(lanes):
            slopes = slope_ref[lane, pl.ds(base + EDGE, TILE), :]
            sources = source_ref[lane, pl.ds(base, span), :]

            def segment(label, kept):
                window_ref[...] = jnp.where(labels == label, sources, 0.0)
                inner = jnp.where(center == label, slopes, 0.0)
                for tap in range(taps):
                    first = EDGE + tap - half
                    part = fold(inner * window_ref[first : first + TILE, :])
                    sums_ref[lane, tap] += jnp.sum(part, axis=0)
                return kept

            lax.fori_loop(low_ref[index], high_ref[index] + 1, segment, 0)
        return carry

    lax.fori_loop(0, chunks, chunk, 0)
    for lane in range(lanes):
        dtaps_ref[:, lane * TILE : (lane + 1) * TILE] = jnp.sum(sums_ref[lane], axis=1)


def taps_backward(slope, gated, plan, taps):
    lanes, padded, _ = slope.shape
    chunks = plan["chunks"]
    shape = (taps, lanes * TILE)
    return call(
        functools.partial(taps_body, chunks=chunks, lanes=lanes, taps=taps),
        "taps_backward",
        shaped(shape, F32),
        grid_spec=pltpu.PrefetchScalarGridSpec(
            num_scalar_prefetch=2,
            grid=(1,),
            in_specs=[
                fixed(*slope.shape), fixed(*gated.shape), fixed(*plan["flat_lab"].shape),
            ],
            out_specs=fixed(*shape),
            scratch_shapes=[
                pltpu.VMEM((lanes, padded, TILE), F32),
                pltpu.VMEM((TILE + 2 * EDGE, TILE), F32),
                pltpu.VMEM((lanes, taps, 8, TILE), F32),
            ],
        ),
    )(plan["low"], plan["high"], slope, gated, plan["flat_lab"])


def swap(values, bit, axis="tensor"):
    count = lax.axis_size(axis)
    return lax.ppermute(values, axis, [(i, i ^ bit) for i in range(count)])


def gather(mine):
    return [mine, swap(mine, 1), swap(mine, 2)]


def tie(value, other):
    return lax.optimization_barrier((value, other))


def complete(blocks, near):
    blocks[2], near[0] = tie(blocks[2], near[0])
    blocks.append(swap(blocks[2], 1))


def scatter(own, beside, far, sent=None):
    arriving = []
    for across, diagonal in far:
        outgoing = (across.astype(F32) + swap(diagonal, 1).astype(F32)).astype(BF16)
        arriving.append(swap(outgoing, 2))
        if sent is not None:
            sent.append(outgoing)
    return [own, swap(beside, 1), arriving]


def sum_bits(values, axis, bit=1):
    while bit < lax.axis_size(axis):
        values = values + swap(values, bit, axis)
        bit *= 2
    return values


def halve_all(grad, gate):
    count = lax.axis_size("dp")
    bits = count.bit_length() - 1
    values = grad.reshape((2,) * bits + (grad.shape[0] // count, grad.shape[1]))
    for bit in range(bits):
        dim = bits - 1 - bit
        keep = (lax.axis_index("dp") >> bit) & 1
        sent = lax.dynamic_index_in_dim(values, 1 - keep, dim, keepdims=False)
        kept = lax.dynamic_index_in_dim(values, keep, dim, keepdims=False)
        if bit == 1:
            sent, gate = tie(sent, gate)
        arrived = swap(sent, 1 << bit, "dp")
        values = kept.astype(F32) + arrived.astype(F32)
        if bit < bits - 1:
            values = values.astype(BF16)
    return values, gate


def settle(grads):
    return lax.psum_scatter(grads, "dp", scatter_dimension=0, tiled=True)


def halves(array):
    return [(array, c, CHUNKS) for c in range(CHUNKS)]


def feed_forward(blocks, w_in, w_out):
    near = list(ff_rows(blocks[0], blocks[1], w_in, w_out))
    complete(blocks, near)
    far = [ff_rows(x1, x2, w_in, w_out) for x1, x2 in zip(halves(blocks[2]), halves(blocks[3]))]
    state = ([near[0]] + [f[0] for f in far], [near[1]] + [f[1] for f in far])
    return scatter(near[2], near[3], [f[2:] for f in far]), state


def feed_back(blocks, state, w_in, w_out):
    hidden, _ = state
    near = list(ff_back_rows(blocks[0], blocks[1], hidden[0], w_out, w_in))
    complete(blocks, near)
    far = [
        ff_back_rows(g1, g2, a, w_out, w_in)
        for g1, g2, a in zip(halves(blocks[2]), halves(blocks[3]), hidden[1:])
    ]
    parts = scatter(near[1], near[2], [f[1:] for f in far], outgoing := [])
    return parts, [near[0]] + [f[0] for f in far], outgoing


def zigzag(blocks):
    far = [item for pair in zip(halves(blocks[2]), halves(blocks[3])) for item in pair]
    return [blocks[0], blocks[1]] + far


def spread(blocks, weight, side, kind):
    near = [project(blocks[0], blocks[1], weight, side, kind)]
    complete(blocks, near)
    return near[0], project(blocks[2], blocks[3], weight, side, kind)


def collect(flat, weight, side):
    count = 4 * CHUNKS
    far = [
        expand((flat, 2 * CHUNKS + c, count), (flat, 3 * CHUNKS + c, count), weight, side)
        for c in range(CHUNKS)
    ]
    own, beside = expand((flat, 0, 4), (flat, 1, 4), weight, side)
    return scatter(own, beside, far)


def delayed(parts, other):
    own, beside, (first, *rest) = parts
    first, other = tie(first, other)
    return [own, beside, [first, *rest]], other


def make_plan(segments, frames, reach, head_width):
    blocks = lax.axis_size("tensor")
    here = lax.axis_index("tensor").astype(jnp.int32)
    size = pad_up(frames, TILE)
    per_block = size // TILE
    tiles = blocks * per_block
    offsets = tile_offsets(blocks, frames, per_block)
    kinds, table = bias_types(offsets, reach)
    flat = segments.reshape(-1).astype(jnp.int32)
    lab = jnp.pad(flat.reshape(blocks, frames), ((0, 0), (0, size - frames)), constant_values=-1)
    lab = lab.reshape(tiles, TILE)
    high = jnp.max(lab, axis=1)
    low = jnp.min(jnp.where(lab < 0, 1 << 20, lab), axis=1)
    seen = (low[:, None] <= high[None, :]) & (low[None, :] <= high[:, None])
    position = jnp.arange(tiles, dtype=jnp.int32)
    first = jnp.min(jnp.where(seen, position[None, :], tiles), axis=1)
    last = jnp.max(jnp.where(seen, position[None, :], -1), axis=1)
    count1 = last - first + 1
    count = (count1 + 1) // 2
    start = jnp.minimum(first, tiles - 2 * count)
    order = jnp.arange(blocks, dtype=jnp.int32) ^ here
    place = (order[:, None] * per_block + jnp.arange(per_block, dtype=jnp.int32)[None, :]).reshape(-1)
    total = blocks * frames
    chunks = pad_up(total, TILE) // TILE
    padded = jnp.pad(flat, (EDGE, chunks * TILE - total + EDGE), constant_values=-1)
    body = padded[EDGE : EDGE + chunks * TILE].reshape(chunks, TILE)
    return dict(
        kinds=kinds,
        kind=jnp.asarray(table.reshape(-1)),
        place=place,
        tiles=tiles,
        start=start,
        count=count,
        lab=jnp.broadcast_to(lab[:, :, None], (tiles, TILE, TILE)),
        labrow=lab[:, None, :],
        scale=float(head_width) ** -0.5,
        frames=frames,
        chunks=chunks,
        order=order,
        low=jnp.min(jnp.where(body < 0, 1 << 20, body), axis=1),
        high=jnp.max(body, axis=1),
        flat_lab=jnp.broadcast_to(padded[:, None], (padded.shape[0], TILE)),
    )


def shards(
    inputs, segments, cotangent, gain_one, first_in, first_out, gain_two, w_query, w_key, w_value,
    w_output, rel_table, gain_three, w_glu, kernel, w_back, gain_four, second_in, second_out,
    gain_five,
):
    frames, _, width = inputs.shape
    size = pad_up(frames, TILE)
    heads = rel_table.shape[0]
    reach = rel_table.shape[1] // 2
    head_width = w_query.shape[1] // heads

    def padded(values):
        return jnp.pad(values.reshape(frames, width), ((0, size - frames), (0, 0)))

    def total(sums):
        return sum(jnp.sum(part, axis=0) for part in sums)

    plan = make_plan(segments, frames, reach, head_width)
    onehot = column_onehot(plan["kinds"], reach)
    bias = bias_tiles(rel_table, onehot, plan["kinds"])
    w_qkv = jnp.concatenate([w_query, w_key, w_value], 1)
    channels = kernel.shape[1]
    glu_matrix = w_glu.reshape(width, 2 * channels)

    start = padded(inputs)
    h_one = gather(enter(start, gain_one))
    parts, state_one = feed_forward(h_one, first_in, first_out)
    h_two, one = join(start, parts, gain_two, 0.5)
    h_two = gather(h_two)
    out, lse, qkv = attend(spread(h_two, w_qkv, 0, BF16), bias, plan)
    h_three, two = join(one, collect(out, w_output, 0), gain_three, 1.0)
    h_three = gather(h_three)
    act, gated, mixed, glu = conv_forward(spread(h_three, glu_matrix, 0, BF16), kernel, plan)
    h_four, three = join(two, collect(act, w_back, 0), gain_four, 1.0)
    h_four = gather(h_four)
    parts, state_four = feed_forward(h_four, second_in, second_out)

    grads, output, e4, sums = turn(three, parts, gain_five, padded(cotangent), 0.5, 0.5)
    grad_five = total(sums)
    grads = gather(grads)
    parts, inner, _ = feed_back(grads, state_four, second_in, second_out)
    parts, grad_w = delayed(
        parts, weight_grads([(zigzag(grads), state_four[1]), (zigzag(h_four), inner)])
    )
    settled_four = settle(grad_w)
    grads, e3, sums = join_back(e4, three, parts, gain_four, 1.0)
    grad_four = total(sums)
    grads = gather(grads)
    dglu, slope = conv_backward(spread(grads, w_back, 1, BF16), glu, kernel, plan, mixed)
    parts, grad_w = delayed(
        collect(dglu, glu_matrix, 1), weight_grads([(grads, [act]), (h_three, [dglu])])
    )
    settled_three = settle(grad_w)
    grads, e2, sums = join_back(e3, two, parts, gain_three, 1.0)
    grad_three = total(sums)
    grads = gather(grads)
    grad_kernel = taps_backward(slope, gated, plan, kernel.shape[0])
    grads[2], grad_kernel = tie(grads[2], grad_kernel)
    pulled = spread(grads, w_output, 1, BF16)
    (first, second), settled_four = tie(pulled, settled_four)
    dqkv, table_sums = attend_back((first, second), qkv, bias, plan, out, lse)
    parts, grad_w = delayed(
        collect(dqkv, w_qkv, 1), weight_grads([(grads, [out]), (h_two, [dqkv])])
    )
    parts, settled_three = delayed(parts, settled_three)
    settled_two = settle(grad_w)
    grads, e1, sums = join_back(e2, one, parts, gain_two, 0.5)
    grad_two = total(sums)
    grads = gather(grads)
    parts, inner, outgoing = feed_back(grads, state_one, first_in, first_out)
    grad_w = weight_grads([(zigzag(grads), state_one[1])])
    grad_first_out = settle(grad_w)
    own, beside, (near_rows, far_rows) = parts
    near_rows, settled_two = tie(near_rows, settled_two)
    (_, _, (near_rows, _)), grad_first_in = delayed(
        [own, beside, [near_rows, far_rows]], weight_grads([(zigzag(h_one), inner)])
    )
    grad_first_in, far_rows = halve_all(grad_first_in, far_rows)
    parts = [own, beside, [near_rows, far_rows]]
    e0, sums = join_back(e1, start, parts, gain_one, 0.0)
    small, sums = tie(
        (table_sums, grad_kernel, grad_two, grad_three, grad_four, grad_five), sums
    )
    table_sums, grad_kernel, grad_two, grad_three, grad_four, grad_five = small
    grad_one = total(sums)
    grad_table = lax.dot_general(
        table_sums.reshape(heads, -1), onehot, (((1,), (1,)), ((), ())),
        precision=lax.Precision.HIGHEST, preferred_element_type=F32,
    )
    small = jnp.concatenate(
        [grad_one, grad_two, grad_three, grad_four, grad_five]
        + [grad_table.reshape(-1), grad_kernel.reshape(-1)]
    )
    gains = sum_bits(small[: 5 * width], "tensor")
    small = jnp.concatenate([gains, small[5 * width :]])
    small = sum_bits(small, "dp", 2)
    small = small + swap(small, 1, "dp")
    grad_gains = [small[i * width : (i + 1) * width] for i in range(5)]
    rest = small[5 * width :]
    grad_table = rest[: grad_table.size].reshape(grad_table.shape)
    grad_kernel = rest[grad_table.size :].reshape(grad_kernel.shape)
    part, own = w_query.shape[1], w_output.shape[0]
    settled_two, settled_three, settled_four, grad_first_out = (
        x.astype(F32) for x in (settled_two, settled_three, settled_four, grad_first_out)
    )
    return (
        jnp.concatenate(output, 0)[:frames].reshape(inputs.shape),
        e0[:frames].reshape(inputs.shape),
        grad_gains[0],
        grad_first_in,
        grad_first_out.T,
        grad_gains[1],
        settled_two[:, own : own + part],
        settled_two[:, own + part : own + 2 * part],
        settled_two[:, own + 2 * part :],
        settled_two[:, :own].T,
        grad_table,
        grad_gains[2],
        settled_three[:, channels:].reshape(-1, 2, channels),
        grad_kernel,
        settled_three[:, :channels].T,
        grad_gains[3],
        settled_four[:, second_out.shape[0] :],
        settled_four[:, : second_out.shape[0]].T,
        grad_gains[4],
    )


def solution(mesh):
    in_specs = (
        P("tensor", "dp", None), P("dp", None), P("tensor", "dp", None), P(),
        P(None, "tensor"), P("tensor", None), P(), P(None, "tensor"), P(None, "tensor"),
        P(None, "tensor"), P("tensor", None), P("tensor", None), P(), P(None, None, "tensor"),
        P(None, "tensor"), P("tensor", None), P(), P(None, "tensor"), P("tensor", None), P(),
    )
    out_specs = (
        P("tensor", "dp", None), P("tensor", "dp", None), P(), P("dp", "tensor"),
        P("tensor", "dp"), P(), P("dp", "tensor"), P("dp", "tensor"), P("dp", "tensor"),
        P("tensor", "dp"), P("tensor", None), P(), P("dp", None, "tensor"), P(None, "tensor"),
        P("tensor", "dp"), P(), P("dp", "tensor"), P("tensor", "dp"), P(),
    )
    return jax.shard_map(shards, mesh=mesh, in_specs=in_specs, out_specs=out_specs, check_vma=False)
```
